32 devices in a mesh: ctx: 4 (over y, core), fsdp: 8 (over z, x).
Axes of the slice: x: 2, y: 2, z: 4, core: 2. Of those that a mesh axis runs over, the one named last changes fastest.
Arguments:
- inputs: bfloat16 [8, 512, 2048], P('fsdp', 'ctx'), may hold values from -6 to 6
- lengths: int32 [8], P('fsdp'), may hold values from 256 to 512, as said below
- norm1_gain: bfloat16 [2048], P('fsdp'), may hold values from 0.5 to 1.5
- norm1_bias: bfloat16 [2048], P('fsdp'), may hold values from -1.25 to 1.25
- query_weight: bfloat16 [2048, 2048], P('fsdp'), may hold values from -3 to 3, as said below
- query_bias: bfloat16 [2048], P('fsdp'), may hold values from -3 to 3
- keyval_weight: bfloat16 [2048, 256], P('fsdp'), may hold values from -0.125 to 0.125
- value_bias: bfloat16 [128], P('fsdp'), may hold values from -3 to 3
- output_weight: bfloat16 [2048, 2048], P('fsdp'), may hold values from -0.75 to 0.75
- output_bias: bfloat16 [2048], P('fsdp'), may hold values from -3 to 3
- norm2_gain: bfloat16 [2048], P('fsdp'), may hold values from 0.5 to 1.5
- norm2_bias: bfloat16 [2048], P('fsdp'), may hold values from -1.25 to 1.25
- up_weight: bfloat16 [2048, 8192], P('fsdp'), may hold values from -0.125 to 0.125
- up_bias: bfloat16 [8192], P('fsdp'), may hold values from -3 to 3
- down_weight: bfloat16 [8192, 2048], P('fsdp'), may hold values from -0.0625 to 0.0625
- down_bias: bfloat16 [2048], P('fsdp'), may hold values from -3 to 3
- cotangent: bfloat16 [8, 512, 2048], P('fsdp', 'ctx'), may hold values from -6 to 6
Outputs:
- result: bfloat16 [8, 512, 2048], P('fsdp', 'ctx')
- input_grad: bfloat16 [8, 512, 2048], P('fsdp', 'ctx')
- grad_norm1_gain: float32 [2048], P('fsdp')
- grad_norm1_bias: float32 [2048], P('fsdp')
- grad_query_weight: float32 [2048, 2048], P('fsdp')
- grad_query_bias: float32 [2048], P('fsdp')
- grad_keyval_weight: float32 [2048, 256], P('fsdp')
- grad_value_bias: float32 [128], P('fsdp')
- grad_output_weight: float32 [2048, 2048], P('fsdp')
- grad_output_bias: float32 [2048], P('fsdp')
- grad_norm2_gain: float32 [2048], P('fsdp')
- grad_norm2_bias: float32 [2048], P('fsdp')
- grad_up_weight: float32 [2048, 8192], P('fsdp')
- grad_up_bias: float32 [8192], P('fsdp')
- grad_down_weight: float32 [8192, 2048], P('fsdp')
- grad_down_bias: float32 [2048], P('fsdp')
- clipped_query_weight: bfloat16 [2048, 2048], P('fsdp')
- clipped_query_bias: bfloat16 [2048], P('fsdp')
- clipped_keyval_weight: bfloat16 [2048, 256], P('fsdp')
The draws below stay inside these ranges and needn't reach their ends.
Inputs may be any that keep to these rules, and one draw needn't show every extreme that they name: Sequence b's live tokens are its first lengths[b]; in every draw some sequence is live over all 512 tokens. `query_weight`: a dense matrix.
All inputs are finite; a program needn't handle non-finite values.
Results may differ from the reference program's by a relative error of at most 0.019.
Values may be sent and summed in bfloat16 or wider, within the bound.
A program may use at most 384 MiB of HBM per device.

```python
import math
from functools import partial
import jax
import jax.numpy as jnp
from jax import lax

D = 2048
H = 16
HD = 128
FF = 8192
SEQS = 8
SEQLEN = 512


def draw_lengths(key, part):
    drawn = jax.random.randint(jax.random.fold_in(key, 11), (SEQS,), SEQLEN // 2, SEQLEN + 1)
    chosen = jax.random.randint(jax.random.fold_in(key, 12), (), 0, SEQS)
    return jnp.where(jnp.arange(SEQS) == chosen, SEQLEN, drawn).astype(jnp.int32)


def draw_query_weight(key, part):
    entries = jnp.clip(jax.random.normal(jax.random.fold_in(key, 21), (D, D), jnp.float32), -6.0, 6.0)
    logs = jax.random.uniform(jax.random.fold_in(key, 22), (H,), jnp.float32, math.log(0.7), math.log(2.5))
    scales = jnp.exp(logs)
    order = jax.random.permutation(jax.random.fold_in(key, 23), H)
    heads = jnp.arange(H)
    scales = jnp.where(heads == order[0], 3.0, scales)
    scales = jnp.where(heads == order[1], 0.7, scales)
    column = jnp.repeat(scales, HD)
    return (entries * column[None, :] / math.sqrt(D)).astype(jnp.bfloat16)


def shard_levels(key, shape, cuts, least, largest):
    def one(position, parts):
        steps = jax.random.uniform(jax.random.fold_in(jax.random.fold_in(key, 6), position), (parts,), jnp.float32, least / len(cuts), largest / len(cuts))
        return jnp.repeat(jnp.exp(steps), shape[position] // parts).reshape((-1,) + (1,) * (len(shape) - position - 1))

    factor_of = one(*cuts[0])
    for cut in cuts[1:]:
        factor_of = factor_of * one(*cut)
    return factor_of


def bell_draw(own_key, extent, deviation, limit, cuts=(), kind=jnp.bfloat16):
    factor_of = shard_levels(own_key, extent, cuts, -0.22, 0.18) if cuts else 1.0
    values = jax.random.normal(own_key, extent, jnp.float32) * deviation * factor_of
    return jnp.minimum(jnp.maximum(values, -limit), limit).astype(kind)


def setup_inputs(seed: int = 0) -> dict:
    streams_of = jax.random.split(jax.random.key(seed), 18)
    return {
        "inputs": bell_draw(streams_of[0], (SEQS, SEQLEN, D), 1.0, 6.0, ((0, 8), (1, 4))),
        "lengths": draw_lengths(jax.random.fold_in(streams_of[17], 71), 0),
        "norm1_gain": jnp.clip(1.0 + 0.1 * jax.random.normal(streams_of[2], (D,), jnp.float32), 0.5, 1.5).astype(jnp.bfloat16),
        "norm1_bias": bell_draw(streams_of[3], (D,), 0.2, 1.25, ((0, 8),)),
        "query_weight": draw_query_weight(jax.random.fold_in(streams_of[17], 71), 0),
        "query_bias": bell_draw(streams_of[5], (D,), 0.5, 3.0, ((0, 8),)),
        "keyval_weight": bell_draw(streams_of[6], (D, 2 * HD), D ** -0.5, 0.125, ((0, 8),)),
        "value_bias": bell_draw(streams_of[7], (HD,), 0.5, 3.0, ((0, 8),)),
        "output_weight": bell_draw(streams_of[8], (D, D), (D // 32) ** -0.5, 0.75, ((0, 8),)),
        "output_bias": bell_draw(streams_of[9], (D,), 0.5, 3.0, ((0, 8),)),
        "norm2_gain": jnp.clip(1.0 + 0.1 * jax.random.normal(streams_of[10], (D,), jnp.float32), 0.5, 1.5).astype(jnp.bfloat16),
        "norm2_bias": bell_draw(streams_of[11], (D,), 0.2, 1.25, ((0, 8),)),
        "up_weight": bell_draw(streams_of[12], (D, FF), D ** -0.5, 0.125, ((0, 8),)),
        "up_bias": bell_draw(streams_of[13], (FF,), 0.5, 3.0, ((0, 8),)),
        "down_weight": bell_draw(streams_of[14], (FF, D), FF ** -0.5, 0.0625, ((0, 8),)),
        "down_bias": bell_draw(streams_of[15], (D,), 0.5, 3.0, ((0, 8),)),
        "cotangent": bell_draw(streams_of[16], (SEQS, SEQLEN, D), 1.0, 6.0, ((0, 8), (1, 4))),
    }


EPSILON = 1e-05
CLIP_LIMIT = 10.0
HIGHEST = lax.Precision.HIGHEST

@jax.custom_vjp
def low(v):
    return lax.optimization_barrier(v.astype(jnp.bfloat16)).astype(jnp.float32)

@jax.custom_vjp
def low_back(v):
    return v

def low_keep(v):
    return (low(v), None)

def low_pass(kept, grad):
    return (grad,)

def back_keep(v):
    return (v, None)

def back_low(kept, grad):
    return (low(grad),)
low.defvjp(low_keep, low_pass)
low_back.defvjp(back_keep, back_low)

def both_ways(values):
    return low_back(low(values))

def layer_norm(values, gain, shift):
    center = values - lax.optimization_barrier(jnp.mean(values, -1, keepdims=True))
    spread = lax.optimization_barrier(jnp.mean(center * center, -1, keepdims=True))
    return center * lax.rsqrt(spread + EPSILON) * gain + shift

def product(left, right):
    return jnp.dot(left, right, precision=HIGHEST)

def attend(packed):
    queries, keys, values, length = packed
    positions = jnp.arange(SEQLEN, dtype=jnp.int32)
    allowed = (positions[None, :] <= positions[:, None]) & (positions[None, :] < length)
    scores = low_back(jnp.einsum('ind,jd->nij', queries, keys, precision=HIGHEST) * HD ** (-0.5))
    masked = jnp.where(allowed[None], scores, -jnp.inf)
    log_total = jax.nn.logsumexp(masked, axis=-1, keepdims=True)
    probs = low(jnp.where(allowed[None], jnp.exp(masked - log_total), 0.0))
    attended = jnp.einsum('nij,jd->ind', probs, values, precision=HIGHEST)
    live_query = positions < length
    chosen = allowed[None] & live_query[None, :, None]
    top_logit = lax.optimization_barrier(jnp.max(jnp.where(chosen, scores, -jnp.inf), axis=(1, 2)))
    return (attended, top_logit)

def forward(lengths, inputs, norm1_gain, norm1_bias, query_weight, query_bias, keyval_weight, value_bias, output_weight, output_bias, norm2_gain, norm2_bias, up_weight, up_bias, down_weight, down_bias):
    normed = low(layer_norm(inputs, norm1_gain, norm1_bias))
    queries = both_ways(product(normed, query_weight) + query_bias)
    keyvals = product(normed, keyval_weight)
    keys = both_ways(keyvals[..., :HD])
    values = both_ways(keyvals[..., HD:] + value_bias)
    heads_view = queries.reshape(SEQS, SEQLEN, H, HD)
    attended, top_logit = lax.map(jax.checkpoint(attend), (heads_view, keys, values, lengths))
    attended = both_ways(attended.reshape(SEQS, SEQLEN, D))
    middle = inputs + low_back(product(attended, output_weight) + output_bias)
    normed_two = low(layer_norm(middle, norm2_gain, norm2_bias))
    pre_act = low_back(product(normed_two, up_weight) + up_bias)
    act = low(jax.nn.gelu(pre_act, approximate=True))
    mlp_out = low_back(product(act, down_weight) + down_bias)
    live_rows = (jnp.arange(SEQLEN, dtype=jnp.int32)[None, :] < lengths[:, None]).astype(inputs.dtype)
    return (live_rows[..., None] * (middle + mlp_out), lax.optimization_barrier(jnp.max(top_logit, 0)))

def reference(inputs, lengths, norm1_gain, norm1_bias, query_weight, query_bias, keyval_weight, value_bias, output_weight, output_bias, norm2_gain, norm2_bias, up_weight, up_bias, down_weight, down_bias, cotangent):
    members = (inputs, norm1_gain, norm1_bias, query_weight, query_bias, keyval_weight, value_bias, output_weight, output_bias, norm2_gain, norm2_bias, up_weight, up_bias, down_weight, down_bias)
    floats = tuple((member.astype(jnp.float32) for member in members))
    result, pullback, top_logit = jax.vjp(partial(forward, lengths), *floats, has_aux=True)
    grads = pullback(cotangent.astype(jnp.float32))
    factors = CLIP_LIMIT / jnp.maximum(top_logit, CLIP_LIMIT)
    column_scale = jnp.repeat(jnp.sqrt(factors), HD)
    clipped_query_weight = (floats[3] * column_scale[None, :]).astype(jnp.bfloat16)
    clipped_query_bias = (floats[4] * column_scale).astype(jnp.bfloat16)
    key_scale = jnp.sqrt(jnp.min(factors))
    keyval_scale = jnp.concatenate([jnp.full((HD,), 1.0, floats[5].dtype) * key_scale, jnp.ones((HD,), floats[5].dtype)])
    clipped_keyval_weight = (floats[5] * keyval_scale[None, :]).astype(jnp.bfloat16)
    return (result.astype(jnp.bfloat16), grads[0].astype(jnp.bfloat16), grads[1].astype(jnp.float32), grads[2].astype(jnp.float32), grads[3].astype(jnp.float32), grads[4].astype(jnp.float32), grads[5].astype(jnp.float32), grads[6].astype(jnp.float32), grads[7].astype(jnp.float32), grads[8].astype(jnp.float32), grads[9].astype(jnp.float32), grads[10].astype(jnp.float32), grads[11].astype(jnp.float32), grads[12].astype(jnp.float32), grads[13].astype(jnp.float32), grads[14].astype(jnp.float32), clipped_query_weight, clipped_query_bias, clipped_keyval_weight)
```

```python
import functools
import math

import jax
import jax.numpy as jnp
from jax import lax
from jax.experimental import pallas as pl
from jax.experimental.pallas import tpu as pltpu
from jax.sharding import Mesh, PartitionSpec as P

H = 16
HD = 128
EPSILON = 1e-05
CLIP_LIMIT = 10.0
NEGATIVE = -1e30
BF = jnp.bfloat16
F32 = jnp.float32
GELU_A = 0.044715
GELU_C = math.sqrt(2.0 / math.pi)
SCALE = HD ** (-0.5)
MIB = 1 << 20


def mm(left, right):
    return jnp.dot(left, right, preferred_element_type=F32)


def mm_tn(left, right):
    return lax.dot_general(left, right, (((0,), (0,)), ((), ())), preferred_element_type=F32)


def mm_nt(left, right):
    return lax.dot_general(left, right, (((1,), (1,)), ((), ())), preferred_element_type=F32)


def shift(value, axis, count, step):
    return lax.ppermute(value, axis, [(i, (i + step) % count) for i in range(count)])


def pick(value, index, dim):
    return lax.dynamic_index_in_dim(value, index, dim, keepdims=False)


def in_order(parts, here, count, dim):
    if count == 1:
        return jnp.expand_dims(parts[0], dim)
    if count == 2:
        first = here == 0
        return jnp.stack(
            [jnp.where(first, parts[0], parts[1]), jnp.where(first, parts[1], parts[0])], dim
        )
    shape = list(parts[0].shape)
    shape.insert(dim, count)
    whole = jnp.zeros(shape, parts[0].dtype)
    for j, part in enumerate(parts):
        whole = lax.dynamic_update_index_in_dim(whole, part, lax.rem(here - j + count, count), dim)
    return whole


def gather(value, axis, count, dim):
    parts = [value] + [shift(value, axis, count, j) for j in range(1, count)]
    return in_order(parts, lax.axis_index(axis), count, dim)


def swap_blocks(value, axis, count, dim):
    here = lax.axis_index(axis)
    parts = [pick(value, here, dim)]
    for j in range(1, count):
        parts.append(shift(pick(value, lax.rem(here + j, count), dim), axis, count, j))
    return in_order(parts, here, count, dim)


def sum_blocks(value, axis, count, dim):
    here = lax.axis_index(axis)
    total = pick(value, here, dim).astype(F32)
    for j in range(1, count):
        block = pick(value, lax.rem(here + j, count), dim).astype(BF)
        total = total + shift(block, axis, count, j).astype(F32)
    return total


def sum_copies(value, axis, count):
    low = value.astype(BF)
    total = low.astype(F32)
    for j in range(1, count):
        total = total + shift(low, axis, count, j).astype(F32)
    return total


def attention_masks(rows, length):
    row = lax.broadcasted_iota(jnp.int32, (rows, rows), 0)
    col = lax.broadcasted_iota(jnp.int32, (rows, rows), 1)
    return (col <= row) & (col < length)


def attend_back_kernel(length_ref, q_ref, k_ref, v_ref, g_ref, gq_ref, gk_ref, gv_ref):
    rows = q_ref.shape[0]
    length = length_ref[0]
    scores = mm_nt(q_ref[...], k_ref[...]) * SCALE
    masked = jnp.where(attention_masks(rows, length), scores, NEGATIVE)
    top = jnp.max(masked, 1, keepdims=True)
    weights = jnp.exp(masked - top)
    weights = weights / jnp.sum(weights, 1, keepdims=True)
    grad_weights = mm_nt(g_ref[...], v_ref[...])
    delta = jnp.sum(weights * grad_weights, 1, keepdims=True)
    grad_scores = (weights * (grad_weights - delta)).astype(BF)
    gq_ref[...] = (mm(grad_scores, k_ref[...]) * SCALE).astype(BF)
    grad_keys = mm_tn(grad_scores, q_ref[...]) * SCALE
    grad_values = mm_tn(weights.astype(BF), g_ref[...])

    @pl.when(pl.program_id(0) == 0)
    def _():
        gk_ref[...] = grad_keys
        gv_ref[...] = grad_values

    @pl.when(pl.program_id(0) > 0)
    def _():
        gk_ref[...] += grad_keys
        gv_ref[...] += grad_values


def attend_back(length, queries, keys, values, grads):
    rows, width = queries.shape
    heads = width // HD
    block = pl.BlockSpec((rows, HD), lambda n, s: (0, n))
    whole = pl.BlockSpec((rows, HD), lambda n, s: (0, 0))
    return pl.pallas_call(
        attend_back_kernel,
        grid_spec=pltpu.PrefetchScalarGridSpec(
            num_scalar_prefetch=1,
            grid=(heads,),
            in_specs=[block, whole, whole, block],
            out_specs=[block, whole, whole],
        ),
        out_shape=[
            jax.ShapeDtypeStruct((rows, width), BF),
            jax.ShapeDtypeStruct((rows, HD), F32),
            jax.ShapeDtypeStruct((rows, HD), F32),
        ],
        compiler_params=pltpu.CompilerParams(vmem_limit_bytes=48 * MIB),
        cost_estimate=pl.CostEstimate(
            flops=10 * heads * rows * rows * HD,
            bytes_accessed=8 * rows * width,
            transcendentals=heads * rows * rows,
        ),
        name="attend_back",
    )(length, queries, keys, values, grads)


MESH = pl.DeviceIdType.MESH
SEMS = 96
SMALL_ROWS = 16


class Links:
    def __init__(self, sends, recvs, locals_):
        self.sends, self.recvs, self.locals_ = sends, recvs, locals_
        self.used, self.used_local = 0, 0
        self.open = []

    def push(self, src, dst, axis, target):
        index = self.used
        self.used += 1
        copy = pltpu.make_async_remote_copy(
            src_ref=src,
            dst_ref=dst,
            send_sem=self.sends.at[index],
            recv_sem=self.recvs.at[index],
            device_id={axis: target},
            device_id_type=MESH,
        )
        copy.start()
        self.open.append(copy)
        return copy

    def local(self, src, dst):
        index = self.used_local
        self.used_local += 1
        copy = pltpu.make_async_copy(src, dst, self.locals_.at[index])
        copy.start()
        return copy

    def drain(self):
        for copy in self.open:
            copy.wait_send()


def wait_all(copies):
    for copy in copies:
        copy.wait()


def wait_recvs(copies):
    for copy in copies:
        copy.wait_recv()


def around(axis, here, count):
    return [(axis, lax.rem(here + j, count)) for j in range(1, count)]


def greet(groups):
    barrier = pltpu.get_barrier_semaphore()
    count = 0
    for group in groups:
        for axis, target in group:
            pl.semaphore_signal(barrier, inc=1, device_id={axis: target}, device_id_type=MESH)
            count += 1
    pl.semaphore_wait(barrier, count)


class Gather:
    def __init__(self, links, buf, place):
        self.links, self.buf, (self.z, self.Z, self.x, self.X) = links, buf, place
        block = buf.at[self.z * self.X + self.x]
        self.from_z = [links.push(block, block, *to) for to in around("z", self.z, self.Z)]
        self.from_x = [links.push(block, block, *to) for to in around("x", self.x, self.X)]

    def forward(self, j):
        self.from_z[j - 1].wait_recv()
        block = self.buf.at[lax.rem(self.z - j + self.Z, self.Z) * self.X + self.x]
        self.from_x += [
            self.links.push(block, block, *to) for to in around("x", self.x, self.X)
        ]

    def finish(self):
        wait_recvs(self.from_x)


def forward_kernel(
    sizes,
    length_ref,
    rows,
    gmlp,
    wq,
    wkv,
    small,
    wo,
    up,
    down,
    seq_o,
    wqkv_o,
    wo_o,
    wup,
    wdown,
    gmall,
    ntall,
    normed_o,
    qkv_o,
    att_o,
    mid_o,
    top_o,
    vec_o,
    v_seq,
    v_hat,
    v_norm,
    v_w,
    v_small,
    v_vec,
    v_qkv,
    v_att,
    v_wo,
    v_br,
    v_brall,
    v_mid,
    v_nt,
    v_top,
    v_topz,
    v_topx,
    v_tall,
    sends,
    recvs,
    locals_,
):
    Y, K, Z, X = sizes
    C, S = Y * K, Z * X
    y, k, z, x = (lax.axis_index(name) for name in ("y", "k", "z", "x"))
    c = y * K + k
    me = z * X + x
    R, D = rows.shape
    T = C * R
    cols = D // C
    qkv_cols = cols + 2 * HD
    here = wq.shape[0]
    part = wdown.shape[1]
    heads = cols // HD
    length = length_ref[0]
    links = Links(sends, recvs, locals_)
    place = (z, Z, x, X)
    to_z, to_x = around("z", z, Z), around("x", x, X)
    to_y, to_k = around("y", y, Y), around("k", k, K)
    zs = [lax.rem(z - j + Z, Z) for j in range(Z)]
    ys = [lax.rem(y - j + Y, Y) for j in range(Y)]
    others = [
        (jy, jk, lax.rem(y + jy, Y), lax.rem(k + jk, K))
        for jy in range(Y)
        for jk in range(K)
        if jy or jk
    ]

    greet([to_z, to_x, to_y, to_k])

    first = [
        links.local(wq.at[:, pl.ds(pl.multiple_of(c * cols, cols), cols)], v_w.at[me, :, pl.ds(0, cols)]),
        links.local(wkv, v_w.at[me, :, pl.ds(cols, 2 * HD)]),
        links.local(small, v_small.at[me]),
        links.local(rows, v_seq.at[pl.ds(c * R, R)]),
    ]
    own_wo = links.local(wo.at[:, pl.ds(pl.multiple_of(c * cols, cols), cols)], v_wo.at[me])
    wait_all(first)
    qkv_gather = Gather(links, v_w, place)
    small_gather = Gather(links, v_small, place)
    mine = v_seq.at[pl.ds(c * R, R)]
    seq_y = [links.push(mine, mine, *to) for to in to_y]
    seq_k = [links.push(mine, mine, *to) for to in to_k]
    for j in range(1, Y):
        seq_y[j - 1].wait_recv()
        block = v_seq.at[pl.ds((ys[j] * K + k) * R, R)]
        seq_k += [links.push(block, block, *to) for to in to_k]
    wait_recvs(seq_k)
    save_seq = links.local(v_seq, seq_o)

    step = 64

    @pl.loop(0, T // step)
    def _(i):
        span = pl.ds(pl.multiple_of(i * step, step), step)
        values = v_seq[span, :].astype(F32)
        center = values - jnp.mean(values, 1, keepdims=True)
        rstd = lax.rsqrt(jnp.mean(center * center, 1, keepdims=True) + EPSILON)
        v_hat[span, :] = center * rstd

    for j in (1, Z - 1, 2):
        qkv_gather.forward(j)
        small_gather.forward(j)
    own_wo.wait()
    wo_gather = Gather(links, v_wo, place)
    qkv_gather.finish()
    small_gather.finish()

    own_up = []
    up_z = []
    up_x = []
    for j in range(Z):
        target = lax.rem(z + j, Z)
        for i in range(X):
            unit = ((target * X + i) * K + k) * part
            src = up.at[:, pl.ds(pl.multiple_of(unit, part), part)]
            dst = wup.at[me, :, pl.ds(i * part, part)]
            if j == 0:
                own_up.append(links.local(src, dst))
            else:
                up_z.append(links.push(src, dst, "z", target))
    own_down = links.local(down.at[pl.ds(pl.multiple_of(k * part, part), part)], wdown.at[x])
    down_x = [
        links.push(down.at[pl.ds(pl.multiple_of(k * part, part), part)], wdown.at[x], *to)
        for to in to_x
    ]
    own_gm = links.local(gmlp, gmall.at[z, k])
    gm_z = [links.push(gmlp, gmall.at[z, k], *to) for to in to_z]
    gm_k = [links.push(gmlp, gmall.at[z, k], *to) for to in to_k]

    for s in range(S):
        v_vec[:, pl.ds(s * here, here)] = v_small[s]
    gain = v_vec[0:1, :].astype(F32)
    bias = v_vec[1:2, :].astype(F32)

    @pl.loop(0, T // step)
    def _(i):
        span = pl.ds(pl.multiple_of(i * step, step), step)
        v_norm[span, :] = (v_hat[span, :] * gain + bias).astype(BF)

    save_norm = links.local(v_norm, normed_o)
    save_vec = links.local(v_vec, vec_o)
    q_bias = v_vec[2:3, pl.ds(pl.multiple_of(c * cols, cols), cols)].astype(F32)
    v_bias = jnp.zeros((1, HD), F32)
    for s in range(S):
        v_bias = v_bias + v_small[s, 12:13, 0:HD].astype(F32)
    wide = min(cols, 256)
    for n in range(cols // wide):
        span = slice(n * wide, (n + 1) * wide)
        weights = v_w[:, :, span].reshape(D, wide)
        v_qkv[:, span] = (mm(v_norm[...], weights) + q_bias[:, span]).astype(BF)
    weights = v_w[:, :, cols:].reshape(D, 2 * HD)
    kv_bias = jnp.concatenate([jnp.zeros((1, HD), F32), v_bias], 1)
    v_qkv[:, cols:] = (mm(v_norm[...], weights) + kv_bias).astype(BF)
    save_qkv = links.local(v_qkv, qkv_o)

    @pl.loop(0, heads)
    def _(n):
        span = pl.ds(pl.multiple_of(n * HD, HD), HD)
        scores = mm_nt(v_qkv[:, span], v_qkv[:, cols : cols + HD]) * SCALE
        masked = jnp.where(attention_masks(T, length), scores, NEGATIVE)
        top = jnp.max(masked, 1, keepdims=True)
        weights = jnp.exp(masked - top)
        probs = (weights / jnp.sum(weights, 1, keepdims=True)).astype(BF)
        own = pl.ds(pl.multiple_of(c * cols + n * HD, HD), HD)
        v_att[:, own] = mm(probs, v_qkv[:, cols + HD :]).astype(BF)
        live = lax.broadcasted_iota(jnp.int32, (T, 1), 0) < length
        best = jnp.max(jnp.where(live, top, NEGATIVE), 0, keepdims=True)
        v_top[pl.ds(n, 1), :] = jnp.broadcast_to(best, (1, HD))

    def att_block(source):
        return v_att.at[:, pl.ds(pl.multiple_of(source * cols, cols), cols)]

    att_y = [links.push(att_block(c), att_block(c), *to) for to in to_y]
    att_k = [links.push(att_block(c), att_block(c), *to) for to in to_k]
    top_z = [links.push(v_top, v_topz.at[j], *to) for j, to in enumerate(to_z)]
    for j in (1, Z - 1, 2):
        wo_gather.forward(j)
    for j in range(1, Y):
        att_y[j - 1].wait_recv()
        att_k += [links.push(att_block(ys[j] * K + k), att_block(ys[j] * K + k), *to) for to in to_k]
    wait_recvs(top_z)
    best = v_top[...]
    for j in range(Z - 1):
        best = jnp.maximum(best, v_topz[j])
    v_topx[0] = best
    top_x = [links.push(v_topx.at[0], v_topx.at[j + 1], *to) for j, to in enumerate(to_x)]
    wait_recvs(att_k)
    save_att = links.local(v_att, att_o)
    wo_gather.finish()

    narrow = min(cols, 256)
    for n in range(cols // narrow):
        span = slice(n * narrow, (n + 1) * narrow)
        weights = v_wo[:, :, span].reshape(D, narrow)
        v_br[:, :, span] = mm(v_att[...], weights).astype(BF).reshape(C, R, narrow)
    br_in = []
    for jy, jk, ty, tk in others:
        index = links.used
        links.used += 1
        copy = pltpu.make_async_remote_copy(
            src_ref=v_br.at[ty * K + tk],
            dst_ref=v_brall.at[c],
            send_sem=sends.at[index],
            recv_sem=recvs.at[index],
            device_id={"y": ty, "k": tk},
            device_id_type=MESH,
        )
        copy.start()
        links.open.append(copy)
        br_in.append(copy)
    v_brall[c] = v_br[c]
    wait_recvs(top_x)
    best = v_topx[0]
    for j in range(1, X):
        best = jnp.maximum(best, v_topx[j])
    v_tall[c] = best
    top_y = [links.push(v_tall.at[c], v_tall.at[c], *to) for to in to_y]
    top_k = [links.push(v_tall.at[c], v_tall.at[c], *to) for to in to_k]
    wait_recvs(br_in)

    for q in range(C):
        span = slice(q * cols, (q + 1) * cols)
        rows_in = v_seq[pl.ds(pl.multiple_of(c * R, R), R), span].astype(F32)
        v_mid[:, span] = rows_in + v_brall[q].astype(F32) + v_vec[3:4, span].astype(F32)
    save_mid = links.local(v_mid, mid_o)
    gain_two = v_vec[4:5, :].astype(F32)
    bias_two = v_vec[5:6, :].astype(F32)

    @pl.loop(0, R // step)
    def _(i):
        span = pl.ds(pl.multiple_of(i * step, step), step)
        values = v_mid[span, :]
        center = values - jnp.mean(values, 1, keepdims=True)
        rstd = lax.rsqrt(jnp.mean(center * center, 1, keepdims=True) + EPSILON)
        v_nt[span, :] = (center * rstd * gain_two + bias_two).astype(BF)

    own_nt = links.local(v_nt, ntall.at[z, k])
    nt_z = [links.push(v_nt, ntall.at[z, k], *to) for to in to_z]
    nt_k = [links.push(v_nt, ntall.at[z, k], *to) for to in to_k]

    for j in range(1, Y):
        top_y[j - 1].wait_recv()
        block = v_tall.at[ys[j] * K + k]
        top_k += [links.push(block, block, *to) for to in to_k]
    wait_recvs(top_k)
    save_top = links.local(v_tall, top_o)

    wait_all(own_up)
    up_x += [links.push(wup.at[me], wup.at[me], *to) for to in to_x]
    for j in (1, Z - 1, 2):
        wait_recvs(up_z[(j - 1) * X : j * X])
        block = wup.at[zs[j] * X + x]
        up_x += [links.push(block, block, *to) for to in to_x]
    for j in (1, Z - 1, 2):
        gm_z[j - 1].wait_recv()
        gm_k += [links.push(gmall.at[zs[j], k], gmall.at[zs[j], k], *to) for to in to_k]
    for j in (1, Z - 1, 2):
        nt_z[j - 1].wait_recv()
        nt_k += [links.push(ntall.at[zs[j], k], ntall.at[zs[j], k], *to) for to in to_k]
    save_w = links.local(v_w, wqkv_o)
    save_wo = links.local(v_wo, wo_o)
    wait_recvs(down_x + up_x + gm_k + nt_k)
    wait_all(
        [own_down, own_gm, own_nt, save_seq, save_norm, save_vec, save_qkv, save_att, save_mid]
        + [save_top, save_w, save_wo]
    )
    links.drain()


def forward_call(sizes, lengths, rows, gmlp, wq, wkv, small, wo, up, down):
    Y, K, Z, X = sizes
    C, S = Y * K, Z * X
    R, D = rows.shape
    T = C * R
    cols = D // C
    qkv_cols = cols + 2 * HD
    here = wq.shape[0]
    part = down.shape[0] // K
    heads = cols // HD
    shape = jax.ShapeDtypeStruct
    anywhere = pl.BlockSpec(memory_space=pl.ANY)
    outs = [
        shape((T, D), BF),
        shape((S, here, qkv_cols), BF),
        shape((S, here, cols), BF),
        shape((S, here, X * part), BF),
        shape((X, part, D), BF),
        shape((Z, K, R, D), BF),
        shape((Z, K, R, D), BF),
        shape((T, D), BF),
        shape((T, qkv_cols), BF),
        shape((T, D), BF),
        shape((R, D), F32),
        shape((C, 8, HD), F32),
        shape((SMALL_ROWS, D), BF),
    ]
    return pl.pallas_call(
        functools.partial(forward_kernel, sizes),
        in_specs=[pl.BlockSpec(memory_space=pltpu.SMEM)] + [anywhere] * 8,
        out_specs=[anywhere] * len(outs),
        out_shape=outs,
        scratch_shapes=[
            pltpu.VMEM((T, D), BF),
            pltpu.VMEM((T, D), F32),
            pltpu.VMEM((T, D), BF),
            pltpu.VMEM((S, here, qkv_cols), BF),
            pltpu.VMEM((S, SMALL_ROWS, here), BF),
            pltpu.VMEM((SMALL_ROWS, D), BF),
            pltpu.VMEM((T, qkv_cols), BF),
            pltpu.VMEM((T, D), BF),
            pltpu.VMEM((S, here, cols), BF),
            pltpu.VMEM((C, R, cols), BF),
            pltpu.VMEM((C, R, cols), BF),
            pltpu.VMEM((R, D), F32),
            pltpu.VMEM((R, D), BF),
            pltpu.VMEM((8, HD), F32),
            pltpu.VMEM((Z - 1, 8, HD), F32),
            pltpu.VMEM((X, 8, HD), F32),
            pltpu.VMEM((C, 8, HD), F32),
            pltpu.SemaphoreType.DMA((SEMS,)),
            pltpu.SemaphoreType.DMA((SEMS,)),
            pltpu.SemaphoreType.DMA((32,)),
        ],
        compiler_params=pltpu.CompilerParams(
            collective_id=1, has_side_effects=True, vmem_limit_bytes=60 * MIB
        ),
        name="layer_forward",
    )(lengths, rows, gmlp, wq, wkv, small, wo, up, down)


def norm_parts(values):
    center = values - jnp.mean(values, -1, keepdims=True)
    rstd = lax.rsqrt(jnp.mean(center * center, -1, keepdims=True) + EPSILON)
    return center * rstd, rstd


def norm_back(grad, gain, xhat, rstd):
    scaled = grad * gain
    return rstd * (
        scaled
        - jnp.mean(scaled, -1, keepdims=True)
        - xhat * jnp.mean(scaled * xhat, -1, keepdims=True)
    )


def body(
    sizes,
    inputs,
    lengths,
    norm1_gain,
    norm1_bias,
    query_weight,
    query_bias,
    keyval_weight,
    value_bias,
    output_weight,
    output_bias,
    norm2_gain,
    norm2_bias,
    up_weight,
    up_bias,
    down_weight,
    down_bias,
    cotangent,
):
    Y, K, Z, X = sizes
    C, S = Y * K, Z * X
    y, k, z, x = (lax.axis_index(name) for name in ("y", "k", "z", "x"))
    c = y * K + k
    R, D = inputs.shape[1:]
    rows_here = query_weight.shape[0]
    ff_here = down_weight.shape[0]
    ff_part = ff_here // K
    FF = ff_here * S
    T = C * R
    cols = D // C
    heads = H // C
    qkv_cols = cols + 2 * HD
    small_len = 7 * rows_here + ff_here + HD // S
    small_rows = -(-small_len // qkv_cols)
    small_rows = -(-small_rows // 16) * 16
    packed_rows = rows_here + small_rows

    pieces = [norm1_gain, norm1_bias, query_bias, output_bias, norm2_gain, norm2_bias, down_bias]
    shard = z * X + x
    lanes = jnp.arange(HD) // (HD // S) == shard
    value_row = jnp.where(lanes, jnp.tile(value_bias, S), 0).astype(BF)
    small = jnp.zeros((SMALL_ROWS, rows_here), BF)
    for row, piece in enumerate(pieces):
        small = small + jnp.pad(piece[None, :], ((row, SMALL_ROWS - 1 - row), (0, 0)))
    small = small + jnp.pad(up_bias.reshape(-1, rows_here), ((8, 4), (0, 0)))
    small = small + jnp.pad(value_row[None, :], ((12, 3), (0, rows_here - HD)))

    length = lengths[0]
    positions = c * R + jnp.arange(R, dtype=jnp.int32)
    live_rows = (positions < length).astype(F32)[:, None]
    grad_out = live_rows * cotangent[0].astype(F32)
    grad_mlp = grad_out.astype(BF)
    rows_low = inputs[0]
    (
        seq_low,
        wqkv,
        wo,
        wup,
        wdown,
        grad_mlp_all,
        normed_two_all,
        normed,
        qkv,
        attended_all,
        middle,
        tops,
        vectors,
    ) = forward_call(
        sizes,
        lengths,
        rows_low,
        grad_mlp,
        query_weight,
        keyval_weight,
        small,
        output_weight,
        up_weight,
        down_weight,
    )
    wqkv = wqkv.reshape(D, qkv_cols)
    wo = wo.reshape(D, cols)
    wup = wup.reshape(D, X * ff_part)
    wdown = wdown.reshape(X * ff_part, D)
    grad_mlp_all = grad_mlp_all.reshape(Z * K * R, D)
    normed_two_all = normed_two_all.reshape(Z * K * R, D)
    queries, keys, values = qkv[:, :cols], qkv[:, cols : cols + HD], qkv[:, cols + HD :]
    top_logit = tops[:, :heads, 0].reshape(H)
    gain_one = vectors[0].astype(F32)
    gain_two = vectors[4].astype(F32)
    d_bias = vectors[6].astype(F32)
    u_bias = vectors[8:12].reshape(K, 4 // K, Z, X, rows_here)
    u_bias_own = pick(pick(u_bias, k, 0), z, 1)
    u_bias_own = jnp.moveaxis(u_bias_own, 0, 1).reshape(-1).astype(F32)
    rows_in = rows_low.astype(F32)
    seq_hat, seq_rstd = norm_parts(seq_low.astype(F32))
    hat_two, rstd_two = norm_parts(middle)

    pre_act = mm(normed_two_all, wup) + u_bias_own
    tanh = jnp.tanh(GELU_C * (pre_act + GELU_A * pre_act * pre_act * pre_act))
    act = (0.5 * pre_act * (1.0 + tanh)).astype(BF)
    slope = 0.5 * (1.0 + tanh) + 0.5 * pre_act * (1.0 - tanh * tanh) * GELU_C * (
        1.0 + 3.0 * GELU_A * pre_act * pre_act
    )
    grad_act = mm_nt(grad_mlp_all, wdown)
    grad_pre_wide = grad_act * slope
    grad_pre = grad_pre_wide.astype(BF)
    grad_two_part = mm_nt(grad_pre, wup).astype(BF)
    grad_two = lax.psum_scatter(grad_two_part, ("z", "k"), tiled=True).astype(F32)
    mlp_part = mm(act, wdown).astype(BF)
    mlp_out = lax.psum_scatter(mlp_part, ("z", "k"), tiled=True).astype(F32)
    result = (live_rows * (middle + mlp_out + d_bias)).astype(BF)[None]

    grad_up_bias = jnp.sum(grad_pre.astype(F32), 0)
    grad_down_bias = jnp.sum(grad_mlp.astype(F32), 0)

    gdown = mm_tn(act, grad_mlp_all).astype(BF).reshape(X, ff_part, D)
    gdown = sum_blocks(gdown, "x", X, 0)
    gdown = sum_copies(gdown, "y", Y).astype(BF)
    grad_down_weight = gather(gdown, "k", K, 0).reshape(ff_here, D).astype(F32)

    gup = mm_tn(normed_two_all, grad_pre).astype(BF)
    gup = gup.reshape(Z, X, Y, rows_here // Y, X * ff_part)
    gup = sum_blocks(gup, "x", X, 1)
    gup = sum_blocks(gup, "y", Y, 1).astype(BF)
    gup = swap_blocks(gup, "z", Z, 0)
    gup = gather(gather(gup, "y", Y, 0), "k", K, 1)
    gup = gup.reshape(Y, K, Z, rows_here // Y, X, ff_part).transpose(0, 3, 2, 4, 1, 5)
    grad_up_weight = gup.reshape(rows_here, FF).astype(F32)

    grad_gain_two = jnp.sum(grad_two * hat_two, 0)
    grad_shift_two = jnp.sum(grad_two, 0)
    grad_middle = grad_out + norm_back(grad_two, gain_two, hat_two, rstd_two)
    grad_branch = grad_middle.astype(BF)
    grad_output_bias = jnp.sum(grad_branch.astype(F32), 0)
    grad_branch_cols = swap_blocks(grad_branch.reshape(R, C, cols), ("y", "k"), C, 1)
    grad_branch_cols = jnp.moveaxis(grad_branch_cols, 1, 0).reshape(T, cols)
    grad_att = mm_nt(grad_branch_cols, wo).astype(BF).reshape(T, Y, K, cols)
    grad_att = sum_blocks(grad_att, "k", K, 2)
    grad_att = sum_blocks(grad_att, "y", Y, 1).astype(BF)
    gout = mm_tn(attended_all, grad_branch_cols).astype(BF).reshape(Z, X, rows_here, cols)
    gout = sum_blocks(gout, "x", X, 1).astype(BF)
    gout = lax.psum_scatter(gout, "z")
    gout = gather(gather(gout, "y", Y, 1), "k", K, 2)
    grad_output_weight = gout.reshape(rows_here, D).astype(F32)

    grad_queries, grad_keys, grad_values = attend_back(lengths, queries, keys, values, grad_att)
    grad_qkv = jnp.concatenate([grad_queries, grad_keys.astype(BF), grad_values.astype(BF)], 1)
    grad_one_part = mm_nt(grad_qkv, wqkv)
    grad_gain_one = jnp.sum(grad_one_part * seq_hat, 0)
    grad_shift_one = jnp.sum(grad_one_part, 0)
    grad_one = grad_one_part.astype(BF).reshape(Y, K, R, D)
    grad_one = sum_blocks(grad_one, "k", K, 1)
    grad_one = sum_blocks(grad_one, "y", Y, 0)
    hat_one, rstd_one = norm_parts(rows_in)
    input_grad = (grad_middle + norm_back(grad_one, gain_one, hat_one, rstd_one)).astype(BF)[None]

    gqkv = mm_tn(normed, grad_qkv).astype(BF).reshape(Z, X, rows_here, qkv_cols)
    qkv_bias_grad = jnp.sum(grad_qkv.astype(F32), 0)
    grad_query_bias = lax.dynamic_update_slice_in_dim(
        jnp.zeros((D,), F32), qkv_bias_grad[:cols], c * cols, 0
    )
    grad_up_bias_all = lax.dynamic_update_slice(
        jnp.zeros((Z, X, K, ff_part), F32),
        grad_up_bias.reshape(1, X, 1, ff_part),
        (z, 0, k, 0),
    ).reshape(S, ff_here)
    small_grads = jnp.concatenate(
        [
            item.reshape(S, rows_here)
            for item in (
                grad_gain_one,
                grad_shift_one,
                grad_query_bias,
                grad_output_bias,
                grad_gain_two,
                grad_shift_two,
                grad_down_bias,
            )
        ]
        + [grad_up_bias_all, qkv_bias_grad[cols + HD :].reshape(S, HD // S)],
        1,
    )
    small_grads = jnp.pad(small_grads, ((0, 0), (0, small_rows * qkv_cols - small_len)))
    small_grads = small_grads.astype(BF).reshape(Z, X, small_rows, qkv_cols)
    gpacked = jnp.concatenate([gqkv, small_grads], 2)
    gpacked = sum_blocks(gpacked, "x", X, 1).astype(BF)
    gpacked = lax.psum_scatter(gpacked, "z")
    gpacked = gather(gather(gpacked, "y", Y, 0), "k", K, 1).reshape(C, packed_rows, qkv_cols)
    grad_query_weight = (
        jnp.moveaxis(gpacked[:, :rows_here, :cols], 0, 1).reshape(rows_here, D).astype(F32)
    )
    grad_keyval_weight = jnp.sum(gpacked[:, :rows_here, cols:].astype(F32), 0)
    small_sums = jnp.sum(gpacked[:, rows_here:].astype(F32), 0).reshape(-1)
    place = 0
    small_outs = []
    for size in [rows_here] * 7 + [ff_here, HD // S]:
        small_outs.append(small_sums[place : place + size])
        place += size

    factors = CLIP_LIMIT / jnp.maximum(top_logit, CLIP_LIMIT)
    column_scale = jnp.repeat(jnp.sqrt(factors), HD)
    clipped_query_weight = (query_weight.astype(F32) * column_scale[None, :]).astype(BF)
    bias_scale = lax.dynamic_slice_in_dim(column_scale, shard * rows_here, rows_here, 0)
    clipped_query_bias = (query_bias.astype(F32) * bias_scale).astype(BF)
    key_scale = jnp.sqrt(jnp.min(factors))
    keyval_scale = jnp.concatenate([jnp.ones((HD,), F32) * key_scale, jnp.ones((HD,), F32)])
    clipped_keyval_weight = (keyval_weight.astype(F32) * keyval_scale[None, :]).astype(BF)

    return (
        result,
        input_grad,
        small_outs[0],
        small_outs[1],
        grad_query_weight,
        small_outs[2],
        grad_keyval_weight,
        small_outs[8],
        grad_output_weight,
        small_outs[3],
        small_outs[4],
        small_outs[5],
        grad_up_weight,
        small_outs[7],
        grad_down_weight,
        small_outs[6],
        clipped_query_weight,
        clipped_query_bias,
        clipped_keyval_weight,
    )


def solution(mesh):
    ctx, fsdp = mesh.shape["ctx"], mesh.shape["fsdp"]
    sizes = (ctx // 2, 2, 4, fsdp // 4)
    fine = Mesh(mesh.devices.reshape(sizes), ("y", "k", "z", "x"))
    tokens = P(("z", "x"), ("y", "k"), None)
    vector = P(("z", "x"))
    matrix = P(("z", "x"), None)
    return jax.shard_map(
        functools.partial(body, sizes),
        mesh=fine,
        in_specs=(
            tokens, vector, vector, vector, matrix, vector, matrix, vector, matrix, vector,
            vector, vector, matrix, vector, matrix, vector, tokens,
        ),
        out_specs=(
            tokens, tokens, vector, vector, matrix, vector, matrix, vector, matrix, vector,
            vector, vector, matrix, vector, matrix, vector, matrix, vector, matrix,
        ),
        check_vma=False,
    )
```

```python
import functools
import math

import jax
import jax.numpy as jnp
from jax import lax
from jax.experimental import pallas as pl
from jax.experimental.pallas import tpu as pltpu
from jax.sharding import Mesh, PartitionSpec as P

H = 16
HD = 128
EPSILON = 1e-05
CLIP_LIMIT = 10.0
NEGATIVE = -1e30
BF = jnp.bfloat16
F32 = jnp.float32
GELU_A = 0.044715
GELU_C = math.sqrt(2.0 / math.pi)
SCALE = HD ** (-0.5)
MIB = 1 << 20


def mm(left, right):
    return jnp.dot(left, right, preferred_element_type=F32)


def mm_tn(left, right):
    return lax.dot_general(left, right, (((0,), (0,)), ((), ())), preferred_element_type=F32)


def mm_nt(left, right):
    return lax.dot_general(left, right, (((1,), (1,)), ((), ())), preferred_element_type=F32)


def shift(value, axis, count, step):
    return lax.ppermute(value, axis, [(i, (i + step) % count) for i in range(count)])


def pick(value, index, dim):
    return lax.dynamic_index_in_dim(value, index, dim, keepdims=False)


def in_order(parts, here, count, dim):
    if count == 1:
        return jnp.expand_dims(parts[0], dim)
    if count == 2:
        first = here == 0
        return jnp.stack(
            [jnp.where(first, parts[0], parts[1]), jnp.where(first, parts[1], parts[0])], dim
        )
    shape = list(parts[0].shape)
    shape.insert(dim, count)
    whole = jnp.zeros(shape, parts[0].dtype)
    for j, part in enumerate(parts):
        whole = lax.dynamic_update_index_in_dim(whole, part, lax.rem(here - j + count, count), dim)
    return whole


def gather(value, axis, count, dim):
    parts = [value] + [shift(value, axis, count, j) for j in range(1, count)]
    return in_order(parts, lax.axis_index(axis), count, dim)


def swap_blocks(value, axis, count, dim):
    here = lax.axis_index(axis)
    parts = [pick(value, here, dim)]
    for j in range(1, count):
        parts.append(shift(pick(value, lax.rem(here + j, count), dim), axis, count, j))
    return in_order(parts, here, count, dim)


def sum_blocks(value, axis, count, dim):
    here = lax.axis_index(axis)
    total = pick(value, here, dim).astype(F32)
    for j in range(1, count):
        block = pick(value, lax.rem(here + j, count), dim).astype(BF)
        total = total + shift(block, axis, count, j).astype(F32)
    return total


def sum_copies(value, axis, count):
    low = value.astype(BF)
    total = low.astype(F32)
    for j in range(1, count):
        total = total + shift(low, axis, count, j).astype(F32)
    return total


def attention_masks(rows, length):
    row = lax.broadcasted_iota(jnp.int32, (rows, rows), 0)
    col = lax.broadcasted_iota(jnp.int32, (rows, rows), 1)
    return (col <= row) & (col < length)


MESH = pl.DeviceIdType.MESH
SMALL_ROWS = 16


def sem_count(sizes):
    return 112 if sizes[0] * sizes[3] <= 4 else 240


class Move:
    def __init__(self, copy, send_if, recv_if):
        self.copy, self.send_if, self.recv_if = copy, send_if, recv_if

    def start(self):
        guarded(self.send_if, self.copy.start)

    def wait_send(self):
        guarded(self.send_if, self.copy.wait_send)

    def wait_recv(self):
        guarded(self.recv_if, self.copy.wait_recv)


def guarded(condition, action):
    if condition is None:
        action()
    else:

        @pl.when(condition)
        def _():
            action()


class Links:
    def __init__(self, sends, recvs, locals_):
        self.sends, self.recvs, self.locals_ = sends, recvs, locals_
        self.used, self.used_local = 0, 0
        self.open = []

    def plan(self, src, dst, where, send_if=None, recv_if=None):
        index = self.used
        self.used += 1
        assert self.used <= self.sends.shape[0]
        copy = pltpu.make_async_remote_copy(
            src_ref=src,
            dst_ref=dst,
            send_sem=self.sends.at[index],
            recv_sem=self.recvs.at[index],
            device_id=where,
            device_id_type=MESH,
        )
        move = Move(copy, send_if, recv_if)
        self.open.append(move)
        return move

    def push(self, src, dst, axis, target=None, when=None):
        where = axis if isinstance(axis, dict) else {axis: target}
        move = self.plan(src, dst, where, when, when)
        move.start()
        return move

    def sent(self, moves):
        for move in moves:
            move.wait_send()
            self.open = [other for other in self.open if other is not move]

    def local(self, src, dst):
        index = self.used_local
        self.used_local += 1
        assert self.used_local < self.locals_.shape[0]
        copy = pltpu.make_async_copy(src, dst, self.locals_.at[index])
        copy.start()
        return copy

    def drain(self):
        for move in self.open:
            move.wait_send()


class Line:
    def __init__(self, links, block, z, Z, source=None):
        self.z, self.Z = z, Z
        self.hops = []
        right, left = {"z": jnp.minimum(z + 1, Z - 1)}, {"z": jnp.maximum(z - 1, 0)}
        for h in range(1, Z):
            low, high = jnp.maximum(z - h + 1, 0), jnp.minimum(z + h - 1, Z - 1)
            ahead, back = block(low), block(high)
            own = source is not None and h == 1
            self.hops.append(
                [
                    links.plan(
                        source if own else ahead,
                        ahead,
                        right,
                        (z >= h - 1) & (z < Z - 1),
                        z >= h,
                    ),
                    links.plan(
                        source if own else back,
                        back,
                        left,
                        (z <= Z - h) & (z > 0),
                        z < Z - h,
                    ),
                ]
            )
        for move in self.hops[0]:
            move.start()

    def hop(self, h):
        for move in self.hops[h - 1]:
            move.wait_recv()
        if h < self.Z - 1:
            for move in self.hops[h]:
                move.start()
        z, Z = self.z, self.Z
        return [
            (jnp.maximum(z - h, 0), z >= h),
            (jnp.minimum(z + h, Z - 1), z < Z - h),
        ]


def wait_all(copies):
    for copy in copies:
        copy.wait()


def wait_recvs(copies):
    for copy in copies:
        copy.wait_recv()


def around(axis, here, count):
    return [(axis, lax.rem(here + j, count)) for j in range(1, count)]


def greet(groups, corners):
    barrier = pltpu.get_barrier_semaphore()
    count = 0
    for where in [{axis: target} for group in groups for axis, target in group] + corners:
        pl.semaphore_signal(barrier, inc=1, device_id=where, device_id_type=MESH)
        count += 1
    pl.semaphore_wait(barrier, count)


class Gather:
    def __init__(self, links, buf, place):
        self.links, self.buf, (self.z, self.Z, self.x, self.X) = links, buf, place
        self.line = Line(links, lambda at: buf.at[at * self.X + self.x], self.z, self.Z)
        self.from_x = []
        self.spread(self.z, None)

    def spread(self, at, when):
        block = self.buf.at[at * self.X + self.x]
        self.from_x += [
            self.links.push(block, block, *to, when=when) for to in around("x", self.x, self.X)
        ]

    def hop(self, h):
        for at, when in self.line.hop(h):
            self.spread(at, when)

    def finish(self):
        wait_recvs(self.from_x)


def forward_kernel(
    sizes,
    length_ref,
    rows,
    gmlp,
    wq,
    wkv,
    small,
    wo,
    up,
    down,
    seq_o,
    wqkv_o,
    wo_o,
    wup,
    wdown,
    gmall,
    ntall,
    normed_o,
    qkv_o,
    att_o,
    mid_o,
    top_o,
    vec_o,
    v_seq,
    v_hat,
    v_norm,
    v_w,
    v_small,
    v_vec,
    v_qkv,
    v_att,
    v_wo,
    v_br,
    v_brall,
    v_mid,
    v_nt,
    v_top,
    v_topz,
    v_topx,
    v_tall,
    sends,
    recvs,
    locals_,
):
    Y, K, Z, X = sizes
    C, S = Y * K, Z * X
    y, k, z, x = (lax.axis_index(name) for name in ("y", "k", "z", "x"))
    c = y * K + k
    me = z * X + x
    R, D = rows.shape
    T = C * R
    cols = D // C
    qkv_cols = cols + 2 * HD
    here = wq.shape[0]
    part = wdown.shape[1]
    heads = cols // HD
    length = length_ref[0]
    links = Links(sends, recvs, locals_)
    place = (z, Z, x, X)
    to_z, to_x = around("z", z, Z), around("x", x, X)
    to_y, to_k = around("y", y, Y), around("k", k, K)
    zs = [lax.rem(z - j + Z, Z) for j in range(Z)]
    ys = [lax.rem(y - j + Y, Y) for j in range(Y)]
    others = [
        (lax.rem(y + jy, Y), lax.rem(k + jk, K))
        for jy in range(Y)
        for jk in range(K)
        if jy or jk
    ]
    corners = [
        {"y": lax.rem(y + jy, Y), "k": lax.rem(k + jk, K)}
        for jy in range(1, Y)
        for jk in range(1, K)
    ]

    greet([to_z, to_x, to_y, to_k], corners)

    first = [
        links.local(wq.at[:, pl.ds(pl.multiple_of(c * cols, cols), cols)], v_w.at[me, :, pl.ds(0, cols)]),
        links.local(wkv, v_w.at[me, :, pl.ds(cols, 2 * HD)]),
        links.local(small, v_small.at[me]),
        links.local(rows, v_seq.at[pl.ds(c * R, R)]),
    ]
    own_wo = links.local(wo.at[:, pl.ds(pl.multiple_of(c * cols, cols), cols)], v_wo.at[me])
    wait_all(first)
    qkv_gather = Gather(links, v_w, place)
    small_gather = Gather(links, v_small, place)
    mine = v_seq.at[pl.ds(c * R, R)]
    seq_y = [links.push(mine, mine, *to) for to in to_y]
    seq_k = [links.push(mine, mine, *to) for to in to_k]
    for j in range(1, Y):
        seq_y[j - 1].wait_recv()
        block = v_seq.at[pl.ds((ys[j] * K + k) * R, R)]
        seq_k += [links.push(block, block, *to) for to in to_k]
    qkv_gather.hop(1)
    small_gather.hop(1)
    wait_recvs(seq_k)
    save_seq = links.local(v_seq, seq_o)

    step = 64

    @pl.loop(0, T // step)
    def _(i):
        span = pl.ds(pl.multiple_of(i * step, step), step)
        values = v_seq[span, :].astype(F32)
        center = values - jnp.mean(values, 1, keepdims=True)
        rstd = lax.rsqrt(jnp.mean(center * center, 1, keepdims=True) + EPSILON)
        v_hat[span, :] = center * rstd

    qkv_gather.hop(2)
    small_gather.hop(2)
    own_wo.wait()
    wo_gather = Gather(links, v_wo, place)
    qkv_gather.hop(3)
    small_gather.hop(3)

    slab = here // Y
    slab_y = pl.ds(pl.multiple_of(y * slab, slab), slab)
    own_up, up_z, up_x, up_y = [], [], [], []
    for j in range(Z):
        target = lax.rem(z + j, Z)
        for i in range(X):
            unit = pl.ds(pl.multiple_of(((target * X + i) * K + k) * part, part), part)
            side = pl.ds(i * part, part)
            if j == 0:
                own_up.append(links.local(up.at[:, unit], wup.at[me, :, side]))
            else:
                up_z.append(
                    links.push(up.at[slab_y, unit], wup.at[me, slab_y, side], "z", target)
                )

    def up_on(at, axis, to):
        block = wup.at[at, slab_y]
        return links.push(block, block, *to)

    qkv_gather.finish()
    small_gather.finish()
    piece = part // Y
    own_down = links.local(down.at[pl.ds(pl.multiple_of(k * part, part), part)], wdown.at[x])
    down_src = down.at[pl.ds(pl.multiple_of(k * part + y * piece, piece), piece)]
    piece_y = pl.ds(pl.multiple_of(y * piece, piece), piece)
    down_x = [links.push(down_src, wdown.at[x, piece_y], *to) for to in to_x]
    own_gm = links.local(gmlp, gmall.at[z, k])
    gm_line = Line(links, lambda at: gmall.at[at, k], z, Z, gmlp)
    gm_k = [links.push(gmlp, gmall.at[z, k], *to) for to in to_k]

    def gm_hop(h):
        for at, when in gm_line.hop(h):
            gm_k.extend(
                links.push(gmall.at[at, k], gmall.at[at, k], *to, when=when) for to in to_k
            )

    wo_gather.hop(1)

    for s in range(S):
        v_vec[:, pl.ds(s * here, here)] = v_small[s]
    gain = v_vec[0:1, :].astype(F32)
    bias = v_vec[1:2, :].astype(F32)

    @pl.loop(0, T // step)
    def _(i):
        span = pl.ds(pl.multiple_of(i * step, step), step)
        v_norm[span, :] = (v_hat[span, :] * gain + bias).astype(BF)

    save_norm = links.local(v_norm, normed_o)
    save_vec = links.local(v_vec, vec_o)
    q_bias = v_vec[2:3, pl.ds(pl.multiple_of(c * cols, cols), cols)].astype(F32)
    v_bias = jnp.zeros((1, HD), F32)
    for s in range(S):
        v_bias = v_bias + v_small[s, 12:13, 0:HD].astype(F32)
    wide = min(cols, 256)
    for n in range(cols // wide):
        span = slice(n * wide, (n + 1) * wide)
        weights = v_w[:, :, span].reshape(D, wide)
        v_qkv[:, span] = (mm(v_norm[...], weights) + q_bias[:, span]).astype(BF)
    weights = v_w[:, :, cols:].reshape(D, 2 * HD)
    kv_bias = jnp.concatenate([jnp.zeros((1, HD), F32), v_bias], 1)
    v_qkv[:, cols:] = (mm(v_norm[...], weights) + kv_bias).astype(BF)
    save_qkv = links.local(v_qkv, qkv_o)
    wo_gather.hop(2)

    @pl.loop(0, heads)
    def _(n):
        span = pl.ds(pl.multiple_of(n * HD, HD), HD)
        scores = mm_nt(v_qkv[:, span], v_qkv[:, cols : cols + HD]) * SCALE
        masked = jnp.where(attention_masks(T, length), scores, NEGATIVE)
        top = jnp.max(masked, 1, keepdims=True)
        weights = jnp.exp(masked - top)
        probs = (weights / jnp.sum(weights, 1, keepdims=True)).astype(BF)
        own = pl.ds(pl.multiple_of(c * cols + n * HD, HD), HD)
        v_att[:, own] = mm(probs, v_qkv[:, cols + HD :]).astype(BF)
        live = lax.broadcasted_iota(jnp.int32, (T, 1), 0) < length
        best = jnp.max(jnp.where(live, top, NEGATIVE), 0, keepdims=True)
        v_top[pl.ds(n, 1), :] = jnp.broadcast_to(best, (1, HD))

    def att_block(source):
        return v_att.at[:, pl.ds(pl.multiple_of(source * cols, cols), cols)]

    att_y = [links.push(att_block(c), att_block(c), *to) for to in to_y]
    att_k = [links.push(att_block(c), att_block(c), *to) for to in to_k]
    top_z = [links.push(v_top, v_topz.at[j], *to) for j, to in enumerate(to_z)]
    wo_gather.hop(3)
    gm_hop(1)
    wait_all(own_up)
    up_x += [up_on(me, "x", to) for to in to_x]
    for j in range(1, Y):
        att_y[j - 1].wait_recv()
        att_k += [links.push(att_block(ys[j] * K + k), att_block(ys[j] * K + k), *to) for to in to_k]
    wait_recvs(top_z)
    best = v_top[...]
    for j in range(Z - 1):
        best = jnp.maximum(best, v_topz[j])
    v_topx[0] = best
    top_x = [links.push(v_topx.at[0], v_topx.at[j + 1], *to) for j, to in enumerate(to_x)]
    wait_recvs(att_k)
    save_att = links.local(v_att, att_o)
    wo_gather.finish()

    narrow = min(cols, 256)
    for n in range(cols // narrow):
        span = slice(n * narrow, (n + 1) * narrow)
        weights = v_wo[:, :, span].reshape(D, narrow)
        v_br[:, :, span] = mm(v_att[...], weights).astype(BF).reshape(C, R, narrow)
    br_in = []
    for ty, tk in others:
        br_in.append(links.push(v_br.at[ty * K + tk], v_brall.at[c], {"y": ty, "k": tk}, None))
    v_brall[c] = v_br[c]
    down_y = []
    for j, move in enumerate(down_x):
        move.wait_recv()
        block = wdown.at[lax.rem(x - j - 1 + X, X), piece_y]
        down_y += [links.push(block, block, *to) for to in to_y]
    for j in (1, Z - 1, 2):
        wait_recvs(up_z[(j - 1) * X : j * X])
        up_x += [up_on(zs[j] * X + x, "x", to) for to in to_x]
        up_y += [up_on(zs[j] * X + x, "y", to) for to in to_y]
    gm_hop(2)
    wait_recvs(top_x)
    best = v_topx[0]
    for j in range(1, X):
        best = jnp.maximum(best, v_topx[j])
    v_tall[c] = best
    top_y = [links.push(v_tall.at[c], v_tall.at[c], *to) for to in to_y]
    top_k = [links.push(v_tall.at[c], v_tall.at[c], *to) for to in to_k]
    wait_recvs(br_in)

    for q in range(C):
        span = slice(q * cols, (q + 1) * cols)
        rows_in = v_seq[pl.ds(pl.multiple_of(c * R, R), R), span].astype(F32)
        v_mid[:, span] = rows_in + v_brall[q].astype(F32) + v_vec[3:4, span].astype(F32)
    save_mid = links.local(v_mid, mid_o)
    gain_two = v_vec[4:5, :].astype(F32)
    bias_two = v_vec[5:6, :].astype(F32)

    @pl.loop(0, R // step)
    def _(i):
        span = pl.ds(pl.multiple_of(i * step, step), step)
        values = v_mid[span, :]
        center = values - jnp.mean(values, 1, keepdims=True)
        rstd = lax.rsqrt(jnp.mean(center * center, 1, keepdims=True) + EPSILON)
        v_nt[span, :] = (center * rstd * gain_two + bias_two).astype(BF)

    own_nt = links.local(v_nt, ntall.at[z, k])
    nt_line = Line(links, lambda at: ntall.at[at, k], z, Z, v_nt)
    nt_k = [links.push(v_nt, ntall.at[z, k], *to) for to in to_k]

    def nt_hop(h):
        for at, when in nt_line.hop(h):
            nt_k.extend(
                links.push(ntall.at[at, k], ntall.at[at, k], *to, when=when) for to in to_k
            )

    for j in range(1, Y):
        top_y[j - 1].wait_recv()
        block = v_tall.at[ys[j] * K + k]
        top_k += [links.push(block, block, *to) for to in to_k]
    wait_recvs(top_k)
    save_top = links.local(v_tall, top_o)

    nt_hop(1)
    order = [0, 1, Z - 1, 2]
    for place_x, j in enumerate(order):
        for i in range(1, X):
            up_x[place_x * (X - 1) + i - 1].wait_recv()
            block_at = zs[j] * X + lax.rem(x - i + X, X)
            up_y += [up_on(block_at, "y", to) for to in to_y]
    gm_hop(3)
    nt_hop(2)
    nt_hop(3)
    save_w = links.local(v_w, wqkv_o)
    save_wo = links.local(v_wo, wo_o)
    wait_recvs(down_y + up_y + gm_k + nt_k)
    wait_all(
        [own_down, own_gm, own_nt, save_seq, save_norm, save_vec, save_qkv, save_att, save_mid]
        + [save_top, save_w, save_wo]
    )
    links.drain()


def forward_call(sizes, lengths, rows, gmlp, wq, wkv, small, wo, up, down):
    Y, K, Z, X = sizes
    C, S = Y * K, Z * X
    R, D = rows.shape
    T = C * R
    cols = D // C
    qkv_cols = cols + 2 * HD
    here = wq.shape[0]
    part = down.shape[0] // K
    heads = cols // HD
    shape = jax.ShapeDtypeStruct
    anywhere = pl.BlockSpec(memory_space=pl.ANY)
    outs = [
        shape((T, D), BF),
        shape((S, here, qkv_cols), BF),
        shape((S, here, cols), BF),
        shape((S, here, X * part), BF),
        shape((X, part, D), BF),
        shape((Z, K, R, D), BF),
        shape((Z, K, R, D), BF),
        shape((T, D), BF),
        shape((T, qkv_cols), BF),
        shape((T, D), BF),
        shape((R, D), F32),
        shape((C, 8, HD), F32),
        shape((SMALL_ROWS, D), BF),
    ]
    return pl.pallas_call(
        functools.partial(forward_kernel, sizes),
        in_specs=[pl.BlockSpec(memory_space=pltpu.SMEM)] + [anywhere] * 8,
        out_specs=[anywhere] * len(outs),
        out_shape=outs,
        scratch_shapes=[
            pltpu.VMEM((T, D), BF),
            pltpu.VMEM((T, D), F32),
            pltpu.VMEM((T, D), BF),
            pltpu.VMEM((S, here, qkv_cols), BF),
            pltpu.VMEM((S, SMALL_ROWS, here), BF),
            pltpu.VMEM((SMALL_ROWS, D), BF),
            pltpu.VMEM((T, qkv_cols), BF),
            pltpu.VMEM((T, D), BF),
            pltpu.VMEM((S, here, cols), BF),
            pltpu.VMEM((C, R, cols), BF),
            pltpu.VMEM((C, R, cols), BF),
            pltpu.VMEM((R, D), F32),
            pltpu.VMEM((R, D), BF),
            pltpu.VMEM((8, HD), F32),
            pltpu.VMEM((Z - 1, 8, HD), F32),
            pltpu.VMEM((X, 8, HD), F32),
            pltpu.VMEM((C, 8, HD), F32),
            pltpu.SemaphoreType.DMA((sem_count(sizes),)),
            pltpu.SemaphoreType.DMA((sem_count(sizes),)),
            pltpu.SemaphoreType.DMA((32,)),
        ],
        compiler_params=pltpu.CompilerParams(
            collective_id=1, has_side_effects=True, vmem_limit_bytes=60 * MIB
        ),
        name="layer_forward",
    )(lengths, rows, gmlp, wq, wkv, small, wo, up, down)


def rows_loop(total, step, work):
    @pl.loop(0, total // step)
    def _(i):
        work(pl.ds(pl.multiple_of(i * step, step), step))


def backward_kernel(
    sizes,
    length_ref,
    rows,
    gmlp,
    mid,
    seq,
    normed,
    qkv,
    att,
    wqkv,
    wo,
    vec,
    gub,
    g2part,
    mlppart,
    gdown,
    gup,
    result_o,
    igrad_o,
    gdown_o,
    gup_o,
    gwo_o,
    gwq_o,
    gkv_o,
    small_o,
    h_dx,
    h_dy,
    h_ux,
    h_us,
    h_uy,
    h_ds,
    v_own,
    v_kin,
    v_zin,
    m_own,
    m_kin,
    m_zin,
    v_rows,
    v_gm,
    v_mid,
    v_hat,
    v_vec,
    v_gbr,
    v_gbc,
    v_wo,
    v_ga,
    v_gak,
    v_gay,
    v_gatt,
    v_big,
    v_norm,
    v_qkv,
    v_gqkv,
    v_gk,
    v_gv,
    v_wqkv,
    v_dwo,
    v_dwox,
    v_dwoz,
    v_dwq,
    v_dwqx,
    v_dwqz,
    v_g1k,
    v_g1y,
    v_mean,
    v_rstd,
    v_sg,
    v_sgb,
    v_sgx,
    v_sgz,
    v_sga,
    v_gub,
    v_a,
    v_b,
    v_out,
    sends,
    recvs,
    locals_,
):
    Y, K, Z, X = sizes
    C, S = Y * K, Z * X
    y, k, z, x = (lax.axis_index(name) for name in ("y", "k", "z", "x"))
    c = y * K + k
    me = z * X + x
    R, D = rows.shape
    T = C * R
    cols = D // C
    here = wqkv.shape[1]
    part = gdown.shape[1]
    heads = cols // HD
    step = 64
    length = length_ref[0]
    links = Links(sends, recvs, locals_)
    to_z, to_x = around("z", z, Z), around("x", x, X)
    to_y, to_k = around("y", y, Y), around("k", k, K)
    zs = [lax.rem(z - j + Z, Z) for j in range(Z)]
    ys = [lax.rem(y - j + Y, Y) for j in range(Y)]
    others = [
        (lax.rem(y + jy, Y), lax.rem(k + jk, K))
        for jy in range(Y)
        for jk in range(K)
        if jy or jk
    ]
    corners = [
        {"y": lax.rem(y + jy, Y), "k": lax.rem(k + jk, K)}
        for jy in range(1, Y)
        for jk in range(1, K)
    ]

    greet([to_z, to_x, to_y, to_k], corners)

    g2_k = [links.push(g2part.at[:, t], v_kin.at[j], a, t) for j, (a, t) in enumerate(to_k)]
    own_g2 = links.local(g2part.at[:, k], v_own)
    load = [
        links.local(rows, v_rows),
        links.local(gmlp, v_gm),
        links.local(mid, v_mid),
        links.local(vec, v_vec),
        links.local(wo, v_wo),
        links.local(gub, v_gub),
        links.local(att, v_big),
        links.local(qkv, v_qkv),
        links.local(normed, v_norm),
        links.local(wqkv, v_wqkv),
    ]
    gd_x = [links.push(gdown.at[t], h_dx.at[j], a, t) for j, (a, t) in enumerate(to_x)]
    gu_x = [links.push(gup.at[:, t], h_ux.at[j], a, t) for j, (a, t) in enumerate(to_x)]

    def add_into(own, extra, count):
        for block in range(Z):

            def work(span, block=block):
                total = own[block, span, :].astype(F32)
                for j in range(count):
                    total = total + extra[j, block, span, :].astype(F32)
                own[block, span, :] = total.astype(BF)

            rows_loop(R, step, work)

    own_g2.wait()
    wait_recvs(g2_k)
    add_into(v_own, v_kin, K - 1)
    g2_z = [links.push(v_own.at[t], v_zin.at[j], a, t) for j, (a, t) in enumerate(to_z)]
    mlp_k = [links.push(mlppart.at[:, t], m_kin.at[j], a, t) for j, (a, t) in enumerate(to_k)]
    own_mlp = links.local(mlppart.at[:, k], m_own)
    wait_all(load)

    v_sg[...] = jnp.zeros_like(v_sg)

    def second_norm(span):
        values = v_mid[span, :]
        center = values - jnp.mean(values, 1, keepdims=True)
        rstd = lax.rsqrt(jnp.mean(center * center, 1, keepdims=True) + EPSILON)
        v_hat[span, :] = center * rstd
        v_rstd[span, :] = jnp.broadcast_to(rstd, (step, HD))
        v_sg[6:7, :] += jnp.sum(v_gm[span, :].astype(F32), 0, keepdims=True)

    rows_loop(R, step, second_norm)
    own_mlp.wait()
    wait_recvs(mlp_k)
    add_into(m_own, m_kin, K - 1)
    gain_two = v_vec[4:5, :].astype(F32)
    wait_recvs(g2_z)

    def second_back(span):
        grad = v_own[z, span, :].astype(F32)
        for j in range(Z - 1):
            grad = grad + v_zin[j, span, :].astype(F32)
        hat = v_hat[span, :]
        v_sg[4:5, :] += jnp.sum(grad * hat, 0, keepdims=True)
        v_sg[5:6, :] += jnp.sum(grad, 0, keepdims=True)
        scaled = grad * gain_two
        back = v_rstd[span, 0:1] * (
            scaled
            - jnp.mean(scaled, 1, keepdims=True)
            - hat * jnp.mean(scaled * hat, 1, keepdims=True)
        )
        grad_middle = v_gm[span, :].astype(F32) + back
        v_hat[span, :] = grad_middle
        low = grad_middle.astype(BF)
        v_sg[3:4, :] += jnp.sum(low.astype(F32), 0, keepdims=True)
        for q in range(C):
            v_gbr[q, span, :] = low[:, q * cols : (q + 1) * cols]

    rows_loop(R, step, second_back)
    gb = []
    for ty, tk in others:
        gb.append(links.push(v_gbr.at[ty * K + tk], v_gbc.at[c], {"y": ty, "k": tk}, None))
    v_gbc[c] = v_gbr[c]
    mlp_z = [links.push(m_own.at[t], m_zin.at[j], a, t) for j, (a, t) in enumerate(to_z)]
    wait_recvs(gb)

    grads_c = v_gbc[...].reshape(T, cols)
    per = cols // here
    for s in range(S):
        span = slice((s % per) * here, (s % per + 1) * here)
        v_ga[s // per, :, span] = mm_nt(grads_c, v_wo[s]).astype(BF)
    ga_k = [
        links.push(v_ga.at[q * K + t], v_gak.at[j, q], a, t)
        for j, (a, t) in enumerate(to_k)
        for q in range(Y)
    ]
    for s in range(S):
        v_dwo[s // X, s % X] = mm_tn(
            v_big[:, s * here : (s + 1) * here], v_gbc[...].reshape(T, cols)
        ).astype(BF)
    do_x = [links.push(v_dwo.at[:, t], v_dwox.at[j], a, t) for j, (a, t) in enumerate(to_x)]
    load_seq = links.local(seq, v_big)
    wait_recvs(ga_k)
    for q in range(Y):

        def ga_sum(span, q=q):
            total = v_ga[q * K + k, span, :].astype(F32)
            for j in range(K - 1):
                total = total + v_gak[j, q, span, :].astype(F32)
            v_gak[0, q, span, :] = total.astype(BF)

        rows_loop(T, step, ga_sum)
    ga_y = [links.push(v_gak.at[0, t], v_gay.at[j], a, t) for j, (a, t) in enumerate(to_y)]
    load_seq.wait()

    def stats(span):
        values = v_big[span, :].astype(F32)
        mean = jnp.mean(values, 1, keepdims=True)
        center = values - mean
        rstd = lax.rsqrt(jnp.mean(center * center, 1, keepdims=True) + EPSILON)
        v_mean[span, :] = jnp.broadcast_to(mean, (step, HD))
        v_rstd[span, :] = jnp.broadcast_to(rstd, (step, HD))

    rows_loop(T, step, stats)
    wait_recvs(ga_y)

    def ga_last(span):
        total = v_gak[0, y, span, :].astype(F32)
        for j in range(Y - 1):
            total = total + v_gay[j, span, :].astype(F32)
        v_gatt[span, :] = total.astype(BF)

    rows_loop(T, step, ga_last)

    v_gk[...] = jnp.zeros_like(v_gk)
    v_gv[...] = jnp.zeros_like(v_gv)

    @pl.loop(0, heads)
    def _(n):
        span = pl.ds(pl.multiple_of(n * HD, HD), HD)
        keys = v_qkv[:, cols : cols + HD]
        scores = mm_nt(v_qkv[:, span], keys) * SCALE
        masked = jnp.where(attention_masks(T, length), scores, NEGATIVE)
        weights = jnp.exp(masked - jnp.max(masked, 1, keepdims=True))
        weights = weights / jnp.sum(weights, 1, keepdims=True)
        grads = v_gatt[:, span]
        grad_weights = mm_nt(grads, v_qkv[:, cols + HD :])
        delta = jnp.sum(weights * grad_weights, 1, keepdims=True)
        grad_scores = (weights * (grad_weights - delta)).astype(BF)
        v_gqkv[:, span] = (mm(grad_scores, keys) * SCALE).astype(BF)
        v_gk[...] += mm_tn(grad_scores, v_qkv[:, span]) * SCALE
        v_gv[...] += mm_tn(weights.astype(BF), grads)

    v_gqkv[:, cols : cols + HD] = v_gk[...].astype(BF)
    v_gqkv[:, cols + HD :] = v_gv[...].astype(BF)
    for s in range(S):
        v_dwq[s // X, s % X] = mm_tn(v_norm[:, s * here : (s + 1) * here], v_gqkv[...]).astype(BF)
    dq_x = [links.push(v_dwq.at[:, t], v_dwqx.at[j], a, t) for j, (a, t) in enumerate(to_x)]

    for s in range(S):
        span = slice(s * here, (s + 1) * here)
        grad = mm_nt(v_gqkv[...], v_wqkv[s])
        v_norm[:, span] = grad.astype(BF)
        hat = (v_big[:, span].astype(F32) - v_mean[:, 0:1]) * v_rstd[:, 0:1]
        v_sg[0:1, span] = jnp.sum(grad * hat, 0, keepdims=True)
        v_sg[1:2, span] = jnp.sum(grad, 0, keepdims=True)

    def chunk(ref, q, t):
        return ref.at[pl.ds(pl.multiple_of((q * K + t) * R, R), R)]

    g1_k = [
        links.push(chunk(v_norm, q, t), v_g1k.at[j, q], a, t)
        for j, (a, t) in enumerate(to_k)
        for q in range(Y)
    ]

    v_sg[2:3, pl.ds(pl.multiple_of(c * cols, cols), cols)] = jnp.sum(
        v_gqkv[:, 0:cols].astype(F32), 0, keepdims=True
    )
    value_sum = jnp.sum(v_gqkv[:, cols + HD :].astype(F32), 0, keepdims=True)
    for s in range(S):
        v_sg[12:13, s * here : s * here + HD] = value_sum
    units = part // here
    for i in range(X):
        to = pl.ds(pl.multiple_of((z * X + i) * here, here), here)
        for r in range(units):
            start = i * part + r * here
            bias_part = v_gub[0:1, start : start + here]
            for kk in range(K):
                row = 8 + kk * units + r
                v_sg[row : row + 1, to] = jnp.where(k == kk, bias_part, 0.0)
    for s in range(S):
        v_sgb[s // X, s % X] = v_sg[:, s * here : (s + 1) * here]
    sg_x = [links.push(v_sgb.at[:, t], v_sgx.at[j], a, t) for j, (a, t) in enumerate(to_x)]

    wait_recvs(gd_x)
    half = v_a.shape[0]

    def add_blocks(pairs, target, width):
        count = target.shape[0]

        @pl.loop(0, count // half)
        def _(i):
            span = pl.ds(pl.multiple_of(i * half, half), half)
            sem = locals_.at[63]
            for n, source in enumerate(pairs):
                buf = v_a if n == 0 else v_b
                copy = pltpu.make_async_copy(source.at[span], buf.at[:, pl.ds(0, width)], sem)
                copy.start()
                copy.wait()
                if n > 0:

                    def work(inner):
                        v_out[inner, 0:width] = (
                            (v_a if n == 1 else v_out)[inner, 0:width].astype(F32)
                            + v_b[inner, 0:width].astype(F32)
                        ).astype(BF)

                    rows_loop(half, step, work)
            copy = pltpu.make_async_copy(v_out.at[:, pl.ds(0, width)], target.at[span], sem)
            copy.start()
            copy.wait()

    add_blocks([gdown.at[x]] + [h_dx.at[j] for j in range(X - 1)], gdown_o.at[k], D)
    gd_y = [links.push(gdown_o.at[k], h_dy.at[j], *to) for j, to in enumerate(to_y)]

    wait_recvs(gu_x)
    for q in range(Z):
        add_blocks(
            [gup.at[q, x]] + [h_ux.at[j, q] for j in range(X - 1)], h_us.at[q], X * part
        )
    slab = here // Y

    def slab_of(ref, t):
        return ref.at[:, pl.ds(pl.multiple_of(t * slab, slab), slab)]

    gu_y = [
        links.push(slab_of(h_us, t), h_uy.at[j], a, t) for j, (a, t) in enumerate(to_y)
    ]

    wait_recvs(g1_k)
    for q in range(Y):

        def g1_sum(span, q=q):
            own = pl.ds(pl.multiple_of((q * K + k) * R + span.start, step), step)
            total = v_norm[own, :].astype(F32)
            for j in range(K - 1):
                total = total + v_g1k[j, q, span, :].astype(F32)
            v_g1k[0, q, span, :] = total.astype(BF)

        rows_loop(R, step, g1_sum)
    g1_y = [links.push(v_g1k.at[0, t], v_g1y.at[j], a, t) for j, (a, t) in enumerate(to_y)]

    def sum_x(own, extra, copies):
        wait_recvs(copies)
        for q in range(Z):
            total = own[q, x].astype(F32)
            for j in range(X - 1):
                total = total + extra[j, q].astype(F32)
            extra[0, q] = total.astype(extra.dtype)

    sum_x(v_dwo, v_dwox, do_x)
    do_z = [links.push(v_dwox.at[0, t], v_dwoz.at[j], a, t) for j, (a, t) in enumerate(to_z)]
    sum_x(v_dwq, v_dwqx, dq_x)
    dq_z = [links.push(v_dwqx.at[0, t], v_dwqz.at[j], a, t) for j, (a, t) in enumerate(to_z)]
    sum_x(v_sgb, v_sgx, sg_x)
    sg_z = [links.push(v_sgx.at[0, t], v_sgz.at[j], a, t) for j, (a, t) in enumerate(to_z)]

    wait_recvs(gu_y)
    for q in range(Z):
        load_a = links.local(
            h_us.at[q, pl.ds(pl.multiple_of(y * slab, slab), slab)],
            v_a.at[pl.ds(0, slab), pl.ds(0, X * part)],
        )
        load_a.wait()
        total = v_a[0:slab, 0 : X * part].astype(F32)
        for j in range(Y - 1):
            load_b = links.local(h_uy.at[j, q], v_b.at[pl.ds(0, slab), pl.ds(0, X * part)])
            load_b.wait()
            total = total + v_b[0:slab, 0 : X * part].astype(F32)
        v_out[0:slab, 0 : X * part] = total.astype(BF)
        store = links.local(
            v_out.at[pl.ds(0, slab), pl.ds(0, X * part)],
            h_us.at[q, pl.ds(pl.multiple_of(y * slab, slab), slab)],
        )
        store.wait()
    own_rows = pl.ds(pl.multiple_of(y * slab, slab), slab)
    gu_z = []
    own_gu = []
    for i in range(X):
        span = pl.ds(i * part, part)
        own_gu.append(
            links.local(h_us.at[z, own_rows, span], gup_o.at[z * X + i, k, own_rows])
        )
        for a, t in to_z:
            gu_z.append(
                links.push(h_us.at[t, own_rows, span], gup_o.at[z * X + i, k, own_rows], a, t)
            )

    d_bias = v_vec[6:7, :].astype(F32)
    wait_recvs(mlp_z)

    def finish_result(span):
        total = m_own[z, span, :].astype(F32)
        for j in range(Z - 1):
            total = total + m_zin[j, span, :].astype(F32)
        row = lax.broadcasted_iota(jnp.int32, (step, 1), 0) + span.start + c * R
        value = v_mid[span, :] + total + d_bias
        m_kin[0, 0, span, :] = jnp.where(row < length, value, 0.0).astype(BF)

    rows_loop(R, step, finish_result)
    save_result = links.local(m_kin.at[0, 0], result_o)

    gain_one = v_vec[0:1, :].astype(F32)
    wait_recvs(g1_y)

    def finish_input(span):
        grad = v_g1k[0, y, span, :].astype(F32)
        for j in range(Y - 1):
            grad = grad + v_g1y[j, span, :].astype(F32)
        values = v_rows[span, :].astype(F32)
        center = values - jnp.mean(values, 1, keepdims=True)
        rstd = lax.rsqrt(jnp.mean(center * center, 1, keepdims=True) + EPSILON)
        hat = center * rstd
        scaled = grad * gain_one
        back = rstd * (
            scaled
            - jnp.mean(scaled, 1, keepdims=True)
            - hat * jnp.mean(scaled * hat, 1, keepdims=True)
        )
        v_kin[0, 0, span, :] = (v_hat[span, :] + back).astype(BF)

    rows_loop(R, step, finish_input)
    save_input = links.local(v_kin.at[0, 0], igrad_o)

    wait_recvs(gd_y)
    add_blocks([gdown_o.at[k]] + [h_dy.at[j] for j in range(Y - 1)], h_ds, D)
    links.sent(gd_y)
    own_gd = links.local(h_ds, gdown_o.at[k])
    gd_k = [links.push(h_ds, gdown_o.at[k], *to) for to in to_k]

    def sum_z(own, extra, copies):
        wait_recvs(copies)
        total = own[0, z].astype(F32)
        for j in range(Z - 1):
            total = total + extra[j].astype(F32)
        extra[0] = total.astype(extra.dtype)

    block_c = pl.ds(pl.multiple_of(c * cols, cols), cols)

    def cols_of(q):
        return pl.ds(pl.multiple_of(q * cols, cols), cols)

    sum_z(v_dwox, v_dwoz, do_z)
    last = [links.local(v_dwoz.at[0], gwo_o.at[:, block_c])]
    wo_y = [links.push(v_dwoz.at[0], gwo_o.at[:, block_c], *to) for to in to_y]
    wo_k = [links.push(v_dwoz.at[0], gwo_o.at[:, block_c], *to) for to in to_k]

    wait_all(own_gu)
    wait_recvs(gu_z)
    mine = gup_o.at[:, k, own_rows]
    gu_y2 = [links.push(mine, mine, *to) for to in to_y]

    sum_z(v_dwqx, v_dwqz, dq_z)
    wide = pl.ds(0, cols)
    tail = pl.ds(cols, 2 * HD)
    last.append(links.local(v_dwqz.at[0, :, wide], gwq_o.at[:, block_c]))
    last.append(links.local(v_dwqz.at[0, :, tail], gkv_o.at[c]))
    wq_y = [links.push(v_dwqz.at[0, :, wide], gwq_o.at[:, block_c], *to) for to in to_y]
    wq_k = [links.push(v_dwqz.at[0, :, wide], gwq_o.at[:, block_c], *to) for to in to_k]
    kv_y = [links.push(v_dwqz.at[0, :, tail], gkv_o.at[c], *to) for to in to_y]
    kv_k = [links.push(v_dwqz.at[0, :, tail], gkv_o.at[c], *to) for to in to_k]
    sum_z(v_sgx, v_sgz, sg_z)
    v_sga[c] = v_sgz[0]
    sg_y = [links.push(v_sga.at[c], v_sga.at[c], *to) for to in to_y]
    sg_k = [links.push(v_sga.at[c], v_sga.at[c], *to) for to in to_k]

    for j in range(1, Y):
        q = ys[j] * K + k
        wo_y[j - 1].wait_recv()
        wo_k += [links.push(gwo_o.at[:, cols_of(q)], gwo_o.at[:, cols_of(q)], *to) for to in to_k]
        wq_y[j - 1].wait_recv()
        wq_k += [links.push(gwq_o.at[:, cols_of(q)], gwq_o.at[:, cols_of(q)], *to) for to in to_k]
        kv_y[j - 1].wait_recv()
        kv_k += [links.push(gkv_o.at[q], gkv_o.at[q], *to) for to in to_k]
        sg_y[j - 1].wait_recv()
        sg_k += [links.push(v_sga.at[q], v_sga.at[q], *to) for to in to_k]
    wait_recvs(gu_y2)
    gu_k = [links.push(gup_o.at[:, k], gup_o.at[:, k], *to) for to in to_k]
    wait_recvs(sg_k)
    total = v_sga[0]
    for q in range(1, C):
        total = total + v_sga[q]
    v_sgz[0] = total
    last.append(links.local(v_sgz.at[0], small_o))
    wait_recvs(gd_k + wo_k + wq_k + kv_k + gu_k)
    wait_all(last + [own_gd, save_result, save_input])
    links.drain()


def backward_call(sizes, lengths, rows, gmlp, mid, seq, normed, qkv, att, wqkv, wo, vec, gub,
                  g2part, mlppart, gdown, gup):
    Y, K, Z, X = sizes
    C, S = Y * K, Z * X
    R, D = rows.shape
    T = C * R
    cols = D // C
    qkv_cols = cols + 2 * HD
    here = wqkv.shape[1]
    part = gdown.shape[1]
    half = min(part, here)
    shape = jax.ShapeDtypeStruct
    anywhere = pl.BlockSpec(memory_space=pl.ANY)
    outs = [
        shape((R, D), BF),
        shape((R, D), BF),
        shape((K, part, D), BF),
        shape((S, K, here, part), BF),
        shape((here, D), BF),
        shape((here, D), BF),
        shape((C, here, 2 * HD), BF),
        shape((SMALL_ROWS, here), F32),
        shape((X - 1, part, D), BF),
        shape((Y - 1, part, D), BF),
        shape((X - 1, Z, here, X * part), BF),
        shape((Z, here, X * part), BF),
        shape((Y - 1, Z, here // Y, X * part), BF),
        shape((part, D), BF),
    ]
    return pl.pallas_call(
        functools.partial(backward_kernel, sizes),
        in_specs=[pl.BlockSpec(memory_space=pltpu.SMEM)] + [anywhere] * 15,
        out_specs=[anywhere] * len(outs),
        out_shape=outs,
        scratch_shapes=[
            pltpu.VMEM((Z, R, D), BF),
            pltpu.VMEM((K - 1, Z, R, D), BF),
            pltpu.VMEM((Z - 1, R, D), BF),
            pltpu.VMEM((Z, R, D), BF),
            pltpu.VMEM((K - 1, Z, R, D), BF),
            pltpu.VMEM((Z - 1, R, D), BF),
            pltpu.VMEM((R, D), BF),
            pltpu.VMEM((R, D), BF),
            pltpu.VMEM((R, D), F32),
            pltpu.VMEM((R, D), F32),
            pltpu.VMEM((SMALL_ROWS, D), BF),
            pltpu.VMEM((C, R, cols), BF),
            pltpu.VMEM((C, R, cols), BF),
            pltpu.VMEM((S, here, cols), BF),
            pltpu.VMEM((C, T, cols), BF),
            pltpu.VMEM((K - 1, Y, T, cols), BF),
            pltpu.VMEM((Y - 1, T, cols), BF),
            pltpu.VMEM((T, cols), BF),
            pltpu.VMEM((T, D), BF),
            pltpu.VMEM((T, D), BF),
            pltpu.VMEM((T, qkv_cols), BF),
            pltpu.VMEM((T, qkv_cols), BF),
            pltpu.VMEM((T, HD), F32),
            pltpu.VMEM((T, HD), F32),
            pltpu.VMEM((S, here, qkv_cols), BF),
            pltpu.VMEM((Z, X, here, cols), BF),
            pltpu.VMEM((X - 1, Z, here, cols), BF),
            pltpu.VMEM((Z - 1, here, cols), BF),
            pltpu.VMEM((Z, X, here, qkv_cols), BF),
            pltpu.VMEM((X - 1, Z, here, qkv_cols), BF),
            pltpu.VMEM((Z - 1, here, qkv_cols), BF),
            pltpu.VMEM((K - 1, Y, R, D), BF),
            pltpu.VMEM((Y - 1, R, D), BF),
            pltpu.VMEM((T, HD), F32),
            pltpu.VMEM((T, HD), F32),
            pltpu.VMEM((SMALL_ROWS, D), F32),
            pltpu.VMEM((Z, X, SMALL_ROWS, here), F32),
            pltpu.VMEM((X - 1, Z, SMALL_ROWS, here), F32),
            pltpu.VMEM((Z - 1, SMALL_ROWS, here), F32),
            pltpu.VMEM((C, SMALL_ROWS, here), F32),
            pltpu.VMEM((1, X * part), F32),
            pltpu.VMEM((half, D), BF),
            pltpu.VMEM((half, D), BF),
            pltpu.VMEM((half, D), BF),
            pltpu.SemaphoreType.DMA((sem_count(sizes),)),
            pltpu.SemaphoreType.DMA((sem_count(sizes),)),
            pltpu.SemaphoreType.DMA((64,)),
        ],
        compiler_params=pltpu.CompilerParams(
            collective_id=2, has_side_effects=True, vmem_limit_bytes=62 * MIB
        ),
        name="layer_backward",
    )(lengths, rows, gmlp, mid, seq, normed, qkv, att, wqkv, wo, vec, gub, g2part, mlppart, gdown, gup)


def spread_kernel(src, dst):
    dst[...] = src[0].astype(F32)


def spread(blocks):
    count, height, width = blocks.shape
    return pl.pallas_call(
        spread_kernel,
        grid=(count,),
        in_specs=[pl.BlockSpec((1, height, width), lambda i: (i, 0, 0))],
        out_specs=pl.BlockSpec((height, width), lambda i: (0, i)),
        out_shape=jax.ShapeDtypeStruct((height, count * width), F32),
        name="spread",
    )(blocks)


def norm_parts(values):
    center = values - jnp.mean(values, -1, keepdims=True)
    rstd = lax.rsqrt(jnp.mean(center * center, -1, keepdims=True) + EPSILON)
    return center * rstd, rstd


def norm_back(grad, gain, xhat, rstd):
    scaled = grad * gain
    return rstd * (
        scaled
        - jnp.mean(scaled, -1, keepdims=True)
        - xhat * jnp.mean(scaled * xhat, -1, keepdims=True)
    )


def body(
    sizes,
    inputs,
    lengths,
    norm1_gain,
    norm1_bias,
    query_weight,
    query_bias,
    keyval_weight,
    value_bias,
    output_weight,
    output_bias,
    norm2_gain,
    norm2_bias,
    up_weight,
    up_bias,
    down_weight,
    down_bias,
    cotangent,
):
    Y, K, Z, X = sizes
    C, S = Y * K, Z * X
    y, k, z, x = (lax.axis_index(name) for name in ("y", "k", "z", "x"))
    c = y * K + k
    R, D = inputs.shape[1:]
    rows_here = query_weight.shape[0]
    ff_here = down_weight.shape[0]
    ff_part = ff_here // K
    FF = ff_here * S
    T = C * R
    cols = D // C
    heads = H // C
    qkv_cols = cols + 2 * HD
    small_len = 7 * rows_here + ff_here + HD // S
    small_rows = -(-small_len // qkv_cols)
    small_rows = -(-small_rows // 16) * 16
    packed_rows = rows_here + small_rows

    pieces = [norm1_gain, norm1_bias, query_bias, output_bias, norm2_gain, norm2_bias, down_bias]
    shard = z * X + x
    lanes = jnp.arange(HD) // (HD // S) == shard
    value_row = jnp.where(lanes, jnp.tile(value_bias, S), 0).astype(BF)
    small = jnp.zeros((SMALL_ROWS, rows_here), BF)
    for row, piece in enumerate(pieces):
        small = small + jnp.pad(piece[None, :], ((row, SMALL_ROWS - 1 - row), (0, 0)))
    small = small + jnp.pad(up_bias.reshape(-1, rows_here), ((8, 4), (0, 0)))
    small = small + jnp.pad(value_row[None, :], ((12, 3), (0, rows_here - HD)))

    length = lengths[0]
    positions = c * R + jnp.arange(R, dtype=jnp.int32)
    live_rows = (positions < length).astype(F32)[:, None]
    grad_out = live_rows * cotangent[0].astype(F32)
    grad_mlp = grad_out.astype(BF)
    rows_low = inputs[0]
    (
        seq_low,
        wqkv,
        wo,
        wup,
        wdown,
        grad_mlp_all,
        normed_two_all,
        normed,
        qkv,
        attended_all,
        middle,
        tops,
        vectors,
    ) = forward_call(
        sizes,
        lengths,
        rows_low,
        grad_mlp,
        query_weight,
        keyval_weight,
        small,
        output_weight,
        up_weight,
        down_weight,
    )
    wup = wup.reshape(D, X * ff_part)
    wdown = wdown.reshape(X * ff_part, D)
    grad_mlp_all = grad_mlp_all.reshape(Z * K * R, D)
    normed_two_all = normed_two_all.reshape(Z * K * R, D)
    top_logit = tops[:, :heads, 0].reshape(H)
    u_bias = vectors[8:12].reshape(K, 4 // K, Z, X, rows_here)
    u_bias_own = pick(pick(u_bias, k, 0), z, 1)
    u_bias_own = jnp.moveaxis(u_bias_own, 0, 1).reshape(-1).astype(F32)

    pre_act = mm(normed_two_all, wup) + u_bias_own
    tanh = jnp.tanh(GELU_C * (pre_act + GELU_A * pre_act * pre_act * pre_act))
    act = (0.5 * pre_act * (1.0 + tanh)).astype(BF)
    slope = 0.5 * (1.0 + tanh) + 0.5 * pre_act * (1.0 - tanh * tanh) * GELU_C * (
        1.0 + 3.0 * GELU_A * pre_act * pre_act
    )
    grad_act = mm_nt(grad_mlp_all, wdown)
    grad_pre_wide = grad_act * slope
    grad_pre = grad_pre_wide.astype(BF)
    grad_two_part = mm_nt(grad_pre, wup).astype(BF).reshape(Z, K, R, D)
    mlp_part = mm(act, wdown).astype(BF).reshape(Z, K, R, D)
    grad_up_bias = jnp.sum(grad_pre.astype(F32), 0)[None, :]
    gdown = mm_tn(act, grad_mlp_all).astype(BF).reshape(X, ff_part, D)
    gup = mm_tn(normed_two_all, grad_pre).astype(BF).reshape(Z, X, rows_here, X * ff_part)
    backs = backward_call(
        sizes,
        lengths,
        rows_low,
        grad_mlp,
        middle,
        seq_low,
        normed,
        qkv,
        attended_all,
        wqkv,
        wo,
        vectors,
        grad_up_bias,
        grad_two_part,
        mlp_part,
        gdown,
        gup,
    )
    result, input_grad, gdown, gup, gwo, gwq, gkv, small_sums = backs[:8]
    grad_down_weight = gdown.reshape(ff_here, D).astype(F32)
    grad_up_weight = spread(gup.reshape(S * K, rows_here, ff_part))
    grad_output_weight = gwo.astype(F32)
    grad_query_weight = gwq.astype(F32)
    grad_keyval_weight = jnp.sum(gkv.astype(F32), 0)
    grad_value_bias = lax.dynamic_slice_in_dim(small_sums[12], shard * (HD // S), HD // S, 0)

    factors = CLIP_LIMIT / jnp.maximum(top_logit, CLIP_LIMIT)
    column_scale = jnp.repeat(jnp.sqrt(factors), HD)
    clipped_query_weight = (query_weight.astype(F32) * column_scale[None, :]).astype(BF)
    bias_scale = lax.dynamic_slice_in_dim(column_scale, shard * rows_here, rows_here, 0)
    clipped_query_bias = (query_bias.astype(F32) * bias_scale).astype(BF)
    key_scale = jnp.sqrt(jnp.min(factors))
    keyval_scale = jnp.concatenate([jnp.ones((HD,), F32) * key_scale, jnp.ones((HD,), F32)])
    clipped_keyval_weight = (keyval_weight.astype(F32) * keyval_scale[None, :]).astype(BF)

    return (
        result[None],
        input_grad[None],
        small_sums[0],
        small_sums[1],
        grad_query_weight,
        small_sums[2],
        grad_keyval_weight,
        grad_value_bias,
        grad_output_weight,
        small_sums[3],
        small_sums[4],
        small_sums[5],
        grad_up_weight,
        small_sums[8:12].reshape(-1),
        grad_down_weight,
        small_sums[6],
        clipped_query_weight,
        clipped_query_bias,
        clipped_keyval_weight,
    )


def solution(mesh):
    ctx, fsdp = mesh.shape["ctx"], mesh.shape["fsdp"]
    sizes = (ctx // 2, 2, 4, fsdp // 4)
    fine = Mesh(mesh.devices.reshape(sizes), ("y", "k", "z", "x"))
    tokens = P(("z", "x"), ("y", "k"), None)
    vector = P(("z", "x"))
    matrix = P(("z", "x"), None)
    return jax.shard_map(
        functools.partial(body, sizes),
        mesh=fine,
        in_specs=(
            tokens, vector, vector, vector, matrix, vector, matrix, vector, matrix, vector,
            vector, vector, matrix, vector, matrix, vector, tokens,
        ),
        out_specs=(
            tokens, tokens, vector, vector, matrix, vector, matrix, vector, matrix, vector,
            vector, vector, matrix, vector, matrix, vector, matrix, vector, matrix,
        ),
        check_vma=False,
    )
```

```python
import functools
import math

import jax
import jax.numpy as jnp
from jax import lax
from jax.experimental import pallas as pl
from jax.experimental.pallas import tpu as pltpu
from jax.sharding import Mesh, PartitionSpec as P

H = 16
HD = 128
EPSILON = 1e-05
CLIP_LIMIT = 10.0
NEGATIVE = -1e30
BF = jnp.bfloat16
F32 = jnp.float32
GELU_A = 0.044715
GELU_C = math.sqrt(2.0 / math.pi)
SCALE = HD ** (-0.5)
MIB = 1 << 20
VMEM_LIMIT = 63 * MIB


def mm(left, right):
    return jnp.dot(left, right, preferred_element_type=F32)


def mm_tn(left, right):
    return lax.dot_general(left, right, (((0,), (0,)), ((), ())), preferred_element_type=F32)


def mm_nt(left, right):
    return lax.dot_general(left, right, (((1,), (1,)), ((), ())), preferred_element_type=F32)


def shift(value, axis, count, step):
    return lax.ppermute(value, axis, [(i, (i + step) % count) for i in range(count)])


def pick(value, index, dim):
    return lax.dynamic_index_in_dim(value, index, dim, keepdims=False)


def in_order(parts, here, count, dim):
    if count == 1:
        return jnp.expand_dims(parts[0], dim)
    if count == 2:
        first = here == 0
        return jnp.stack(
            [jnp.where(first, parts[0], parts[1]), jnp.where(first, parts[1], parts[0])], dim
        )
    shape = list(parts[0].shape)
    shape.insert(dim, count)
    whole = jnp.zeros(shape, parts[0].dtype)
    for j, part in enumerate(parts):
        whole = lax.dynamic_update_index_in_dim(whole, part, lax.rem(here - j + count, count), dim)
    return whole


def gather(value, axis, count, dim):
    parts = [value] + [shift(value, axis, count, j) for j in range(1, count)]
    return in_order(parts, lax.axis_index(axis), count, dim)


def swap_blocks(value, axis, count, dim):
    here = lax.axis_index(axis)
    parts = [pick(value, here, dim)]
    for j in range(1, count):
        parts.append(shift(pick(value, lax.rem(here + j, count), dim), axis, count, j))
    return in_order(parts, here, count, dim)


def sum_blocks(value, axis, count, dim):
    here = lax.axis_index(axis)
    total = pick(value, here, dim).astype(F32)
    for j in range(1, count):
        block = pick(value, lax.rem(here + j, count), dim).astype(BF)
        total = total + shift(block, axis, count, j).astype(F32)
    return total


def sum_copies(value, axis, count):
    low = value.astype(BF)
    total = low.astype(F32)
    for j in range(1, count):
        total = total + shift(low, axis, count, j).astype(F32)
    return total


def attention_masks(rows, length):
    row = lax.broadcasted_iota(jnp.int32, (rows, rows), 0)
    col = lax.broadcasted_iota(jnp.int32, (rows, rows), 1)
    return (col <= row) & (col < length)


MESH = pl.DeviceIdType.MESH
SMALL_ROWS = 16


def sem_count(sizes):
    return 208 if sizes[0] * sizes[3] <= 4 else 448


class Move:
    def __init__(self, copy, send_if, recv_if):
        self.copy, self.send_if, self.recv_if = copy, send_if, recv_if

    def start(self):
        guarded(self.send_if, self.copy.start)

    def wait_send(self):
        guarded(self.send_if, self.copy.wait_send)

    def wait_recv(self):
        guarded(self.recv_if, self.copy.wait_recv)


def guarded(condition, action):
    if condition is None:
        action()
    else:

        @pl.when(condition)
        def _():
            action()


class Links:
    def __init__(self, sends, recvs, locals_):
        self.sends, self.recvs, self.locals_ = sends, recvs, locals_
        self.used, self.used_local = 0, 0
        self.open = []

    def plan(self, src, dst, where, send_if=None, recv_if=None, land=None):
        index = self.used
        self.used += 1
        assert self.used <= self.sends.shape[0]
        copy = pltpu.make_async_remote_copy(
            src_ref=src,
            dst_ref=dst,
            send_sem=self.sends.at[index],
            recv_sem=self.recvs.at[index if land is None else land],
            device_id=where,
            device_id_type=MESH,
        )
        move = Move(copy, send_if, recv_if)
        self.open.append(move)
        return move

    def push(self, src, dst, axis, target=None, when=None):
        where = axis if isinstance(axis, dict) else {axis: target}
        move = self.plan(src, dst, where, when, when)
        move.start()
        return move

    def sent(self, moves):
        for move in moves:
            move.wait_send()
            self.open = [other for other in self.open if other is not move]

    def local(self, src, dst):
        index = self.used_local
        self.used_local += 1
        assert self.used_local < self.locals_.shape[0]
        copy = pltpu.make_async_copy(src, dst, self.locals_.at[index])
        copy.start()
        return copy

    def drain(self):
        for move in self.open:
            move.wait_send()


class Line:
    def __init__(self, links, block, z, Z, source=None):
        self.z, self.Z = z, Z
        self.hops = []
        right, left = {"z": jnp.minimum(z + 1, Z - 1)}, {"z": jnp.maximum(z - 1, 0)}
        for h in range(1, Z):
            low, high = jnp.maximum(z - h + 1, 0), jnp.minimum(z + h - 1, Z - 1)
            ahead, back = block(low), block(high)
            own = source is not None and h == 1
            self.hops.append(
                [
                    links.plan(
                        source if own else ahead,
                        ahead,
                        right,
                        (z >= h - 1) & (z < Z - 1),
                        z >= h,
                    ),
                    links.plan(
                        source if own else back,
                        back,
                        left,
                        (z <= Z - h) & (z > 0),
                        z < Z - h,
                    ),
                ]
            )
        for move in self.hops[0]:
            move.start()

    def hop(self, h):
        for move in self.hops[h - 1]:
            move.wait_recv()
        if h < self.Z - 1:
            for move in self.hops[h]:
                move.start()
        z, Z = self.z, self.Z
        return [
            (jnp.maximum(z - h, 0), z >= h),
            (jnp.minimum(z + h, Z - 1), z < Z - h),
        ]


def wait_all(copies):
    for copy in copies:
        copy.wait()


def wait_recvs(copies):
    for copy in copies:
        copy.wait_recv()


def around(axis, here, count):
    return [(axis, lax.rem(here + j, count)) for j in range(1, count)]


def greet(groups, corners):
    barrier = pltpu.get_barrier_semaphore()
    count = 0
    for where in [{axis: target} for group in groups for axis, target in group] + corners:
        pl.semaphore_signal(barrier, inc=1, device_id=where, device_id_type=MESH)
        count += 1
    pl.semaphore_wait(barrier, count)


class Gather:
    def __init__(self, links, buf, place):
        self.links, self.buf, (self.z, self.Z, self.x, self.X) = links, buf, place
        self.line = Line(links, lambda at: buf.at[at * self.X + self.x], self.z, self.Z)
        self.from_x = []
        self.spread(self.z, None)

    def spread(self, at, when):
        block = self.buf.at[at * self.X + self.x]
        self.from_x += [
            self.links.push(block, block, *to, when=when) for to in around("x", self.x, self.X)
        ]

    def hop(self, h):
        for at, when in self.line.hop(h):
            self.spread(at, when)

    def finish(self):
        wait_recvs(self.from_x)

    def moves(self):
        return self.from_x + [move for hop in self.line.hops for move in hop]


def rows_loop(total, step, work):
    @pl.loop(0, total // step)
    def _(i):
        work(pl.ds(pl.multiple_of(i * step, step), step))


def layer_kernel(sizes, *refs):
    (
        length_ref, rows, cot, wq, wkv, small, wo, up, down,
        result_o, igrad_o, gdown_o, gup_o, gwo_o, gwq_o, gkv_o, small_o, top_o,
        h_seq, h_ux, h_uy, h_dx, h_dy,
        v_big, v_norm, v_w, v_wo, v_qkv, v_rows, v_mid, v_hat, v_mean, v_rstd, v_rs2,
        v_small, v_vec, v_ub, v_gub,
        v_wup, v_wdown, v_nt, v_gm, v_ap, v_g2, v_kin, m_kin, v_zin, m_zin,
        v_br, v_brall, v_gbr, v_gbc, v_gatt, v_gqkv, v_gk, v_gv,
        v_dwox, v_dwoz, v_dwqx, v_dwqz, v_a, v_b,
        v_sg, v_sgb, v_sgx, v_sgz, v_sga, v_top, v_topz, v_topx, v_tall,
        sends, recvs, locals_, ready,
    ) = refs
    Y, K, Z, X = sizes
    C, S = Y * K, Z * X
    y, k, z, x = (lax.axis_index(name) for name in ("y", "k", "z", "x"))
    c = y * K + k
    me = z * X + x
    R, D = rows.shape
    T = C * R
    cols = D // C
    here = wq.shape[0]
    part = v_wdown.shape[1]
    XP = X * part
    heads = cols // HD
    units = part // here
    length = length_ref[0]
    step = 64
    links = Links(sends, recvs, locals_)
    place = (z, Z, x, X)
    to_z, to_x = around("z", z, Z), around("x", x, X)
    to_y, to_k = around("y", y, Y), around("k", k, K)
    zs = [lax.rem(z - j + Z, Z) for j in range(Z)]
    xs = [lax.rem(x - j + X, X) for j in range(X)]
    ys = [lax.rem(y - j + Y, Y) for j in range(Y)]
    others = [
        (lax.rem(y + jy, Y), lax.rem(k + jk, K))
        for jy in range(Y)
        for jk in range(K)
        if jy or jk
    ]
    corners = [
        {"y": lax.rem(y + jy, Y), "k": lax.rem(k + jk, K)}
        for jy in range(1, Y)
        for jk in range(1, K)
    ]

    def at(index, size):
        return pl.ds(pl.multiple_of(index * size, size), size)

    greet([to_z, to_x, to_y, to_k], corners)

    first = [
        links.local(wq.at[:, at(c, cols)], v_w.at[me, :, pl.ds(0, cols)]),
        links.local(wkv, v_w.at[me, :, pl.ds(cols, 2 * HD)]),
        links.local(small, v_small.at[me]),
        links.local(rows, v_big.at[at(c, R)]),
    ]
    own_wo = links.local(wo.at[:, at(c, cols)], v_wo.at[me])
    own_rows = links.local(rows, v_rows)
    own_gm = links.local(cot, v_gm.at[z, k])
    wait_all(first)
    qkv_gather = Gather(links, v_w, place)
    small_gather = Gather(links, v_small, place)
    mine = v_big.at[at(c, R)]
    seq_y = [links.push(mine, mine, *to) for to in to_y]
    seq_k = [links.push(mine, mine, *to) for to in to_k]
    own_gm.wait()

    def mask_rows(span):
        row = lax.broadcasted_iota(jnp.int32, (step, 1), 0) + span.start + c * R
        v_gm[z, k, span, :] = jnp.where(row < length, v_gm[z, k, span, :].astype(F32), 0.0).astype(BF)

    rows_loop(R, step, mask_rows)
    for j in range(1, Y):
        seq_y[j - 1].wait_recv()
        block = v_big.at[at(ys[j] * K + k, R)]
        seq_k += [links.push(block, block, *to) for to in to_k]
    qkv_gather.hop(1)
    small_gather.hop(1)

    slab, piece = here // Y, part // Y
    slab_y, piece_y = at(y, slab), at(y, piece)
    own_up, up_z, up_x, up_y = [], [], [], []
    for j in range(Z):
        target = lax.rem(z + j, Z)
        for i in range(X):
            unit = at((target * X + i) * K + k, part)
            side = pl.ds(i * part, part)
            if j == 0:
                own_up.append(links.local(up.at[:, unit], v_wup.at[me, :, side]))
            else:
                up_z.append(
                    links.push(up.at[slab_y, unit], v_wup.at[me, slab_y, side], "z", target)
                )

    def up_on(index, to):
        block = v_wup.at[index, slab_y]
        return links.push(block, block, *to)

    wait_recvs(seq_k)
    save_seq = links.local(v_big, h_seq)

    def seq_stats(span):
        values = v_big[span, :].astype(F32)
        mean = jnp.mean(values, 1, keepdims=True)
        center = values - mean
        rstd = lax.rsqrt(jnp.mean(center * center, 1, keepdims=True) + EPSILON)
        v_mean[span, :] = jnp.broadcast_to(mean, (step, HD))
        v_rstd[span, :] = jnp.broadcast_to(rstd, (step, HD))

    rows_loop(T, step, seq_stats)
    v_sg[...] = jnp.zeros_like(v_sg)
    v_gub[...] = jnp.zeros_like(v_gub)
    v_gk[...] = jnp.zeros_like(v_gk)
    v_gv[...] = jnp.zeros_like(v_gv)
    qkv_gather.hop(2)
    small_gather.hop(2)
    own_wo.wait()
    wo_gather = Gather(links, v_wo, place)
    qkv_gather.hop(3)
    small_gather.hop(3)
    gm_line = Line(links, lambda to: v_gm.at[to, k], z, Z)
    gm_k = [links.push(v_gm.at[z, k], v_gm.at[z, k], *to) for to in to_k]

    def gm_hop(h):
        for source, when in gm_line.hop(h):
            block = v_gm.at[source, k]
            gm_k.extend(links.push(block, block, *to, when=when) for to in to_k)

    qkv_gather.finish()
    small_gather.finish()
    own_down = links.local(down.at[at(k, part)], v_wdown.at[x])
    down_src = down.at[at(k * Y + y, piece)]
    down_x = [links.push(down_src, v_wdown.at[x, piece_y], *to) for to in to_x]

    for s in range(S):
        v_vec[:, pl.ds(s * here, here)] = v_small[s]
    gain_one = v_vec[0:1, :].astype(F32)
    bias_one = v_vec[1:2, :].astype(F32)

    def first_norm(span):
        hat = (v_big[span, :].astype(F32) - v_mean[span, 0:1]) * v_rstd[span, 0:1]
        v_norm[span, :] = (hat * gain_one + bias_one).astype(BF)

    rows_loop(T, step, first_norm)
    save_seq.wait()
    links.sent(seq_y + seq_k)
    for axis, target in to_y + to_k:
        pl.semaphore_signal(ready, inc=1, device_id={axis: target}, device_id_type=MESH)

    q_bias = v_vec[2:3, at(c, cols)].astype(F32)
    v_bias = jnp.zeros((1, HD), F32)
    for s in range(S):
        v_bias = v_bias + v_small[s, 12:13, 0:HD].astype(F32)
    wide = min(cols, 256)
    for n in range(cols // wide):
        span = slice(n * wide, (n + 1) * wide)
        weights = v_w[:, :, span].reshape(D, wide)
        v_qkv[:, span] = (mm(v_norm[...], weights) + q_bias[:, span]).astype(BF)
    weights = v_w[:, :, cols:].reshape(D, 2 * HD)
    kv_bias = jnp.concatenate([jnp.zeros((1, HD), F32), v_bias], 1)
    v_qkv[:, cols:] = (mm(v_norm[...], weights) + kv_bias).astype(BF)
    wo_gather.hop(1)
    wait_all(own_up)
    up_x += [up_on(me, to) for to in to_x]
    for j in (1, Z - 1, 2):
        wait_recvs(up_z[(j - 1) * X : j * X])
        up_x += [up_on(zs[j] * X + x, to) for to in to_x]

    pl.semaphore_wait(ready, len(to_y) + len(to_k))
    tall = min(T, 256)

    def scores_of(n, r):
        end = (r + 1) * tall
        span = at(n, HD)
        queries = v_qkv[r * tall : end, span]
        keys = v_qkv[0:end, cols : cols + HD]
        row = lax.broadcasted_iota(jnp.int32, (tall, end), 0) + r * tall
        col = lax.broadcasted_iota(jnp.int32, (tall, end), 1)
        allowed = (col <= row) & (col < length)
        masked = jnp.where(allowed, mm_nt(queries, keys) * SCALE, NEGATIVE)
        top = jnp.max(masked, 1, keepdims=True)
        weights = jnp.exp(masked - top)
        return queries, keys, top, weights / jnp.sum(weights, 1, keepdims=True)

    @pl.loop(0, heads)
    def _(n):
        best = jnp.full((1, 1), NEGATIVE, F32)
        for r in range(T // tall):
            end = (r + 1) * tall
            queries, keys, top, weights = scores_of(n, r)
            out = mm(weights.astype(BF), v_qkv[0:end, cols + HD :])
            v_big[r * tall : end, at(c * heads + n, HD)] = out.astype(BF)
            live = lax.broadcasted_iota(jnp.int32, (tall, 1), 0) + r * tall < length
            best = jnp.maximum(best, jnp.max(jnp.where(live, top, NEGATIVE), 0, keepdims=True))
        v_top[pl.ds(n, 1), :] = jnp.broadcast_to(best, (1, HD))

    def att_block(source):
        return v_big.at[:, at(source, cols)]

    att_y = [links.push(att_block(c), att_block(c), *to) for to in to_y]
    att_k = [links.push(att_block(c), att_block(c), *to) for to in to_k]
    top_z = [links.push(v_top, v_topz.at[j], *to) for j, to in enumerate(to_z)]
    wo_gather.hop(2)
    for j in range(1, Y):
        att_y[j - 1].wait_recv()
        block = att_block(ys[j] * K + k)
        att_k += [links.push(block, block, *to) for to in to_k]
    gm_hop(1)
    wo_gather.hop(3)
    for j in (1, Z - 1, 2):
        up_y += [up_on(zs[j] * X + x, to) for to in to_y]
    down_y = []
    for j, move in enumerate(down_x):
        move.wait_recv()
        block = v_wdown.at[xs[j + 1], piece_y]
        down_y += [links.push(block, block, *to) for to in to_y]
    wait_recvs(att_k)
    wo_gather.finish()

    narrow = min(cols, 256)
    for n in range(cols // narrow):
        span = slice(n * narrow, (n + 1) * narrow)
        weights = v_wo[:, :, span].reshape(D, narrow)
        v_br[:, :, span] = mm(v_big[...], weights).astype(BF).reshape(C, R, narrow)
    br_in = [
        links.push(v_br.at[ty * K + tk], v_brall.at[c], {"y": ty, "k": tk}) for ty, tk in others
    ]
    v_brall[c] = v_br[c]
    gm_hop(2)
    own_rows.wait()
    wait_recvs(br_in)

    gain_two = v_vec[4:5, :].astype(F32)
    bias_two = v_vec[5:6, :].astype(F32)
    o_bias = v_vec[3:4, :].astype(F32)

    def second_norm(span):
        branch = jnp.concatenate([v_brall[q, span, :] for q in range(C)], 1)
        middle = v_rows[span, :].astype(F32) + branch.astype(F32) + o_bias
        v_mid[span, :] = middle
        center = middle - jnp.mean(middle, 1, keepdims=True)
        rstd = lax.rsqrt(jnp.mean(center * center, 1, keepdims=True) + EPSILON)
        hat = center * rstd
        v_hat[span, :] = hat
        v_rs2[span, :] = jnp.broadcast_to(rstd, (step, HD))
        v_nt[z, k, span, :] = (hat * gain_two + bias_two).astype(BF)

    rows_loop(R, step, second_norm)
    nt_line = Line(links, lambda to: v_nt.at[to, k], z, Z)
    nt_k = [links.push(v_nt.at[z, k], v_nt.at[z, k], *to) for to in to_k]

    def nt_hop(h):
        fresh = []
        for source, when in nt_line.hop(h):
            block = v_nt.at[source, k]
            fresh += [links.push(block, block, *to, when=when) for to in to_k]
        nt_k.extend(fresh)
        return fresh

    own_nt_k = list(nt_k)
    order = [0, 1, Z - 1, 2]
    for slot, j in enumerate(order):
        for i in range(1, X):
            up_x[slot * (X - 1) + i - 1].wait_recv()
            up_y += [up_on(zs[j] * X + xs[i], to) for to in to_y]
    gm_hop(3)
    for i in range(X):
        for r in range(units):
            to = at(z * X + i, here)
            value = jnp.zeros((1, here), F32)
            for kk in range(K):
                row = 8 + kk * units + r
                value = value + jnp.where(k == kk, v_vec[row : row + 1, to].astype(F32), 0.0)
            v_ub[0:1, i * part + r * here : i * part + (r + 1) * here] = value
    own_down.wait()
    wait_recvs(up_y + down_y + gm_k)

    tokens = K * R
    tile = 256

    def mlp_block(b):
        normed_two = v_nt[b].reshape(tokens, D)
        grads = v_gm[b].reshape(tokens, D)
        own = at(b, tokens)
        for n in range(XP // tile):
            span = slice(n * tile, (n + 1) * tile)
            inner = slice(n * tile % part, n * tile % part + tile)
            weights = v_wup[:, :, span].reshape(D, tile)
            pre = mm(normed_two, weights) + v_ub[0:1, span]
            cube = pre * pre
            tanh = jnp.tanh(GELU_C * pre * (1.0 + GELU_A * cube))
            half = 0.5 + 0.5 * tanh
            v_ap[0, own, span] = (pre * half).astype(BF)
            slope = half + 0.5 * pre * (1.0 - tanh * tanh) * GELU_C * (
                1.0 + 3.0 * GELU_A * cube
            )
            grad = mm_nt(grads, v_wdown[n * tile // part, inner, :])
            grad = (grad * slope).astype(BF)
            v_ap[1, own, span] = grad
            v_gub[0:1, span] += jnp.sum(grad.astype(F32), 0, keepdims=True)
        grad_pre = v_ap[1, own, :]
        for s in range(S):
            out = mm_nt(grad_pre, v_wup[s]).astype(BF)
            v_g2[b, :, :, s * here : (s + 1) * here] = out.reshape(K, R, here)

    far = jnp.where(z < 2, 3, 0)
    turn = [
        z,
        jnp.where(z == 0, 1, jnp.where(z == 1, 2, jnp.where(z == 2, 1, 2))),
        jnp.where(z == 0, 2, jnp.where(z == 1, 0, jnp.where(z == 2, 3, 1))),
        far,
    ]
    g2_k, g2_z = [], []
    z_base = links.used
    links.used += Z - 1

    def g2_out(i):
        b = turn[i]
        g2_k.append(
            [links.push(v_g2.at[b, t], v_kin.at[j, b], a, t) for j, (a, t) in enumerate(to_k)]
        )

    def g2_sum(i):
        b = turn[i]
        wait_recvs(g2_k[i])

        def work(span):
            total = v_g2[b, k, span, :].astype(F32)
            for j in range(K - 1):
                total = total + v_kin[j, b, span, :].astype(F32)
            v_g2[b, k, span, :] = total.astype(BF)

        rows_loop(R, step, work)
        if i:
            away = lax.rem(b - z + Z, Z)
            move = links.plan(
                v_g2.at[b, k], v_zin.at[away - 1], {"z": b}, land=z_base + away - 1
            )
            move.start()
            g2_z.append(move)

    fresh = own_nt_k
    for i in range(Z):
        wait_recvs(fresh)
        mlp_block(turn[i])
        g2_out(i)
        if i:
            g2_sum(i - 1)
        if i + 1 < Z:
            fresh = nt_hop(i + 1)
    g2_sum(Z - 1)

    wait_recvs(top_z)
    best = v_top[...]
    for j in range(Z - 1):
        best = jnp.maximum(best, v_topz[j])
    v_topx[0] = best
    top_x = [links.push(v_topx.at[0], v_topx.at[j + 1], *to) for j, to in enumerate(to_x)]

    links.sent(up_x + up_y)
    acts = v_ap.at[0]
    grads_pre = v_ap.at[1]
    everyone = Z * tokens
    for s in range(S):
        flat = v_nt[:, :, :, s * here : (s + 1) * here].reshape(everyone, here)
        v_wup[s] = mm_tn(flat, grads_pre[...]).astype(BF)
    gu_x = [
        links.push(v_wup.at[q * X + t], h_ux.at[j, q], a, t)
        for j, (a, t) in enumerate(to_x)
        for q in range(Z)
    ]
    links.sent(nt_k)
    for moves in nt_line.hops:
        links.sent(moves)
    for n in range(D // tile):
        span = slice(n * tile, (n + 1) * tile)
        weights = v_wdown[:, :, span].reshape(XP, tile)
        out = mm(acts[...], weights).astype(BF)
        v_nt[:, :, :, span] = out.reshape(Z, K, R, tile)
    mlp_k = [links.push(v_nt.at[:, t], m_kin.at[j], a, t) for j, (a, t) in enumerate(to_k)]
    links.sent(down_y)
    for n in range(XP // tile):
        inner = slice(n * tile % part, n * tile % part + tile)
        left = acts[:, n * tile : (n + 1) * tile]
        v_wdown[n * tile // part, inner, :] = mm_tn(left, v_gm[...].reshape(everyone, D)).astype(BF)
    gd_y = [
        links.push(v_wdown.at[:, at(t, piece)], h_dy.at[j], a, t)
        for j, (a, t) in enumerate(to_y)
    ]
    links.sent(gm_k)
    for moves in gm_line.hops:
        links.sent(moves)

    g2_in = [
        pltpu.make_async_remote_copy(
            src_ref=v_g2.at[z, k],
            dst_ref=v_zin.at[j],
            send_sem=sends.at[z_base],
            recv_sem=recvs.at[z_base + j],
            device_id={"z": zs[1]},
            device_id_type=MESH,
        )
        for j in range(Z - 1)
    ]
    wait_recvs(g2_in)

    def second_back(span):
        grad = v_g2[z, k, span, :].astype(F32)
        for j in range(Z - 1):
            grad = grad + v_zin[j, span, :].astype(F32)
        hat = v_hat[span, :]
        v_sg[4:5, :] += jnp.sum(grad * hat, 0, keepdims=True)
        v_sg[5:6, :] += jnp.sum(grad, 0, keepdims=True)
        scaled = grad * gain_two
        back = v_rs2[span, 0:1] * (
            scaled
            - jnp.mean(scaled, 1, keepdims=True)
            - hat * jnp.mean(scaled * hat, 1, keepdims=True)
        )
        grad_out = v_gm[z, k, span, :].astype(F32)
        v_sg[6:7, :] += jnp.sum(grad_out, 0, keepdims=True)
        grad_middle = grad_out + back
        v_hat[span, :] = grad_middle
        low = grad_middle.astype(BF)
        v_sg[3:4, :] += jnp.sum(low.astype(F32), 0, keepdims=True)
        for q in range(C):
            v_gbr[q, span, :] = low[:, q * cols : (q + 1) * cols]

    rows_loop(R, step, second_back)
    wait_recvs(top_x)
    best = v_topx[0]
    for j in range(1, X):
        best = jnp.maximum(best, v_topx[j])
    v_tall[c] = best
    top_y = [links.push(v_tall.at[c], v_tall.at[c], *to) for to in to_y]
    top_k = [links.push(v_tall.at[c], v_tall.at[c], *to) for to in to_k]
    wait_recvs(mlp_k)
    for q in range(Z):

        def mlp_sum(span, q=q):
            total = v_nt[q, k, span, :].astype(F32)
            for j in range(K - 1):
                total = total + m_kin[j, q, span, :].astype(F32)
            v_nt[q, k, span, :] = total.astype(BF)

        rows_loop(R, step, mlp_sum)
    gb = [
        links.push(v_gbr.at[ty * K + tk], v_gbc.at[c], {"y": ty, "k": tk}) for ty, tk in others
    ]
    v_gbc[c] = v_gbr[c]
    mlp_z = [links.push(v_nt.at[t, k], m_zin.at[j], a, t) for j, (a, t) in enumerate(to_z)]
    for moves in g2_k:
        links.sent(moves)
    links.sent(g2_z)
    wait_recvs(gb)

    for s in range(S):
        out = mm_nt(v_gbc[...].reshape(T, cols), v_wo[s]).astype(BF)
        v_g2[0:Y, :, :, s * here : (s + 1) * here] = out.reshape(Y, K, R, here)
    chunks = pl.ds(0, Y)
    ga_k = [
        links.push(
            v_g2.at[chunks, :, :, at(q * K + t, cols)],
            v_gm.at[chunks, :, :, pl.ds((j * Y + q) * cols, cols)],
            a,
            t,
        )
        for j, (a, t) in enumerate(to_k)
        for q in range(Y)
    ]
    links.sent(wo_gather.moves())
    for s in range(S):
        left = v_big[:, s * here : (s + 1) * here]
        v_wo[s] = mm_tn(left, v_gbc[...].reshape(T, cols)).astype(BF)
    do_x = [
        links.push(v_wo.at[q * X + t], v_dwox.at[j, q], a, t)
        for j, (a, t) in enumerate(to_x)
        for q in range(Z)
    ]
    links.sent(att_y + att_k)
    load_seq = links.local(h_seq, v_big)
    wait_recvs(ga_k)
    base = (K - 1) * Y
    for q in range(Y):
        for i in range(Y):
            for kk in range(K):

                def ga_sum(span, q=q, i=i, kk=kk):
                    total = v_g2[i, kk, span, at(q * K + k, cols)].astype(F32)
                    for j in range(K - 1):
                        side = slice((j * Y + q) * cols, (j * Y + q + 1) * cols)
                        total = total + v_gm[i, kk, span, side].astype(F32)
                    v_gm[i, kk, span, q * cols : (q + 1) * cols] = total.astype(BF)

                rows_loop(R, step, ga_sum)
    ga_y = [
        links.push(
            v_gm.at[chunks, :, :, at(t, cols)],
            v_gm.at[chunks, :, :, pl.ds((base + j) * cols, cols)],
            a,
            t,
        )
        for j, (a, t) in enumerate(to_y)
    ]
    wait_recvs(ga_y)
    for i in range(Y):
        for kk in range(K):

            def ga_last(span, i=i, kk=kk):
                total = v_gm[i, kk, span, at(y, cols)].astype(F32)
                for j in range(Y - 1):
                    side = slice((base + j) * cols, (base + j + 1) * cols)
                    total = total + v_gm[i, kk, span, side].astype(F32)
                to = pl.ds(pl.multiple_of((i * K + kk) * R + span.start, step), step)
                v_gatt[to, :] = total.astype(BF)

            rows_loop(R, step, ga_last)

    @pl.loop(0, heads)
    def _(n):
        span = at(n, HD)
        for r in range(T // tall):
            end = (r + 1) * tall
            own = slice(r * tall, end)
            queries, keys, top, weights = scores_of(n, r)
            grads = v_gatt[own, span]
            grad_weights = mm_nt(grads, v_qkv[0:end, cols + HD :])
            delta = jnp.sum(weights * grad_weights, 1, keepdims=True)
            grad_scores = (weights * (grad_weights - delta)).astype(BF)
            v_gqkv[own, span] = (mm(grad_scores, keys) * SCALE).astype(BF)
            v_gk[0:end, :] += mm_tn(grad_scores, queries) * SCALE
            v_gv[0:end, :] += mm_tn(weights.astype(BF), grads)

    v_gqkv[:, cols : cols + HD] = v_gk[...].astype(BF)
    v_gqkv[:, cols + HD :] = v_gv[...].astype(BF)
    wq_cols = cols + 2 * HD
    per = v_ap.shape[1] // here

    def dwq(index):
        return v_ap.at[index // per, at(lax.rem(index, per), here), pl.ds(0, wq_cols)]

    for s in range(S):
        left = v_norm[:, s * here : (s + 1) * here]
        rows_s = slice(s % per * here, (s % per + 1) * here)
        v_ap[s // per, rows_s, 0:wq_cols] = mm_tn(left, v_gqkv[...]).astype(BF)
    dq_x = [
        links.push(dwq(q * X + t), v_dwqx.at[j, q], a, t)
        for j, (a, t) in enumerate(to_x)
        for q in range(Z)
    ]
    load_seq.wait()

    for s in range(S):
        span = slice(s * here, (s + 1) * here)
        grad = mm_nt(v_gqkv[...], v_w[s])
        v_norm[:, span] = grad.astype(BF)
        hat = (v_big[:, span].astype(F32) - v_mean[:, 0:1]) * v_rstd[:, 0:1]
        v_sg[0:1, span] = jnp.sum(grad * hat, 0, keepdims=True)
        v_sg[1:2, span] = jnp.sum(grad, 0, keepdims=True)
    g1_k = [
        links.push(v_norm.at[at(q * K + t, R)], v_kin.at[j, q], a, t)
        for j, (a, t) in enumerate(to_k)
        for q in range(Y)
    ]

    for j in range(1, Y):
        top_y[j - 1].wait_recv()
        block = v_tall.at[ys[j] * K + k]
        top_k += [links.push(block, block, *to) for to in to_k]

    v_sg[2:3, at(c, cols)] = jnp.sum(v_gqkv[:, 0:cols].astype(F32), 0, keepdims=True)
    value_sum = jnp.sum(v_gqkv[:, cols + HD :].astype(F32), 0, keepdims=True)
    for s in range(S):
        v_sg[12:13, s * here : s * here + HD] = value_sum
    for i in range(X):
        to = at(z * X + i, here)
        for r in range(units):
            start = i * part + r * here
            bias_part = v_gub[0:1, start : start + here]
            for kk in range(K):
                row = 8 + kk * units + r
                v_sg[row : row + 1, to] = jnp.where(k == kk, bias_part, 0.0)
    for s in range(S):
        v_sgb[s // X, s % X] = v_sg[:, s * here : (s + 1) * here]
    sg_x = [links.push(v_sgb.at[:, t], v_sgx.at[j], a, t) for j, (a, t) in enumerate(to_x)]

    bufs = (v_a, v_b)
    spare = (locals_.at[locals_.shape[0] - 1], locals_.at[locals_.shape[0] - 2])

    def add_tiles(tiles):
        def fetch(i):
            source, height, width = tiles[i][:3]
            copy = pltpu.make_async_copy(
                source, bufs[i % 2].at[pl.ds(0, height), pl.ds(0, width)], spare[i % 2]
            )
            copy.start()
            return copy

        coming = fetch(0)
        for i, (source, height, width, load, store) in enumerate(tiles):
            now = coming
            if i + 1 < len(tiles):
                coming = fetch(i + 1)
            now.wait()
            small_step = min(step, height)

            def work(span, i=i, width=width, load=load, store=store):
                extra = bufs[i % 2][span, 0:width].astype(F32)
                store(span, (load(span).astype(F32) + extra).astype(BF))

            rows_loop(height, small_step, work)

    def shifted(start, span):
        return pl.ds(pl.multiple_of(start + span.start, span.size), span.size)

    def up_tile(source, q, start, height):
        def load(span):
            return v_wup[q * X + x, shifted(start, span), :]

        def store(span, value):
            v_wup[q * X + x, shifted(start, span), :] = value

        return source, height, XP, load, store

    wait_recvs(gu_x)
    add_tiles(
        [up_tile(h_ux.at[j, q], q, 0, here) for q in range(Z) for j in range(X - 1)]
    )
    gu_y = [
        links.push(v_wup.at[q * X + x, at(t, slab)], h_uy.at[j, q], a, t)
        for j, (a, t) in enumerate(to_y)
        for q in range(Z)
    ]

    wait_recvs(g1_k)
    for q in range(Y):

        def g1_sum(span, q=q):
            total = v_norm[shifted((q * K + k) * R, span), :].astype(F32)
            for j in range(K - 1):
                total = total + v_kin[j, q, span, :].astype(F32)
            v_kin[0, q, span, :] = total.astype(BF)

        rows_loop(R, step, g1_sum)
    g1_y = [links.push(v_kin.at[0, t], m_kin.at[0, j], a, t) for j, (a, t) in enumerate(to_y)]

    def down_tile(source, index, start, height, side):
        def load(span):
            return v_wdown[index, shifted(start, span), side]

        def store(span, value):
            v_wdown[index, shifted(start, span), side] = value

        return source, height, XP, load, store

    halves = [slice(n * XP, (n + 1) * XP) for n in range(D // XP)]
    wait_recvs(gd_y)
    add_tiles(
        [
            down_tile(h_dy.at[j, i, :, pl.ds(side.start, XP)], i, y * piece, piece, side)
            for i in range(X)
            for side in halves
            for j in range(Y - 1)
        ]
    )
    gd_x = [links.push(v_wdown.at[t, piece_y], h_dx.at[j], a, t) for j, (a, t) in enumerate(to_x)]

    def sum_x(own, extra, copies):
        wait_recvs(copies)
        for q in range(Z):
            total = own(q)[...].astype(F32)
            for j in range(X - 1):
                total = total + extra[j, q].astype(F32)
            extra[0, q] = total.astype(extra.dtype)

    sum_x(lambda q: v_wo.at[q * X + x], v_dwox, do_x)
    do_z = [links.push(v_dwox.at[0, t], v_dwoz.at[j], a, t) for j, (a, t) in enumerate(to_z)]
    sum_x(lambda q: dwq(q * X + x), v_dwqx, dq_x)
    dq_z = [links.push(v_dwqx.at[0, t], v_dwqz.at[j], a, t) for j, (a, t) in enumerate(to_z)]
    sum_x(lambda q: v_sgb.at[q, x], v_sgx, sg_x)
    sg_z = [links.push(v_sgx.at[0, t], v_sgz.at[j], a, t) for j, (a, t) in enumerate(to_z)]

    wait_recvs(gu_y)
    add_tiles(
        [up_tile(h_uy.at[j, q], q, y * slab, slab) for q in range(Z) for j in range(Y - 1)]
    )
    gu_z, own_gu = [], []
    for i in range(X):
        side = pl.ds(i * part, part)
        to = gup_o.at[z * X + i, k, slab_y]
        own_gu.append(links.local(v_wup.at[me, slab_y, side], to))
        for a, t in to_z:
            gu_z.append(links.push(v_wup.at[t * X + x, slab_y, side], to, a, t))

    wait_recvs(top_k)
    save_top = links.local(v_tall, top_o)
    wait_recvs(g1_y)

    def finish_input(span):
        grad = v_kin[0, y, span, :].astype(F32)
        for j in range(Y - 1):
            grad = grad + m_kin[0, j, span, :].astype(F32)
        own = shifted(c * R, span)
        rstd = v_rstd[own, 0:1]
        hat = (v_rows[span, :].astype(F32) - v_mean[own, 0:1]) * rstd
        scaled = grad * gain_one
        back = rstd * (
            scaled
            - jnp.mean(scaled, 1, keepdims=True)
            - hat * jnp.mean(scaled * hat, 1, keepdims=True)
        )
        v_rows[span, :] = (v_hat[span, :] + back).astype(BF)

    rows_loop(R, step, finish_input)
    last = [links.local(v_rows, igrad_o)]

    d_bias = v_vec[6:7, :].astype(F32)
    wait_recvs(mlp_z)

    def finish_result(span):
        total = v_nt[z, k, span, :].astype(F32)
        for j in range(Z - 1):
            total = total + m_zin[j, span, :].astype(F32)
        row = lax.broadcasted_iota(jnp.int32, (step, 1), 0) + span.start + c * R
        value = v_mid[span, :] + total + d_bias
        v_zin[0, span, :] = jnp.where(row < length, value, 0.0).astype(BF)

    rows_loop(R, step, finish_result)
    last.append(links.local(v_zin.at[0], result_o))

    wait_recvs(gd_x)
    add_tiles(
        [
            down_tile(h_dx.at[j, :, pl.ds(side.start, XP)], x, y * piece, piece, side)
            for side in halves
            for j in range(X - 1)
        ]
    )
    gd_block = v_wdown.at[x, piece_y]
    last.append(links.local(gd_block, gdown_o.at[k, piece_y]))
    gd_y2 = [links.push(gd_block, gdown_o.at[k, piece_y], *to) for to in to_y]
    gd_k = [links.push(gd_block, gdown_o.at[k, piece_y], *to) for to in to_k]

    def sum_z(own, extra, copies):
        wait_recvs(copies)
        total = own[0, z].astype(F32)
        for j in range(Z - 1):
            total = total + extra[j].astype(F32)
        extra[0] = total.astype(extra.dtype)

    sum_z(v_dwox, v_dwoz, do_z)
    last.append(links.local(v_dwoz.at[0], gwo_o.at[:, at(c, cols)]))
    wo_y = [links.push(v_dwoz.at[0], gwo_o.at[:, at(c, cols)], *to) for to in to_y]
    wo_k = [links.push(v_dwoz.at[0], gwo_o.at[:, at(c, cols)], *to) for to in to_k]

    wait_all(own_gu)
    wait_recvs(gu_z)
    mine = gup_o.at[:, k, slab_y]
    gu_y2 = [links.push(mine, mine, *to) for to in to_y]
    gu_k = [links.push(mine, mine, *to) for to in to_k]

    sum_z(v_dwqx, v_dwqz, dq_z)
    left, tail = pl.ds(0, cols), pl.ds(cols, 2 * HD)
    last.append(links.local(v_dwqz.at[0, :, left], gwq_o.at[:, at(c, cols)]))
    last.append(links.local(v_dwqz.at[0, :, tail], gkv_o.at[c]))
    wq_y = [links.push(v_dwqz.at[0, :, left], gwq_o.at[:, at(c, cols)], *to) for to in to_y]
    wq_k = [links.push(v_dwqz.at[0, :, left], gwq_o.at[:, at(c, cols)], *to) for to in to_k]
    kv_y = [links.push(v_dwqz.at[0, :, tail], gkv_o.at[c], *to) for to in to_y]
    kv_k = [links.push(v_dwqz.at[0, :, tail], gkv_o.at[c], *to) for to in to_k]
    sum_z(v_sgx, v_sgz, sg_z)
    v_sga[c] = v_sgz[0]
    sg_y = [links.push(v_sga.at[c], v_sga.at[c], *to) for to in to_y]
    sg_k = [links.push(v_sga.at[c], v_sga.at[c], *to) for to in to_k]

    def on_to_core(ref):
        return [links.push(ref, ref, *to) for to in to_k]

    for j in range(1, Y):
        q = ys[j] * K + k
        wo_y[j - 1].wait_recv()
        wo_k += on_to_core(gwo_o.at[:, at(q, cols)])
        gd_y2[j - 1].wait_recv()
        gd_k += on_to_core(gdown_o.at[k, at(ys[j], piece)])
        wq_y[j - 1].wait_recv()
        wq_k += on_to_core(gwq_o.at[:, at(q, cols)])
        kv_y[j - 1].wait_recv()
        kv_k += on_to_core(gkv_o.at[q])
        sg_y[j - 1].wait_recv()
        sg_k += on_to_core(v_sga.at[q])
        gu_y2[j - 1].wait_recv()
        gu_k += on_to_core(gup_o.at[:, k, at(ys[j], slab)])
    wait_recvs(sg_k)
    total = v_sga[0]
    for q in range(1, C):
        total = total + v_sga[q]
    v_sgz[0] = total
    last.append(links.local(v_sgz.at[0], small_o))
    wait_recvs(gd_k + wo_k + wq_k + kv_k + gu_k)
    wait_all(last + [save_top])
    links.drain()


def layer_call(sizes, lengths, rows, cot, wq, wkv, small, wo, up, down):
    Y, K, Z, X = sizes
    C, S = Y * K, Z * X
    R, D = rows.shape
    T = C * R
    cols = D // C
    wq_cols = cols + 2 * HD
    here = wq.shape[0]
    part = down.shape[0] // K
    XP = X * part
    shape = jax.ShapeDtypeStruct
    anywhere = pl.BlockSpec(memory_space=pl.ANY)

    def low(*dims):
        return pltpu.VMEM(dims, BF)

    def wide(*dims):
        return pltpu.VMEM(dims, F32)

    outs = [
        shape((R, D), BF),
        shape((R, D), BF),
        shape((K, part, D), BF),
        shape((S, K, here, part), BF),
        shape((here, D), BF),
        shape((here, D), BF),
        shape((C, here, 2 * HD), BF),
        shape((SMALL_ROWS, here), F32),
        shape((C, 8, HD), F32),
        shape((T, D), BF),
        shape((X - 1, Z, here, XP), BF),
        shape((Y - 1, Z, here // Y, XP), BF),
        shape((X - 1, part // Y, D), BF),
        shape((Y - 1, X, part // Y, D), BF),
    ]
    scratch = [
        low(T, D), low(T, D), low(S, here, wq_cols), low(S, here, cols), low(T, wq_cols),
        low(R, D), wide(R, D), wide(R, D), wide(T, HD), wide(T, HD), wide(R, HD),
        low(S, SMALL_ROWS, here), low(SMALL_ROWS, D), wide(1, XP), wide(1, XP),
        low(S, here, XP), low(X, part, D), low(Z, K, R, D), low(Z, K, R, D),
        low(2, Z * K * R, XP), low(Z, K, R, D), low(K - 1, Z, R, D), low(K - 1, Z, R, D),
        low(Z - 1, R, D), low(Z - 1, R, D),
        low(C, R, cols), low(C, R, cols), low(C, R, cols), low(C, R, cols),
        low(T, cols), low(T, wq_cols), wide(T, HD), wide(T, HD),
        low(X - 1, Z, here, cols), low(Z - 1, here, cols),
        low(X - 1, Z, here, wq_cols), low(Z - 1, here, wq_cols),
        low(here, XP), low(here, XP),
        wide(SMALL_ROWS, D), wide(Z, X, SMALL_ROWS, here), wide(X - 1, Z, SMALL_ROWS, here),
        wide(Z - 1, SMALL_ROWS, here), wide(C, SMALL_ROWS, here),
        wide(8, HD), wide(Z - 1, 8, HD), wide(X, 8, HD), wide(C, 8, HD),
        pltpu.SemaphoreType.DMA((sem_count(sizes),)),
        pltpu.SemaphoreType.DMA((sem_count(sizes),)),
        pltpu.SemaphoreType.DMA((32,)),
        pltpu.SemaphoreType.REGULAR,
    ]
    return pl.pallas_call(
        functools.partial(layer_kernel, sizes),
        in_specs=[pl.BlockSpec(memory_space=pltpu.SMEM)] + [anywhere] * 8,
        out_specs=[anywhere] * len(outs),
        out_shape=outs,
        scratch_shapes=scratch,
        compiler_params=pltpu.CompilerParams(
            collective_id=1, has_side_effects=True, vmem_limit_bytes=VMEM_LIMIT
        ),
        name="layer",
    )(lengths, rows, cot, wq, wkv, small, wo, up, down)[:9]


STEPS = 8


def finish_kernel(
    shard_ref, tops, wq, wkv, q_bias, result, igrad, gup, gdown, gwo, gwq, gkv,
    result_o, igrad_o, gup_o, gdown_o, gwo_o, gwq_o, gkv_o, cq_o, ckv_o, cb_o, v_scale,
):
    groups, heads = tops.shape[0], v_scale.shape[1] // HD // tops.shape[0]
    least = jnp.ones((1, HD), F32)
    for g in range(groups):
        for n in range(heads):
            factor = CLIP_LIMIT / jnp.maximum(tops[g, n : n + 1, :], CLIP_LIMIT)
            least = jnp.minimum(least, factor)
            column = (g * heads + n) * HD
            v_scale[0:1, column : column + HD] = jnp.sqrt(factor)
    cq_o[...] = (wq[...].astype(F32) * v_scale[0:1, :]).astype(BF)
    ckv_o[:, 0:HD] = (wkv[:, 0:HD].astype(F32) * jnp.sqrt(least)).astype(BF)
    ckv_o[:, HD:] = wkv[:, HD:]
    here = q_bias.shape[1]
    own = pl.ds(pl.multiple_of(shard_ref[0] * here, here), here)
    cb_o[...] = (q_bias[...].astype(F32) * v_scale[0:1, own]).astype(BF)
    result_o[...] = result[...]
    igrad_o[...] = igrad[...]
    width = gup.shape[2]
    for n in range(gup.shape[0]):
        gup_o[:, n * width : (n + 1) * width] = gup[n].astype(F32)
    gdown_o[...] = gdown[...].astype(F32)
    gwo_o[...] = gwo[...].astype(F32)
    gwq_o[...] = gwq[...].astype(F32)
    total = gkv[0].astype(F32)
    for g in range(1, groups):
        total = total + gkv[g].astype(F32)
    gkv_o[...] = total


def finish(shard, tops, wq, wkv, q_bias, result, igrad, gup, gdown, gwo, gwq, gkv):
    here, D = wq.shape
    rows, units = result.shape[0], gup.shape[0]
    part = gup.shape[2]
    tall = gdown.shape[0]
    groups = tops.shape[0]

    def down_rows(height, width):
        return pl.BlockSpec((height // STEPS, width), lambda i, s: (i, 0))

    def whole(*dims):
        return pl.BlockSpec(dims, lambda i, s: (0,) * len(dims))

    tokens = down_rows(rows, D)
    square = down_rows(here, D)
    narrow = down_rows(here, 2 * HD)
    shape = jax.ShapeDtypeStruct
    return pl.pallas_call(
        finish_kernel,
        grid_spec=pltpu.PrefetchScalarGridSpec(
            num_scalar_prefetch=1,
            grid=(STEPS,),
            in_specs=[
                whole(*tops.shape), square, narrow, whole(1, here), tokens, tokens,
                pl.BlockSpec((units // STEPS, here, part), lambda i, s: (i, 0, 0)),
                down_rows(tall, D), square, square,
                pl.BlockSpec((groups, here // STEPS, 2 * HD), lambda i, s: (0, i, 0)),
            ],
            out_specs=[
                tokens, tokens,
                pl.BlockSpec((here, units // STEPS * part), lambda i, s: (0, i)),
                down_rows(tall, D), square, square, narrow, square, narrow, whole(1, here),
            ],
            scratch_shapes=[pltpu.VMEM((8, D), F32)],
        ),
        out_shape=[
            shape((rows, D), BF), shape((rows, D), BF), shape((here, units * part), F32),
            shape((tall, D), F32), shape((here, D), F32), shape((here, D), F32),
            shape((here, 2 * HD), F32), shape((here, D), BF), shape((here, 2 * HD), BF),
            shape((1, here), BF),
        ],
        compiler_params=pltpu.CompilerParams(vmem_limit_bytes=VMEM_LIMIT),
        name="finish",
    )(shard, tops, wq, wkv, q_bias, result, igrad, gup, gdown, gwo, gwq, gkv)


def body(
    sizes,
    inputs,
    lengths,
    norm1_gain,
    norm1_bias,
    query_weight,
    query_bias,
    keyval_weight,
    value_bias,
    output_weight,
    output_bias,
    norm2_gain,
    norm2_bias,
    up_weight,
    up_bias,
    down_weight,
    down_bias,
    cotangent,
):
    Y, K, Z, X = sizes
    C, S = Y * K, Z * X
    y, k, z, x = (lax.axis_index(name) for name in ("y", "k", "z", "x"))
    c = y * K + k
    R, D = inputs.shape[1:]
    rows_here = query_weight.shape[0]
    ff_here = down_weight.shape[0]
    ff_part = ff_here // K
    FF = ff_here * S
    T = C * R
    cols = D // C
    heads = H // C
    qkv_cols = cols + 2 * HD
    small_len = 7 * rows_here + ff_here + HD // S
    small_rows = -(-small_len // qkv_cols)
    small_rows = -(-small_rows // 16) * 16
    packed_rows = rows_here + small_rows

    pieces = [norm1_gain, norm1_bias, query_bias, output_bias, norm2_gain, norm2_bias, down_bias]
    shard = z * X + x
    value_row = lax.dynamic_update_slice_in_dim(
        jnp.zeros((rows_here,), BF), value_bias, shard * (HD // S), 0
    )
    row = lax.broadcasted_iota(jnp.int32, (SMALL_ROWS, rows_here), 0)
    spread_row = functools.partial(jnp.broadcast_to, shape=(SMALL_ROWS, rows_here))
    small = jnp.zeros((SMALL_ROWS, rows_here), BF)
    for index, piece in enumerate(pieces):
        small = jnp.where(row == index, spread_row(piece), small)
    for index in range(ff_here // rows_here):
        piece = up_bias[index * rows_here : (index + 1) * rows_here]
        small = jnp.where(row == 8 + index, spread_row(piece), small)
    small = jnp.where(row == 12, spread_row(value_row), small)

    rows_low = inputs[0]
    result, input_grad, gdown, gup, gwo, gwq, gkv, small_sums, tops = layer_call(
        sizes,
        lengths,
        rows_low,
        cotangent[0],
        query_weight,
        keyval_weight,
        small,
        output_weight,
        up_weight,
        down_weight,
    )
    (
        result,
        input_grad,
        grad_up_weight,
        grad_down_weight,
        grad_output_weight,
        grad_query_weight,
        grad_keyval_weight,
        clipped_query_weight,
        clipped_keyval_weight,
        clipped_query_bias,
    ) = finish(
        shard[None],
        tops,
        query_weight,
        keyval_weight,
        query_bias[None],
        result,
        input_grad,
        gup.reshape(S * K, rows_here, ff_part),
        gdown.reshape(ff_here, D),
        gwo,
        gwq,
        gkv,
    )
    grad_value_bias = lax.dynamic_slice_in_dim(small_sums[12], shard * (HD // S), HD // S, 0)

    return (
        result[None],
        input_grad[None],
        small_sums[0],
        small_sums[1],
        grad_query_weight,
        small_sums[2],
        grad_keyval_weight,
        grad_value_bias,
        grad_output_weight,
        small_sums[3],
        small_sums[4],
        small_sums[5],
        grad_up_weight,
        small_sums[8:12].reshape(-1),
        grad_down_weight,
        small_sums[6],
        clipped_query_weight,
        clipped_query_bias[0],
        clipped_keyval_weight,
    )


def solution(mesh):
    ctx, fsdp = mesh.shape["ctx"], mesh.shape["fsdp"]
    sizes = (ctx // 2, 2, 4, fsdp // 4)
    fine = Mesh(mesh.devices.reshape(sizes), ("y", "k", "z", "x"))
    tokens = P(("z", "x"), ("y", "k"), None)
    vector = P(("z", "x"))
    matrix = P(("z", "x"), None)
    return jax.shard_map(
        functools.partial(body, sizes),
        mesh=fine,
        in_specs=(
            tokens, vector, vector, vector, matrix, vector, matrix, vector, matrix, vector,
            vector, vector, matrix, vector, matrix, vector, tokens,
        ),
        out_specs=(
            tokens, tokens, vector, vector, matrix, vector, matrix, vector, matrix, vector,
            vector, vector, matrix, vector, matrix, vector, matrix, vector, matrix,
        ),
        check_vma=False,
    )
```

```python
import functools
import math

import jax
import jax.numpy as jnp
from jax import lax
from jax.experimental import pallas as pl
from jax.experimental.pallas import tpu as pltpu
from jax.sharding import Mesh, PartitionSpec as P

H = 16
HD = 128
EPSILON = 1e-05
CLIP_LIMIT = 10.0
NEGATIVE = -1e30
BF = jnp.bfloat16
F32 = jnp.float32
GELU_A = 0.044715
GELU_C = math.sqrt(2.0 / math.pi)
SCALE = HD ** (-0.5)
MIB = 1 << 20
VMEM_LIMIT = 63 * MIB


def mm(left, right):
    return jnp.dot(left, right, preferred_element_type=F32)


def mm_tn(left, right):
    return lax.dot_general(left, right, (((0,), (0,)), ((), ())), preferred_element_type=F32)


def mm_nt(left, right):
    return lax.dot_general(left, right, (((1,), (1,)), ((), ())), preferred_element_type=F32)


def shift(value, axis, count, step):
    return lax.ppermute(value, axis, [(i, (i + step) % count) for i in range(count)])


def pick(value, index, dim):
    return lax.dynamic_index_in_dim(value, index, dim, keepdims=False)


def in_order(parts, here, count, dim):
    if count == 1:
        return jnp.expand_dims(parts[0], dim)
    if count == 2:
        first = here == 0
        return jnp.stack(
            [jnp.where(first, parts[0], parts[1]), jnp.where(first, parts[1], parts[0])], dim
        )
    shape = list(parts[0].shape)
    shape.insert(dim, count)
    whole = jnp.zeros(shape, parts[0].dtype)
    for j, part in enumerate(parts):
        whole = lax.dynamic_update_index_in_dim(whole, part, lax.rem(here - j + count, count), dim)
    return whole


def gather(value, axis, count, dim):
    parts = [value] + [shift(value, axis, count, j) for j in range(1, count)]
    return in_order(parts, lax.axis_index(axis), count, dim)


def swap_blocks(value, axis, count, dim):
    here = lax.axis_index(axis)
    parts = [pick(value, here, dim)]
    for j in range(1, count):
        parts.append(shift(pick(value, lax.rem(here + j, count), dim), axis, count, j))
    return in_order(parts, here, count, dim)


def sum_blocks(value, axis, count, dim):
    here = lax.axis_index(axis)
    total = pick(value, here, dim).astype(F32)
    for j in range(1, count):
        block = pick(value, lax.rem(here + j, count), dim).astype(BF)
        total = total + shift(block, axis, count, j).astype(F32)
    return total


def sum_copies(value, axis, count):
    low = value.astype(BF)
    total = low.astype(F32)
    for j in range(1, count):
        total = total + shift(low, axis, count, j).astype(F32)
    return total


def attention_masks(rows, length):
    row = lax.broadcasted_iota(jnp.int32, (rows, rows), 0)
    col = lax.broadcasted_iota(jnp.int32, (rows, rows), 1)
    return (col <= row) & (col < length)


MESH = pl.DeviceIdType.MESH
SMALL_ROWS = 16


def sem_count(sizes):
    return 208 if sizes[0] * sizes[3] <= 4 else 448


class Move:
    def __init__(self, copy, send_if, recv_if):
        self.copy, self.send_if, self.recv_if = copy, send_if, recv_if

    def start(self):
        guarded(self.send_if, self.copy.start)

    def wait_send(self):
        guarded(self.send_if, self.copy.wait_send)

    def wait_recv(self):
        guarded(self.recv_if, self.copy.wait_recv)


def guarded(condition, action):
    if condition is None:
        action()
    else:

        @pl.when(condition)
        def _():
            action()


class Links:
    def __init__(self, sends, recvs, locals_):
        self.sends, self.recvs, self.locals_ = sends, recvs, locals_
        self.used, self.used_local = 0, 0
        self.open = []

    def plan(self, src, dst, where, send_if=None, recv_if=None, land=None):
        index = self.used
        self.used += 1
        assert self.used <= self.sends.shape[0]
        copy = pltpu.make_async_remote_copy(
            src_ref=src,
            dst_ref=dst,
            send_sem=self.sends.at[index],
            recv_sem=self.recvs.at[index if land is None else land],
            device_id=where,
            device_id_type=MESH,
        )
        move = Move(copy, send_if, recv_if)
        self.open.append(move)
        return move

    def push(self, src, dst, axis, target=None, when=None):
        where = axis if isinstance(axis, dict) else {axis: target}
        move = self.plan(src, dst, where, when, when)
        move.start()
        return move

    def sent(self, moves):
        for move in moves:
            move.wait_send()
            self.open = [other for other in self.open if other is not move]

    def local(self, src, dst):
        index = self.used_local
        self.used_local += 1
        assert self.used_local < self.locals_.shape[0]
        copy = pltpu.make_async_copy(src, dst, self.locals_.at[index])
        copy.start()
        return copy

    def drain(self):
        for move in self.open:
            move.wait_send()


class Line:
    def __init__(self, links, block, z, Z, source=None):
        self.z, self.Z = z, Z
        self.hops = []
        right, left = {"z": jnp.minimum(z + 1, Z - 1)}, {"z": jnp.maximum(z - 1, 0)}
        for h in range(1, Z):
            low, high = jnp.maximum(z - h + 1, 0), jnp.minimum(z + h - 1, Z - 1)
            ahead, back = block(low), block(high)
            own = source is not None and h == 1
            self.hops.append(
                [
                    links.plan(
                        source if own else ahead,
                        ahead,
                        right,
                        (z >= h - 1) & (z < Z - 1),
                        z >= h,
                    ),
                    links.plan(
                        source if own else back,
                        back,
                        left,
                        (z <= Z - h) & (z > 0),
                        z < Z - h,
                    ),
                ]
            )
        for move in self.hops[0]:
            move.start()

    def hop(self, h):
        for move in self.hops[h - 1]:
            move.wait_recv()
        if h < self.Z - 1:
            for move in self.hops[h]:
                move.start()
        z, Z = self.z, self.Z
        return [
            (jnp.maximum(z - h, 0), z >= h),
            (jnp.minimum(z + h, Z - 1), z < Z - h),
        ]


def wait_all(copies):
    for copy in copies:
        copy.wait()


def wait_recvs(copies):
    for copy in copies:
        copy.wait_recv()


def around(axis, here, count):
    return [(axis, lax.rem(here + j, count)) for j in range(1, count)]


def greet(groups, corners):
    barrier = pltpu.get_barrier_semaphore()
    count = 0
    for where in [{axis: target} for group in groups for axis, target in group] + corners:
        pl.semaphore_signal(barrier, inc=1, device_id=where, device_id_type=MESH)
        count += 1
    pl.semaphore_wait(barrier, count)


class Gather:
    def __init__(self, links, buf, place):
        self.links, self.buf, (self.z, self.Z, self.x, self.X) = links, buf, place
        self.line = Line(links, lambda at: buf.at[at * self.X + self.x], self.z, self.Z)
        self.from_x = []
        self.spread(self.z, None)

    def spread(self, at, when):
        block = self.buf.at[at * self.X + self.x]
        self.from_x += [
            self.links.push(block, block, *to, when=when) for to in around("x", self.x, self.X)
        ]

    def hop(self, h):
        for at, when in self.line.hop(h):
            self.spread(at, when)

    def finish(self):
        wait_recvs(self.from_x)

    def moves(self):
        return self.from_x + [move for hop in self.line.hops for move in hop]


def rows_loop(total, step, work):
    @pl.loop(0, total // step)
    def _(i):
        work(pl.ds(pl.multiple_of(i * step, step), step))


def layer_kernel(sizes, *refs):
    (
        length_ref, rows, cot, wq, wkv, small, wo, up, down,
        result_o, igrad_o, gdown_o, gup_o, gwo_o, gwq_o, gkv_o, small_o, top_o,
        h_seq, h_ux, h_uy, h_dx, h_dy,
        v_big, v_norm, v_w, v_wo, v_qkv, v_rows, v_mid, v_hat, v_mean, v_rstd, v_rs2,
        v_small, v_vec, v_ub, v_gub,
        v_wup, v_wdown, v_nt, v_gm, v_ap, v_g2, v_kin, m_kin, v_zin, m_zin,
        v_br, v_brall, v_gbr, v_gbc, v_gatt, v_gqkv, v_gk, v_gv,
        v_dwox, v_dwoz, v_dwqx, v_dwqz, v_a, v_b,
        v_sg, v_sgb, v_sgx, v_sgz, v_sga, v_top, v_topz, v_topx, v_tall,
        sends, recvs, locals_, ready,
    ) = refs
    Y, K, Z, X = sizes
    C, S = Y * K, Z * X
    y, k, z, x = (lax.axis_index(name) for name in ("y", "k", "z", "x"))
    c = y * K + k
    me = z * X + x
    R, D = rows.shape
    T = C * R
    cols = D // C
    here = wq.shape[0]
    part = v_wdown.shape[1]
    XP = X * part
    heads = cols // HD
    units = part // here
    length = length_ref[0]
    step = 64
    links = Links(sends, recvs, locals_)
    place = (z, Z, x, X)
    to_z, to_x = around("z", z, Z), around("x", x, X)
    to_y, to_k = around("y", y, Y), around("k", k, K)
    zs = [lax.rem(z - j + Z, Z) for j in range(Z)]
    xs = [lax.rem(x - j + X, X) for j in range(X)]
    ys = [lax.rem(y - j + Y, Y) for j in range(Y)]
    others = [
        (lax.rem(y + jy, Y), lax.rem(k + jk, K))
        for jy in range(Y)
        for jk in range(K)
        if jy or jk
    ]
    corners = [
        {"y": lax.rem(y + jy, Y), "k": lax.rem(k + jk, K)}
        for jy in range(1, Y)
        for jk in range(1, K)
    ]

    def at(index, size):
        return pl.ds(pl.multiple_of(index * size, size), size)

    greet([to_z, to_x, to_y, to_k], corners)

    first = [
        links.local(wq.at[:, at(c, cols)], v_w.at[me, :, pl.ds(0, cols)]),
        links.local(wkv, v_w.at[me, :, pl.ds(cols, 2 * HD)]),
        links.local(small, v_small.at[me]),
        links.local(rows, v_big.at[at(c, R)]),
    ]
    own_wo = links.local(wo.at[:, at(c, cols)], v_wo.at[me])
    own_rows = links.local(rows, v_rows)
    own_gm = links.local(cot, v_gm.at[z, k])
    wait_all(first)
    qkv_gather = Gather(links, v_w, place)
    small_gather = Gather(links, v_small, place)
    mine = v_big.at[at(c, R)]
    seq_y = [links.push(mine, mine, *to) for to in to_y]
    seq_k = [links.push(mine, mine, *to) for to in to_k]
    own_gm.wait()

    def mask_rows(span):
        row = lax.broadcasted_iota(jnp.int32, (step, 1), 0) + span.start + c * R
        v_gm[z, k, span, :] = jnp.where(row < length, v_gm[z, k, span, :].astype(F32), 0.0).astype(BF)

    rows_loop(R, step, mask_rows)
    for j in range(1, Y):
        seq_y[j - 1].wait_recv()
        block = v_big.at[at(ys[j] * K + k, R)]
        seq_k += [links.push(block, block, *to) for to in to_k]
    qkv_gather.hop(1)
    small_gather.hop(1)

    slab, piece = here // Y, part // Y
    slab_y, piece_y = at(y, slab), at(y, piece)
    own_up, up_z, up_x, up_y = [], [], [], []
    for j in range(Z):
        target = lax.rem(z + j, Z)
        for i in range(X):
            unit = at((target * X + i) * K + k, part)
            side = pl.ds(i * part, part)
            if j == 0:
                own_up.append(links.local(up.at[:, unit], v_wup.at[me, :, side]))
            else:
                up_z.append(
                    links.push(up.at[slab_y, unit], v_wup.at[me, slab_y, side], "z", target)
                )

    def up_on(index, to):
        block = v_wup.at[index, slab_y]
        return links.push(block, block, *to)

    wait_recvs(seq_k)
    save_seq = links.local(v_big, h_seq)

    def seq_stats(span):
        values = v_big[span, :].astype(F32)
        mean = jnp.mean(values, 1, keepdims=True)
        center = values - mean
        rstd = lax.rsqrt(jnp.mean(center * center, 1, keepdims=True) + EPSILON)
        v_mean[span, :] = jnp.broadcast_to(mean, (step, HD))
        v_rstd[span, :] = jnp.broadcast_to(rstd, (step, HD))

    rows_loop(T, step, seq_stats)
    v_sg[...] = jnp.zeros_like(v_sg)
    v_gub[...] = jnp.zeros_like(v_gub)
    v_gk[...] = jnp.zeros_like(v_gk)
    v_gv[...] = jnp.zeros_like(v_gv)
    qkv_gather.hop(2)
    small_gather.hop(2)
    own_wo.wait()
    wo_gather = Gather(links, v_wo, place)
    qkv_gather.hop(3)
    small_gather.hop(3)
    gm_line = Line(links, lambda to: v_gm.at[to, k], z, Z)
    gm_k = [links.push(v_gm.at[z, k], v_gm.at[z, k], *to) for to in to_k]

    def gm_hop(h):
        for source, when in gm_line.hop(h):
            block = v_gm.at[source, k]
            gm_k.extend(links.push(block, block, *to, when=when) for to in to_k)

    qkv_gather.finish()
    small_gather.finish()
    own_down = links.local(down.at[at(k, part)], v_wdown.at[x])
    down_src = down.at[at(k * Y + y, piece)]
    down_x = [links.push(down_src, v_wdown.at[x, piece_y], *to) for to in to_x]

    for s in range(S):
        v_vec[:, pl.ds(s * here, here)] = v_small[s]
    gain_one = v_vec[0:1, :].astype(F32)
    bias_one = v_vec[1:2, :].astype(F32)

    def first_norm(span):
        hat = (v_big[span, :].astype(F32) - v_mean[span, 0:1]) * v_rstd[span, 0:1]
        v_norm[span, :] = (hat * gain_one + bias_one).astype(BF)

    rows_loop(T, step, first_norm)
    save_seq.wait()
    links.sent(seq_y + seq_k)
    for axis, target in to_y + to_k:
        pl.semaphore_signal(ready, inc=1, device_id={axis: target}, device_id_type=MESH)

    q_bias = v_vec[2:3, at(c, cols)].astype(F32)
    v_bias = jnp.zeros((1, HD), F32)
    for s in range(S):
        v_bias = v_bias + v_small[s, 12:13, 0:HD].astype(F32)
    wide = min(cols, 256)
    for n in range(cols // wide):
        span = slice(n * wide, (n + 1) * wide)
        weights = v_w[:, :, span].reshape(D, wide)
        v_qkv[:, span] = (mm(v_norm[...], weights) + q_bias[:, span]).astype(BF)
    weights = v_w[:, :, cols:].reshape(D, 2 * HD)
    kv_bias = jnp.concatenate([jnp.zeros((1, HD), F32), v_bias], 1)
    v_qkv[:, cols:] = (mm(v_norm[...], weights) + kv_bias).astype(BF)
    wo_gather.hop(1)
    wait_all(own_up)
    up_x += [up_on(me, to) for to in to_x]
    for j in (1, Z - 1, 2):
        wait_recvs(up_z[(j - 1) * X : j * X])
        up_x += [up_on(zs[j] * X + x, to) for to in to_x]

    pl.semaphore_wait(ready, len(to_y) + len(to_k))
    tall = min(T, 256)

    def scores_of(n, r):
        end = (r + 1) * tall
        span = at(n, HD)
        queries = v_qkv[r * tall : end, span]
        keys = v_qkv[0:end, cols : cols + HD]
        row = lax.broadcasted_iota(jnp.int32, (tall, end), 0) + r * tall
        col = lax.broadcasted_iota(jnp.int32, (tall, end), 1)
        allowed = (col <= row) & (col < length)
        masked = jnp.where(allowed, mm_nt(queries, keys) * SCALE, NEGATIVE)
        top = jnp.max(masked, 1, keepdims=True)
        weights = jnp.exp(masked - top)
        return queries, keys, top, weights / jnp.sum(weights, 1, keepdims=True)

    @pl.loop(0, heads)
    def _(n):
        best = jnp.full((1, 1), NEGATIVE, F32)
        for r in range(T // tall):
            end = (r + 1) * tall
            queries, keys, top, weights = scores_of(n, r)
            out = mm(weights.astype(BF), v_qkv[0:end, cols + HD :])
            v_big[r * tall : end, at(c * heads + n, HD)] = out.astype(BF)
            live = lax.broadcasted_iota(jnp.int32, (tall, 1), 0) + r * tall < length
            best = jnp.maximum(best, jnp.max(jnp.where(live, top, NEGATIVE), 0, keepdims=True))
        v_top[pl.ds(n, 1), :] = jnp.broadcast_to(best, (1, HD))

    def att_block(source):
        return v_big.at[:, at(source, cols)]

    att_y = [links.push(att_block(c), att_block(c), *to) for to in to_y]
    att_k = [links.push(att_block(c), att_block(c), *to) for to in to_k]
    top_z = [links.push(v_top, v_topz.at[j], *to) for j, to in enumerate(to_z)]
    wo_gather.hop(2)
    for j in range(1, Y):
        att_y[j - 1].wait_recv()
        block = att_block(ys[j] * K + k)
        att_k += [links.push(block, block, *to) for to in to_k]
    gm_hop(1)
    wo_gather.hop(3)
    for j in (1, Z - 1, 2):
        up_y += [up_on(zs[j] * X + x, to) for to in to_y]
    down_y = []
    for j, move in enumerate(down_x):
        move.wait_recv()
        block = v_wdown.at[xs[j + 1], piece_y]
        down_y += [links.push(block, block, *to) for to in to_y]
    wait_recvs(att_k)
    wo_gather.finish()

    narrow = min(cols, 256)
    for n in range(cols // narrow):
        span = slice(n * narrow, (n + 1) * narrow)
        weights = v_wo[:, :, span].reshape(D, narrow)
        v_br[:, :, span] = mm(v_big[...], weights).astype(BF).reshape(C, R, narrow)
    br_in = [
        links.push(v_br.at[ty * K + tk], v_brall.at[c], {"y": ty, "k": tk}) for ty, tk in others
    ]
    v_brall[c] = v_br[c]
    gm_hop(2)
    own_rows.wait()
    wait_recvs(br_in)

    gain_two = v_vec[4:5, :].astype(F32)
    bias_two = v_vec[5:6, :].astype(F32)
    o_bias = v_vec[3:4, :].astype(F32)

    def second_norm(span):
        branch = jnp.concatenate([v_brall[q, span, :] for q in range(C)], 1)
        middle = v_rows[span, :].astype(F32) + branch.astype(F32) + o_bias
        v_mid[span, :] = middle
        center = middle - jnp.mean(middle, 1, keepdims=True)
        rstd = lax.rsqrt(jnp.mean(center * center, 1, keepdims=True) + EPSILON)
        hat = center * rstd
        v_hat[span, :] = hat
        v_rs2[span, :] = jnp.broadcast_to(rstd, (step, HD))
        v_nt[z, k, span, :] = (hat * gain_two + bias_two).astype(BF)

    rows_loop(R, step, second_norm)
    nt_line = Line(links, lambda to: v_nt.at[to, k], z, Z)
    nt_k = [links.push(v_nt.at[z, k], v_nt.at[z, k], *to) for to in to_k]

    def nt_hop(h):
        fresh = []
        for source, when in nt_line.hop(h):
            block = v_nt.at[source, k]
            fresh += [links.push(block, block, *to, when=when) for to in to_k]
        nt_k.extend(fresh)
        return fresh

    own_nt_k = list(nt_k)
    order = [0, 1, Z - 1, 2]
    for slot, j in enumerate(order):
        for i in range(1, X):
            up_x[slot * (X - 1) + i - 1].wait_recv()
            up_y += [up_on(zs[j] * X + xs[i], to) for to in to_y]
    gm_hop(3)
    for i in range(X):
        for r in range(units):
            to = at(z * X + i, here)
            value = jnp.zeros((1, here), F32)
            for kk in range(K):
                row = 8 + kk * units + r
                value = value + jnp.where(k == kk, v_vec[row : row + 1, to].astype(F32), 0.0)
            v_ub[0:1, i * part + r * here : i * part + (r + 1) * here] = value
    fresh = [own_nt_k, nt_hop(1)]
    own_down.wait()
    wait_recvs(up_y + down_y + gm_k)

    tokens = K * R
    tile = 256

    def mlp_block(b):
        own = at(b, tokens)

        @pl.loop(0, XP // tile, unroll=2)
        def _(n):
            span = at(n, tile)
            inner = at(lax.rem(n, part // tile), tile)
            weights = v_wup[:, :, span].reshape(D, tile)
            pre = mm(v_nt[b].reshape(tokens, D), weights) + v_ub[0:1, span]
            cube = pre * pre
            tanh = jnp.tanh(GELU_C * pre * (1.0 + GELU_A * cube))
            half = 0.5 + 0.5 * tanh
            v_ap[0, own, span] = (pre * half).astype(BF)
            slope = half + 0.5 * pre * (1.0 - tanh * tanh) * GELU_C * (
                1.0 + 3.0 * GELU_A * cube
            )
            grad = mm_nt(v_gm[b].reshape(tokens, D), v_wdown[lax.div(n, part // tile), inner, :])
            grad = (grad * slope).astype(BF)
            v_ap[1, own, span] = grad
            v_gub[0:1, span] += jnp.sum(grad.astype(F32), 0, keepdims=True)

        @pl.loop(0, S, unroll=4)
        def _(s):
            out = mm_nt(v_ap[1, own, :], v_wup[s]).astype(BF)
            v_g2[b, :, :, at(s, here)] = out.reshape(K, R, here)

    far = jnp.where(z < 2, 3, 0)
    turn = [
        z,
        jnp.where(z == 0, 1, jnp.where(z == 1, 2, jnp.where(z == 2, 1, 2))),
        jnp.where(z == 0, 2, jnp.where(z == 1, 0, jnp.where(z == 2, 3, 1))),
        far,
    ]
    g2_k, g2_z = [], []
    z_base = links.used
    links.used += Z - 1

    def g2_out(i):
        b = turn[i]
        g2_k.append(
            [links.push(v_g2.at[b, t], v_kin.at[j, b], a, t) for j, (a, t) in enumerate(to_k)]
        )

    def g2_sum(i):
        b = turn[i]
        wait_recvs(g2_k[i])

        def work(span):
            total = v_g2[b, k, span, :].astype(F32)
            for j in range(K - 1):
                total = total + v_kin[j, b, span, :].astype(F32)
            v_g2[b, k, span, :] = total.astype(BF)

        rows_loop(R, step, work)
        if i:
            away = lax.rem(b - z + Z, Z)
            move = links.plan(
                v_g2.at[b, k], v_zin.at[away - 1], {"z": b}, land=z_base + away - 1
            )
            move.start()
            g2_z.append(move)

    for i in range(Z):
        wait_recvs(fresh[i])
        mlp_block(turn[i])
        g2_out(i)
        if i:
            g2_sum(i - 1)
        if i + 2 < Z:
            fresh.append(nt_hop(i + 2))
    g2_sum(Z - 1)

    wait_recvs(top_z)
    best = v_top[...]
    for j in range(Z - 1):
        best = jnp.maximum(best, v_topz[j])
    v_topx[0] = best
    top_x = [links.push(v_topx.at[0], v_topx.at[j + 1], *to) for j, to in enumerate(to_x)]

    links.sent(up_x + up_y)
    acts = v_ap.at[0]
    grads_pre = v_ap.at[1]
    everyone = Z * tokens

    @pl.loop(0, S, unroll=4)
    def _(s):
        flat = v_nt[:, :, :, at(s, here)].reshape(everyone, here)
        v_wup[s] = mm_tn(flat, grads_pre[...]).astype(BF)

    gu_x = [
        links.push(v_wup.at[q * X + t], h_ux.at[j, q], a, t)
        for j, (a, t) in enumerate(to_x)
        for q in range(Z)
    ]
    links.sent(nt_k)
    for moves in nt_line.hops:
        links.sent(moves)

    @pl.loop(0, D // tile, unroll=4)
    def _(n):
        weights = v_wdown[:, :, at(n, tile)].reshape(XP, tile)
        out = mm(acts[...], weights).astype(BF)
        v_nt[:, :, :, at(n, tile)] = out.reshape(Z, K, R, tile)

    mlp_k = [links.push(v_nt.at[:, t], m_kin.at[j], a, t) for j, (a, t) in enumerate(to_k)]
    links.sent(down_y)

    @pl.loop(0, XP // tile, unroll=2)
    def _(n):
        out = mm_tn(acts[:, at(n, tile)], v_gm[...].reshape(everyone, D)).astype(BF)
        v_wdown[lax.div(n, part // tile), at(lax.rem(n, part // tile), tile), :] = out

    gd_y = [
        links.push(v_wdown.at[:, at(t, piece)], h_dy.at[j], a, t)
        for j, (a, t) in enumerate(to_y)
    ]
    links.sent(gm_k)
    for moves in gm_line.hops:
        links.sent(moves)

    g2_in = [
        pltpu.make_async_remote_copy(
            src_ref=v_g2.at[z, k],
            dst_ref=v_zin.at[j],
            send_sem=sends.at[z_base],
            recv_sem=recvs.at[z_base + j],
            device_id={"z": zs[1]},
            device_id_type=MESH,
        )
        for j in range(Z - 1)
    ]
    wait_recvs(g2_in)

    def second_back(span):
        grad = v_g2[z, k, span, :].astype(F32)
        for j in range(Z - 1):
            grad = grad + v_zin[j, span, :].astype(F32)
        hat = v_hat[span, :]
        v_sg[4:5, :] += jnp.sum(grad * hat, 0, keepdims=True)
        v_sg[5:6, :] += jnp.sum(grad, 0, keepdims=True)
        scaled = grad * gain_two
        back = v_rs2[span, 0:1] * (
            scaled
            - jnp.mean(scaled, 1, keepdims=True)
            - hat * jnp.mean(scaled * hat, 1, keepdims=True)
        )
        grad_out = v_gm[z, k, span, :].astype(F32)
        v_sg[6:7, :] += jnp.sum(grad_out, 0, keepdims=True)
        grad_middle = grad_out + back
        v_hat[span, :] = grad_middle
        low = grad_middle.astype(BF)
        v_sg[3:4, :] += jnp.sum(low.astype(F32), 0, keepdims=True)
        for q in range(C):
            v_gbr[q, span, :] = low[:, q * cols : (q + 1) * cols]

    rows_loop(R, step, second_back)
    wait_recvs(top_x)
    best = v_topx[0]
    for j in range(1, X):
        best = jnp.maximum(best, v_topx[j])
    v_tall[c] = best
    top_y = [links.push(v_tall.at[c], v_tall.at[c], *to) for to in to_y]
    top_k = [links.push(v_tall.at[c], v_tall.at[c], *to) for to in to_k]
    wait_recvs(mlp_k)
    for q in range(Z):

        def mlp_sum(span, q=q):
            total = v_nt[q, k, span, :].astype(F32)
            for j in range(K - 1):
                total = total + m_kin[j, q, span, :].astype(F32)
            v_nt[q, k, span, :] = total.astype(BF)

        rows_loop(R, step, mlp_sum)
    gb = [
        links.push(v_gbr.at[ty * K + tk], v_gbc.at[c], {"y": ty, "k": tk}) for ty, tk in others
    ]
    v_gbc[c] = v_gbr[c]
    mlp_z = [links.push(v_nt.at[t, k], m_zin.at[j], a, t) for j, (a, t) in enumerate(to_z)]
    for moves in g2_k:
        links.sent(moves)
    links.sent(g2_z)
    wait_recvs(gb)

    @pl.loop(0, S, unroll=4)
    def _(s):
        out = mm_nt(v_gbc[...].reshape(T, cols), v_wo[s]).astype(BF)
        v_g2[0:Y, :, :, at(s, here)] = out.reshape(Y, K, R, here)

    chunks = pl.ds(0, Y)
    ga_k = [
        links.push(
            v_g2.at[chunks, :, :, at(q * K + t, cols)],
            v_gm.at[chunks, :, :, pl.ds((j * Y + q) * cols, cols)],
            a,
            t,
        )
        for j, (a, t) in enumerate(to_k)
        for q in range(Y)
    ]
    links.sent(wo_gather.moves())

    @pl.loop(0, S, unroll=4)
    def _(s):
        v_wo[s] = mm_tn(v_big[:, at(s, here)], v_gbc[...].reshape(T, cols)).astype(BF)

    do_x = [
        links.push(v_wo.at[q * X + t], v_dwox.at[j, q], a, t)
        for j, (a, t) in enumerate(to_x)
        for q in range(Z)
    ]
    links.sent(att_y + att_k)
    load_seq = links.local(h_seq, v_big)
    wait_recvs(ga_k)
    base = (K - 1) * Y
    for q in range(Y):
        for i in range(Y):
            for kk in range(K):

                def ga_sum(span, q=q, i=i, kk=kk):
                    total = v_g2[i, kk, span, at(q * K + k, cols)].astype(F32)
                    for j in range(K - 1):
                        side = slice((j * Y + q) * cols, (j * Y + q + 1) * cols)
                        total = total + v_gm[i, kk, span, side].astype(F32)
                    v_gm[i, kk, span, q * cols : (q + 1) * cols] = total.astype(BF)

                rows_loop(R, step, ga_sum)
    ga_y = [
        links.push(
            v_gm.at[chunks, :, :, at(t, cols)],
            v_gm.at[chunks, :, :, pl.ds((base + j) * cols, cols)],
            a,
            t,
        )
        for j, (a, t) in enumerate(to_y)
    ]
    bufs = (v_a, v_b)
    spare = (locals_.at[locals_.shape[0] - 1], locals_.at[locals_.shape[0] - 2])

    def add_tiles(tiles):
        def fetch(i):
            source, height, width = tiles[i][:3]
            copy = pltpu.make_async_copy(
                source, bufs[i % 2].at[pl.ds(0, height), pl.ds(0, width)], spare[i % 2]
            )
            copy.start()
            return copy

        coming = fetch(0)
        for i, (source, height, width, load, store) in enumerate(tiles):
            now = coming
            if i + 1 < len(tiles):
                coming = fetch(i + 1)
            now.wait()
            small_step = min(step, height)

            def work(span, i=i, width=width, load=load, store=store):
                extra = bufs[i % 2][span, 0:width].astype(F32)
                store(span, (load(span).astype(F32) + extra).astype(BF))

            rows_loop(height, small_step, work)

    def shifted(start, span):
        return pl.ds(pl.multiple_of(start + span.start, span.size), span.size)

    def up_tile(source, q, start, height):
        def load(span):
            return v_wup[q * X + x, shifted(start, span), :]

        def store(span, value):
            v_wup[q * X + x, shifted(start, span), :] = value

        return source, height, XP, load, store

    wait_recvs(gu_x)
    add_tiles(
        [up_tile(h_ux.at[j, q], q, 0, here) for q in range(Z) for j in range(X - 1)]
    )
    gu_y = [
        links.push(v_wup.at[q * X + x, at(t, slab)], h_uy.at[j, q], a, t)
        for j, (a, t) in enumerate(to_y)
        for q in range(Z)
    ]

    wait_recvs(ga_y)
    for i in range(Y):
        for kk in range(K):

            def ga_last(span, i=i, kk=kk):
                total = v_gm[i, kk, span, at(y, cols)].astype(F32)
                for j in range(Y - 1):
                    side = slice((base + j) * cols, (base + j + 1) * cols)
                    total = total + v_gm[i, kk, span, side].astype(F32)
                to = pl.ds(pl.multiple_of((i * K + kk) * R + span.start, step), step)
                v_gatt[to, :] = total.astype(BF)

            rows_loop(R, step, ga_last)

    @pl.loop(0, heads)
    def _(n):
        span = at(n, HD)
        for r in range(T // tall):
            end = (r + 1) * tall
            own = slice(r * tall, end)
            queries, keys, top, weights = scores_of(n, r)
            grads = v_gatt[own, span]
            grad_weights = mm_nt(grads, v_qkv[0:end, cols + HD :])
            delta = jnp.sum(weights * grad_weights, 1, keepdims=True)
            grad_scores = (weights * (grad_weights - delta)).astype(BF)
            v_gqkv[own, span] = (mm(grad_scores, keys) * SCALE).astype(BF)
            v_gk[0:end, :] += mm_tn(grad_scores, queries) * SCALE
            v_gv[0:end, :] += mm_tn(weights.astype(BF), grads)

    v_gqkv[:, cols : cols + HD] = v_gk[...].astype(BF)
    v_gqkv[:, cols + HD :] = v_gv[...].astype(BF)
    wq_cols = cols + 2 * HD
    per = v_ap.shape[1] // here

    def dwq(index):
        return v_ap.at[lax.div(index, per), at(lax.rem(index, per), here), pl.ds(0, wq_cols)]

    @pl.loop(0, S, unroll=4)
    def _(s):
        out = mm_tn(v_norm[:, at(s, here)], v_gqkv[...]).astype(BF)
        v_ap[lax.div(s, per), at(lax.rem(s, per), here), 0:wq_cols] = out

    dq_x = [
        links.push(dwq(q * X + t), v_dwqx.at[j, q], a, t)
        for j, (a, t) in enumerate(to_x)
        for q in range(Z)
    ]
    load_seq.wait()

    @pl.loop(0, S, unroll=4)
    def _(s):
        span = at(s, here)
        grad = mm_nt(v_gqkv[...], v_w[s])
        v_norm[:, span] = grad.astype(BF)
        hat = (v_big[:, span].astype(F32) - v_mean[:, 0:1]) * v_rstd[:, 0:1]
        v_sg[0:1, span] = jnp.sum(grad * hat, 0, keepdims=True)
        v_sg[1:2, span] = jnp.sum(grad, 0, keepdims=True)
    g1_k = [
        links.push(v_norm.at[at(q * K + t, R)], v_kin.at[j, q], a, t)
        for j, (a, t) in enumerate(to_k)
        for q in range(Y)
    ]

    for j in range(1, Y):
        top_y[j - 1].wait_recv()
        block = v_tall.at[ys[j] * K + k]
        top_k += [links.push(block, block, *to) for to in to_k]

    v_sg[2:3, at(c, cols)] = jnp.sum(v_gqkv[:, 0:cols].astype(F32), 0, keepdims=True)
    value_sum = jnp.sum(v_gqkv[:, cols + HD :].astype(F32), 0, keepdims=True)
    for s in range(S):
        v_sg[12:13, s * here : s * here + HD] = value_sum
    for i in range(X):
        to = at(z * X + i, here)
        for r in range(units):
            start = i * part + r * here
            bias_part = v_gub[0:1, start : start + here]
            for kk in range(K):
                row = 8 + kk * units + r
                v_sg[row : row + 1, to] = jnp.where(k == kk, bias_part, 0.0)
    for s in range(S):
        v_sgb[s // X, s % X] = v_sg[:, s * here : (s + 1) * here]
    sg_x = [links.push(v_sgb.at[:, t], v_sgx.at[j], a, t) for j, (a, t) in enumerate(to_x)]

    def sum_x(own, extra, copies):
        wait_recvs(copies)
        for q in range(Z):
            total = own(q)[...].astype(F32)
            for j in range(X - 1):
                total = total + extra[j, q].astype(F32)
            extra[0, q] = total.astype(extra.dtype)

    sum_x(lambda q: v_wo.at[q * X + x], v_dwox, do_x)
    do_z = [links.push(v_dwox.at[0, t], v_dwoz.at[j], a, t) for j, (a, t) in enumerate(to_z)]
    wait_recvs(g1_k)
    for q in range(Y):

        def g1_sum(span, q=q):
            total = v_norm[shifted((q * K + k) * R, span), :].astype(F32)
            for j in range(K - 1):
                total = total + v_kin[j, q, span, :].astype(F32)
            v_kin[0, q, span, :] = total.astype(BF)

        rows_loop(R, step, g1_sum)
    g1_y = [links.push(v_kin.at[0, t], m_kin.at[0, j], a, t) for j, (a, t) in enumerate(to_y)]

    def down_tile(source, index, start, height, side):
        def load(span):
            return v_wdown[index, shifted(start, span), side]

        def store(span, value):
            v_wdown[index, shifted(start, span), side] = value

        return source, height, XP, load, store

    halves = [slice(n * XP, (n + 1) * XP) for n in range(D // XP)]
    wait_recvs(gd_y)
    add_tiles(
        [
            down_tile(h_dy.at[j, i, :, pl.ds(side.start, XP)], i, y * piece, piece, side)
            for i in range(X)
            for side in halves
            for j in range(Y - 1)
        ]
    )
    gd_x = [links.push(v_wdown.at[t, piece_y], h_dx.at[j], a, t) for j, (a, t) in enumerate(to_x)]

    wait_recvs(gu_y)
    add_tiles(
        [up_tile(h_uy.at[j, q], q, y * slab, slab) for q in range(Z) for j in range(Y - 1)]
    )
    gu_z, own_gu = [], []
    for i in range(X):
        side = pl.ds(i * part, part)
        to = gup_o.at[z * X + i, k, slab_y]
        own_gu.append(links.local(v_wup.at[me, slab_y, side], to))
        for a, t in to_z:
            gu_z.append(links.push(v_wup.at[t * X + x, slab_y, side], to, a, t))

    sum_x(lambda q: dwq(q * X + x), v_dwqx, dq_x)
    dq_z = [links.push(v_dwqx.at[0, t], v_dwqz.at[j], a, t) for j, (a, t) in enumerate(to_z)]
    sum_x(lambda q: v_sgb.at[q, x], v_sgx, sg_x)
    sg_z = [links.push(v_sgx.at[0, t], v_sgz.at[j], a, t) for j, (a, t) in enumerate(to_z)]

    last = []
    def sum_z(own, extra, copies):
        wait_recvs(copies)
        total = own[0, z].astype(F32)
        for j in range(Z - 1):
            total = total + extra[j].astype(F32)
        extra[0] = total.astype(extra.dtype)

    sum_z(v_dwox, v_dwoz, do_z)
    last.append(links.local(v_dwoz.at[0], gwo_o.at[:, at(c, cols)]))
    wo_y = [links.push(v_dwoz.at[0], gwo_o.at[:, at(c, cols)], *to) for to in to_y]
    wo_k = [links.push(v_dwoz.at[0], gwo_o.at[:, at(c, cols)], *to) for to in to_k]

    wait_recvs(gd_x)
    add_tiles(
        [
            down_tile(h_dx.at[j, :, pl.ds(side.start, XP)], x, y * piece, piece, side)
            for side in halves
            for j in range(X - 1)
        ]
    )
    gd_block = v_wdown.at[x, piece_y]
    last.append(links.local(gd_block, gdown_o.at[k, piece_y]))
    gd_y2 = [links.push(gd_block, gdown_o.at[k, piece_y], *to) for to in to_y]
    gd_k = [links.push(gd_block, gdown_o.at[k, piece_y], *to) for to in to_k]

    wait_all(own_gu)
    wait_recvs(gu_z)
    mine = gup_o.at[:, k, slab_y]
    gu_y2 = [links.push(mine, mine, *to) for to in to_y]
    gu_k = [links.push(mine, mine, *to) for to in to_k]

    wait_recvs(top_k)
    save_top = links.local(v_tall, top_o)
    wait_recvs(g1_y)

    def finish_input(span):
        grad = v_kin[0, y, span, :].astype(F32)
        for j in range(Y - 1):
            grad = grad + m_kin[0, j, span, :].astype(F32)
        own = shifted(c * R, span)
        rstd = v_rstd[own, 0:1]
        hat = (v_rows[span, :].astype(F32) - v_mean[own, 0:1]) * rstd
        scaled = grad * gain_one
        back = rstd * (
            scaled
            - jnp.mean(scaled, 1, keepdims=True)
            - hat * jnp.mean(scaled * hat, 1, keepdims=True)
        )
        v_rows[span, :] = (v_hat[span, :] + back).astype(BF)

    rows_loop(R, step, finish_input)
    last.append(links.local(v_rows, igrad_o))

    d_bias = v_vec[6:7, :].astype(F32)
    wait_recvs(mlp_z)

    def finish_result(span):
        total = v_nt[z, k, span, :].astype(F32)
        for j in range(Z - 1):
            total = total + m_zin[j, span, :].astype(F32)
        row = lax.broadcasted_iota(jnp.int32, (step, 1), 0) + span.start + c * R
        value = v_mid[span, :] + total + d_bias
        v_zin[0, span, :] = jnp.where(row < length, value, 0.0).astype(BF)

    rows_loop(R, step, finish_result)
    last.append(links.local(v_zin.at[0], result_o))

    sum_z(v_dwqx, v_dwqz, dq_z)
    left, tail = pl.ds(0, cols), pl.ds(cols, 2 * HD)
    last.append(links.local(v_dwqz.at[0, :, left], gwq_o.at[:, at(c, cols)]))
    last.append(links.local(v_dwqz.at[0, :, tail], gkv_o.at[c]))
    wq_y = [links.push(v_dwqz.at[0, :, left], gwq_o.at[:, at(c, cols)], *to) for to in to_y]
    wq_k = [links.push(v_dwqz.at[0, :, left], gwq_o.at[:, at(c, cols)], *to) for to in to_k]
    kv_y = [links.push(v_dwqz.at[0, :, tail], gkv_o.at[c], *to) for to in to_y]
    kv_k = [links.push(v_dwqz.at[0, :, tail], gkv_o.at[c], *to) for to in to_k]
    sum_z(v_sgx, v_sgz, sg_z)
    v_sga[c] = v_sgz[0]
    sg_y = [links.push(v_sga.at[c], v_sga.at[c], *to) for to in to_y]
    sg_k = [links.push(v_sga.at[c], v_sga.at[c], *to) for to in to_k]

    def on_to_core(ref):
        return [links.push(ref, ref, *to) for to in to_k]

    for j in range(1, Y):
        q = ys[j] * K + k
        wo_y[j - 1].wait_recv()
        wo_k += on_to_core(gwo_o.at[:, at(q, cols)])
        gd_y2[j - 1].wait_recv()
        gd_k += on_to_core(gdown_o.at[k, at(ys[j], piece)])
        wq_y[j - 1].wait_recv()
        wq_k += on_to_core(gwq_o.at[:, at(q, cols)])
        kv_y[j - 1].wait_recv()
        kv_k += on_to_core(gkv_o.at[q])
        sg_y[j - 1].wait_recv()
        sg_k += on_to_core(v_sga.at[q])
        gu_y2[j - 1].wait_recv()
        gu_k += on_to_core(gup_o.at[:, k, at(ys[j], slab)])
    wait_recvs(sg_k)
    total = v_sga[0]
    for q in range(1, C):
        total = total + v_sga[q]
    v_sgz[0] = total
    last.append(links.local(v_sgz.at[0], small_o))
    wait_recvs(gd_k + wo_k + wq_k + kv_k + gu_k)
    wait_all(last + [save_top])
    links.drain()


def layer_call(sizes, lengths, rows, cot, wq, wkv, small, wo, up, down):
    Y, K, Z, X = sizes
    C, S = Y * K, Z * X
    R, D = rows.shape
    T = C * R
    cols = D // C
    wq_cols = cols + 2 * HD
    here = wq.shape[0]
    part = down.shape[0] // K
    XP = X * part
    shape = jax.ShapeDtypeStruct
    anywhere = pl.BlockSpec(memory_space=pl.ANY)

    def low(*dims):
        return pltpu.VMEM(dims, BF)

    def wide(*dims):
        return pltpu.VMEM(dims, F32)

    outs = [
        shape((R, D), BF),
        shape((R, D), BF),
        shape((K, part, D), BF),
        shape((S, K, here, part), BF),
        shape((here, D), BF),
        shape((here, D), BF),
        shape((C, here, 2 * HD), BF),
        shape((SMALL_ROWS, here), F32),
        shape((C, 8, HD), F32),
        shape((T, D), BF),
        shape((X - 1, Z, here, XP), BF),
        shape((Y - 1, Z, here // Y, XP), BF),
        shape((X - 1, part // Y, D), BF),
        shape((Y - 1, X, part // Y, D), BF),
    ]
    scratch = [
        low(T, D), low(T, D), low(S, here, wq_cols), low(S, here, cols), low(T, wq_cols),
        low(R, D), wide(R, D), wide(R, D), wide(T, HD), wide(T, HD), wide(R, HD),
        low(S, SMALL_ROWS, here), low(SMALL_ROWS, D), wide(1, XP), wide(1, XP),
        low(S, here, XP), low(X, part, D), low(Z, K, R, D), low(Z, K, R, D),
        low(2, Z * K * R, XP), low(Z, K, R, D), low(K - 1, Z, R, D), low(K - 1, Z, R, D),
        low(Z - 1, R, D), low(Z - 1, R, D),
        low(C, R, cols), low(C, R, cols), low(C, R, cols), low(C, R, cols),
        low(T, cols), low(T, wq_cols), wide(T, HD), wide(T, HD),
        low(X - 1, Z, here, cols), low(Z - 1, here, cols),
        low(X - 1, Z, here, wq_cols), low(Z - 1, here, wq_cols),
        low(here, XP), low(here, XP),
        wide(SMALL_ROWS, D), wide(Z, X, SMALL_ROWS, here), wide(X - 1, Z, SMALL_ROWS, here),
        wide(Z - 1, SMALL_ROWS, here), wide(C, SMALL_ROWS, here),
        wide(8, HD), wide(Z - 1, 8, HD), wide(X, 8, HD), wide(C, 8, HD),
        pltpu.SemaphoreType.DMA((sem_count(sizes),)),
        pltpu.SemaphoreType.DMA((sem_count(sizes),)),
        pltpu.SemaphoreType.DMA((32,)),
        pltpu.SemaphoreType.REGULAR,
    ]
    return pl.pallas_call(
        functools.partial(layer_kernel, sizes),
        in_specs=[pl.BlockSpec(memory_space=pltpu.SMEM)] + [anywhere] * 8,
        out_specs=[anywhere] * len(outs),
        out_shape=outs,
        scratch_shapes=scratch,
        compiler_params=pltpu.CompilerParams(
            collective_id=1, has_side_effects=True, vmem_limit_bytes=VMEM_LIMIT
        ),
        name="layer",
    )(lengths, rows, cot, wq, wkv, small, wo, up, down)[:9]


STEPS = 8


def finish_kernel(
    shard_ref, tops, wq, wkv, q_bias, result, igrad, gup, gdown, gwo, gwq, gkv,
    result_o, igrad_o, gup_o, gdown_o, gwo_o, gwq_o, gkv_o, cq_o, ckv_o, cb_o, v_scale,
):
    groups, heads = tops.shape[0], v_scale.shape[1] // HD // tops.shape[0]
    least = jnp.ones((1, HD), F32)
    for g in range(groups):
        for n in range(heads):
            factor = CLIP_LIMIT / jnp.maximum(tops[g, n : n + 1, :], CLIP_LIMIT)
            least = jnp.minimum(least, factor)
            column = (g * heads + n) * HD
            v_scale[0:1, column : column + HD] = jnp.sqrt(factor)
    cq_o[...] = (wq[...].astype(F32) * v_scale[0:1, :]).astype(BF)
    ckv_o[:, 0:HD] = (wkv[:, 0:HD].astype(F32) * jnp.sqrt(least)).astype(BF)
    ckv_o[:, HD:] = wkv[:, HD:]
    here = q_bias.shape[1]
    own = pl.ds(pl.multiple_of(shard_ref[0] * here, here), here)
    cb_o[...] = (q_bias[...].astype(F32) * v_scale[0:1, own]).astype(BF)
    result_o[...] = result[...]
    igrad_o[...] = igrad[...]
    width = gup.shape[2]
    for n in range(gup.shape[0]):
        gup_o[:, n * width : (n + 1) * width] = gup[n].astype(F32)
    gdown_o[...] = gdown[...].astype(F32)
    gwo_o[...] = gwo[...].astype(F32)
    gwq_o[...] = gwq[...].astype(F32)
    total = gkv[0].astype(F32)
    for g in range(1, groups):
        total = total + gkv[g].astype(F32)
    gkv_o[...] = total


def finish(shard, tops, wq, wkv, q_bias, result, igrad, gup, gdown, gwo, gwq, gkv):
    here, D = wq.shape
    rows, units = result.shape[0], gup.shape[0]
    part = gup.shape[2]
    tall = gdown.shape[0]
    groups = tops.shape[0]

    def down_rows(height, width):
        return pl.BlockSpec((height // STEPS, width), lambda i, s: (i, 0))

    def whole(*dims):
        return pl.BlockSpec(dims, lambda i, s: (0,) * len(dims))

    tokens = down_rows(rows, D)
    square = down_rows(here, D)
    narrow = down_rows(here, 2 * HD)
    shape = jax.ShapeDtypeStruct
    return pl.pallas_call(
        finish_kernel,
        grid_spec=pltpu.PrefetchScalarGridSpec(
            num_scalar_prefetch=1,
            grid=(STEPS,),
            in_specs=[
                whole(*tops.shape), square, narrow, whole(1, here), tokens, tokens,
                pl.BlockSpec((units // STEPS, here, part), lambda i, s: (i, 0, 0)),
                down_rows(tall, D), square, square,
                pl.BlockSpec((groups, here // STEPS, 2 * HD), lambda i, s: (0, i, 0)),
            ],
            out_specs=[
                tokens, tokens,
                pl.BlockSpec((here, units // STEPS * part), lambda i, s: (0, i)),
                down_rows(tall, D), square, square, narrow, square, narrow, whole(1, here),
            ],
            scratch_shapes=[pltpu.VMEM((8, D), F32)],
        ),
        out_shape=[
            shape((rows, D), BF), shape((rows, D), BF), shape((here, units * part), F32),
            shape((tall, D), F32), shape((here, D), F32), shape((here, D), F32),
            shape((here, 2 * HD), F32), shape((here, D), BF), shape((here, 2 * HD), BF),
            shape((1, here), BF),
        ],
        compiler_params=pltpu.CompilerParams(vmem_limit_bytes=VMEM_LIMIT),
        name="finish",
    )(shard, tops, wq, wkv, q_bias, result, igrad, gup, gdown, gwo, gwq, gkv)


def body(
    sizes,
    inputs,
    lengths,
    norm1_gain,
    norm1_bias,
    query_weight,
    query_bias,
    keyval_weight,
    value_bias,
    output_weight,
    output_bias,
    norm2_gain,
    norm2_bias,
    up_weight,
    up_bias,
    down_weight,
    down_bias,
    cotangent,
):
    Y, K, Z, X = sizes
    C, S = Y * K, Z * X
    y, k, z, x = (lax.axis_index(name) for name in ("y", "k", "z", "x"))
    c = y * K + k
    R, D = inputs.shape[1:]
    rows_here = query_weight.shape[0]
    ff_here = down_weight.shape[0]
    ff_part = ff_here // K
    FF = ff_here * S
    T = C * R
    cols = D // C
    heads = H // C
    qkv_cols = cols + 2 * HD
    small_len = 7 * rows_here + ff_here + HD // S
    small_rows = -(-small_len // qkv_cols)
    small_rows = -(-small_rows // 16) * 16
    packed_rows = rows_here + small_rows

    pieces = [norm1_gain, norm1_bias, query_bias, output_bias, norm2_gain, norm2_bias, down_bias]
    shard = z * X + x
    value_row = lax.dynamic_update_slice_in_dim(
        jnp.zeros((rows_here,), BF), value_bias, shard * (HD // S), 0
    )
    row = lax.broadcasted_iota(jnp.int32, (SMALL_ROWS, rows_here), 0)
    spread_row = functools.partial(jnp.broadcast_to, shape=(SMALL_ROWS, rows_here))
    small = jnp.zeros((SMALL_ROWS, rows_here), BF)
    for index, piece in enumerate(pieces):
        small = jnp.where(row == index, spread_row(piece), small)
    for index in range(ff_here // rows_here):
        piece = up_bias[index * rows_here : (index + 1) * rows_here]
        small = jnp.where(row == 8 + index, spread_row(piece), small)
    small = jnp.where(row == 12, spread_row(value_row), small)

    rows_low = inputs[0]
    result, input_grad, gdown, gup, gwo, gwq, gkv, small_sums, tops = layer_call(
        sizes,
        lengths,
        rows_low,
        cotangent[0],
        query_weight,
        keyval_weight,
        small,
        output_weight,
        up_weight,
        down_weight,
    )
    (
        result,
        input_grad,
        grad_up_weight,
        grad_down_weight,
        grad_output_weight,
        grad_query_weight,
        grad_keyval_weight,
        clipped_query_weight,
        clipped_keyval_weight,
        clipped_query_bias,
    ) = finish(
        shard[None],
        tops,
        query_weight,
        keyval_weight,
        query_bias[None],
        result,
        input_grad,
        gup.reshape(S * K, rows_here, ff_part),
        gdown.reshape(ff_here, D),
        gwo,
        gwq,
        gkv,
    )
    grad_value_bias = lax.dynamic_slice_in_dim(small_sums[12], shard * (HD // S), HD // S, 0)

    return (
        result[None],
        input_grad[None],
        small_sums[0],
        small_sums[1],
        grad_query_weight,
        small_sums[2],
        grad_keyval_weight,
        grad_value_bias,
        grad_output_weight,
        small_sums[3],
        small_sums[4],
        small_sums[5],
        grad_up_weight,
        small_sums[8:12].reshape(-1),
        grad_down_weight,
        small_sums[6],
        clipped_query_weight,
        clipped_query_bias[0],
        clipped_keyval_weight,
    )


def solution(mesh):
    ctx, fsdp = mesh.shape["ctx"], mesh.shape["fsdp"]
    sizes = (ctx // 2, 2, 4, fsdp // 4)
    fine = Mesh(mesh.devices.reshape(sizes), ("y", "k", "z", "x"))
    tokens = P(("z", "x"), ("y", "k"), None)
    vector = P(("z", "x"))
    matrix = P(("z", "x"), None)
    return jax.shard_map(
        functools.partial(body, sizes),
        mesh=fine,
        in_specs=(
            tokens, vector, vector, vector, matrix, vector, matrix, vector, matrix, vector,
            vector, vector, matrix, vector, matrix, vector, tokens,
        ),
        out_specs=(
            tokens, tokens, vector, vector, matrix, vector, matrix, vector, matrix, vector,
            vector, vector, matrix, vector, matrix, vector, matrix, vector, matrix,
        ),
        check_vma=False,
    )
```
